32 devices in a mesh: dp: 8 (over y, x, core), tensor: 4 (over z).
Axes of the slice: x: 2, y: 2, z: 4, core: 2. Of those that a mesh axis runs over, the one named last changes fastest.
Arguments:
- activations: bfloat16 [16, 1024, 768], P('dp', 'tensor'), may hold values from -6 to 6
- condition: float32 [16, 128], P('dp'), may hold values from -6 to 6
- modulator: bfloat16 [128, 4608], replicated, may hold values from -0.5 to 0.5
- mod_bias: float32 [4608], replicated, may hold values from -3 to 3
- gain_attn: float32 [768], replicated, may hold values from 0.1 to 1.9
- gain_mlp: float32 [768], replicated, may hold values from 0.1 to 1.9
- query_key_value_matrix: bfloat16 [768, 3, 768], P(None, None, 'tensor'), may hold values from -0.21875 to 0.21875
- output_matrix: bfloat16 [768, 768], P('tensor'), may hold values from -3.5 to 3.5
- up_matrix: bfloat16 [768, 3072], P(None, 'tensor'), may hold values from -0.21875 to 0.21875
- up_offset_bias: float32 [3072], P('tensor'), may hold values from -3 to 3
- down_matrix: bfloat16 [3072, 768], P('tensor'), may hold values from -0.109375 to 0.109375
- down_bias: float32 [768], replicated, may hold values from -3 to 3
- upstream: bfloat16 [16, 1024, 768], P('dp', 'tensor'), may hold values from -6 to 6
- span_start: int32 [16], P('dp'), may hold values from 0 to 511
- span_length: int32 [16], P('dp'), may hold values from 256 to 512
- noise_level: int32 [16], P('dp'), may hold values from 0 to 1023
Outputs:
- block_out: bfloat16 [16, 1024, 768], P('dp', 'tensor')
- entering_state_slope: float32 [16, 1024, 768], P('dp', 'tensor')
- condition_grad: float32 [16, 128], P('dp')
- modulator_grad: float32 [128, 4608], replicated
- modbias_grad: float32 [4608], replicated
- gainattn_grad: float32 [768], replicated
- perceptron_norm_gain_slope: float32 [768], replicated
- qkv_grad: float32 [768, 3, 768], P(None, None, 'tensor')
- out_grad: float32 [768, 768], P('tensor')
- up_grad: float32 [768, 3072], P(None, 'tensor')
- upbias_grad: float32 [3072], P('tensor')
- down_grad: float32 [3072, 768], P('tensor')
- downbias_grad: float32 [768], replicated
The draws below stay inside these ranges and needn't reach their ends.
All inputs are finite; a program needn't handle non-finite values.
Results may differ from the reference program's by a relative error of at most 0.017.
The reference program's roundings to bfloat16 on the way count: a program that leaves them out, or rounds other values in their place, can miss the bound.
Values may be sent and summed in bfloat16 or wider, within the bound.
No kernel may reach another device: no remote copies, remote signals or barrier semaphores. Data moves between devices by JAX's collectives and lax.ppermute only.
A program may use at most 192 MiB of HBM per device.

```python
import math
import jax
import jax.numpy as jnp
from jax import lax

D = 768
HEADS = 12
HEAD = 64
MLP = 3072
COND = 128
L = 1024
LEVELS = 1024
B = 16


def set_ends(drawn, stream_key, low, high):
    place = [jax.random.randint(jax.random.fold_in(stream_key, axis), (), 0, length) for axis, length in enumerate(drawn.shape)]
    main_axis = drawn.shape.index(max(drawn.shape))
    beside = place[:main_axis] + [(place[main_axis] + 1) % drawn.shape[main_axis]] + place[main_axis + 1:]
    return drawn.at[tuple(place)].set(low).at[tuple(beside)].set(high)


def shard_levels(key, dims, shards, low, high):
    loudness, own = 1.0, jax.random.fold_in(key, 6)
    for position, blocks in shards:
        draws = jnp.exp(jax.random.uniform(jax.random.fold_in(own, position), (blocks,), jnp.float32, low / len(shards), high / len(shards)))
        loudness = loudness * jnp.repeat(draws, dims[position] // blocks).reshape([-1 if axis == position else 1 for axis in range(len(dims))])
    return loudness


def gaussian(stream_key, shape, scale, most, shards=(), held_as=jnp.bfloat16):
    array = jax.random.normal(stream_key, shape, jnp.float32) * scale
    if len(shards) > 0:
        array = shard_levels(stream_key, shape, shards, -0.22, 0.18) * array
    return jnp.clip(array, min=-most, max=most).astype(held_as)


def setup_inputs(seed: int = 0) -> dict:
    splits = jax.random.split(jax.random.key(seed), 17)
    activations = gaussian(splits[0], (B, L, D), 1.0, 6.0, ((0, 8), (1, 4)))
    condition = gaussian(splits[1], (B, COND), 1.0, 6.0, ((0, 8),), jnp.float32)
    modulator = gaussian(splits[2], (COND, 6 * D), COND ** -0.5, 0.5)
    mod_bias = gaussian(splits[3], (6 * D,), 0.5, 3.0, (), jnp.float32)
    gain_attn = jnp.clip(1.0 + 0.18 * jax.random.normal(splits[4], (D,), jnp.float32), 0.1, 1.9)
    gain_mlp = jnp.clip(1.0 + 0.18 * jax.random.normal(splits[5], (D,), jnp.float32), 0.1, 1.9)
    query_key_value_matrix = gaussian(splits[6], (D, 3, D), D ** -0.5, 0.21875, ((2, 4),))
    output_matrix = gaussian(splits[7], (D, D), (max(D // 256, 1)) ** -0.5, 3.5, ((0, 4),))
    up_matrix = gaussian(splits[8], (D, MLP), D ** -0.5, 0.21875, ((1, 4),))
    up_offset_bias = gaussian(splits[9], (MLP,), 0.5, 3.0, ((0, 4),), jnp.float32)
    down_matrix = gaussian(splits[10], (MLP, D), MLP ** -0.5, 0.109375, ((0, 4),))
    down_bias = gaussian(splits[11], (D,), 0.5, 3.0, (), jnp.float32)
    upstream = gaussian(splits[12], (B, L, D), 1.0, 6.0, ((0, 8), (1, 4)))
    span_start = set_ends(jax.random.randint(splits[13], (B,), 0, L // 2), jax.random.fold_in(splits[13], 1), 0, (L // 2) - 1).astype(jnp.int32)
    span_length = set_ends(jax.random.randint(splits[14], (B,), L // 4, L // 2 + 1), jax.random.fold_in(splits[14], 1), L // 4, (L // 2 + 1) - 1).astype(jnp.int32)
    noise_level = set_ends(jax.random.randint(splits[15], (B,), 0, LEVELS), jax.random.fold_in(splits[15], 1), 0, LEVELS - 1).astype(jnp.int32)
    return {"activations": activations, "condition": condition, "modulator": modulator, "mod_bias": mod_bias, "gain_attn": gain_attn, "gain_mlp": gain_mlp, "query_key_value_matrix": query_key_value_matrix, "output_matrix": output_matrix, "up_matrix": up_matrix, "up_offset_bias": up_offset_bias, "down_matrix": down_matrix, "down_bias": down_bias, "upstream": upstream, "span_start": span_start, "span_length": span_length, "noise_level": noise_level}


@jax.custom_vjp
def low(v):
    return lax.optimization_barrier(v.astype(jnp.bfloat16)).astype(jnp.float32)

@jax.custom_vjp
def low_back(v):
    return v

def low_keep(v):
    return (low(v), None)

def low_pass(kept, grad):
    return (grad,)

def back_keep(v):
    return (v, None)

def back_low(kept, grad):
    return (low(grad),)
low.defvjp(low_keep, low_pass)
low_back.defvjp(back_keep, back_low)
noise_low = 0.1
noise_high = 3.0
epsilon = 1e-05
highest = lax.Precision.HIGHEST

def layer_norm(values, gain_row):
    average = lax.optimization_barrier(jnp.mean(values, axis=-1, keepdims=True))
    centred = values - average
    spread = lax.optimization_barrier(jnp.mean(centred * centred, axis=-1, keepdims=True))
    return centred * lax.rsqrt(spread + epsilon) * gain_row

def modulate(values, gain_row, shift_by, scale_by):
    return layer_norm(values, gain_row) * (1.0 + scale_by) + shift_by

def rotary_tables():
    angular_rate = 10000.0 ** (-2.0 * jnp.arange(HEAD // 2, dtype=jnp.float32) / HEAD)
    places = jnp.arange(L, dtype=jnp.float32)
    angles = places[:, None] * angular_rate[None, :]
    angles = jnp.concatenate([angles, angles], axis=-1)
    return (jnp.cos(angles)[:, None, :], jnp.sin(angles)[:, None, :])

def rotate(values, cosine, sine_rows):
    half_dim = values.shape[-1] // 2
    turned = jnp.concatenate([-values[..., half_dim:], values[..., :half_dim]], axis=-1)
    return values * cosine + turned * sine_rows

def attend(queries, key_rows, value_rows):
    rows_block = min(512, L)
    blocks = queries.reshape(L // rows_block, rows_block, HEADS, HEAD)

    def one_block(query_block):
        scores = jnp.einsum('qhe,khe->hqk', query_block, key_rows, precision=highest) * HEAD ** (-0.5)
        scores = low_back(scores)
        weights = jax.nn.softmax(scores, axis=-1)
        return jnp.einsum('hqk,khe->qhe', low(weights), value_rows, precision=highest)
    return lax.map(jax.checkpoint(one_block), blocks).reshape(L, HEADS, HEAD)

def block_forward(parameters, tokens, condition):
    modulator, mod_bias, gain_attn, gain_mlp, query_key_value_matrix, output_matrix, up_matrix, up_offset_bias, down_matrix, down_bias = parameters
    group_size = tokens.shape[0]
    modulation = jnp.dot(condition, modulator, precision=highest) + mod_bias
    modulation = modulation.reshape(group_size, 6, 1, D)
    shift_attn, scale_attn, gate_attn, shift_mlp, perceptron_stretch, gate_mlp = [modulation[:, number] for number in range(6)]
    first_input = low(modulate(tokens, gain_attn, shift_attn, scale_attn))
    projected = low_back(jnp.einsum('gld,dce->glce', first_input, query_key_value_matrix, precision=highest))
    projected = projected.reshape(group_size, L, 3, HEADS, HEAD)
    cosine, sine_rows = rotary_tables()
    queries = low(rotate(projected[:, :, 0], cosine, sine_rows))
    key_rows = low(rotate(projected[:, :, 1], cosine, sine_rows))
    value_rows = low(projected[:, :, 2])
    blended_rows = jax.vmap(attend)(queries, key_rows, value_rows).reshape(group_size, L, D)
    blended_rows = low_back(low(blended_rows))
    attn_out = low_back(jnp.einsum('gle,ed->gld', blended_rows, output_matrix, precision=highest))
    resid = tokens + gate_attn * attn_out
    later_skip_stream = low(modulate(resid, gain_mlp, shift_mlp, perceptron_stretch))
    up_pre = low_back(jnp.einsum('gld,df->glf', later_skip_stream, up_matrix, precision=highest) + up_offset_bias)
    hidden_rows = low(jax.nn.gelu(up_pre, approximate=True))
    mlp_out = low_back(jnp.einsum('glf,fd->gld', hidden_rows, down_matrix, precision=highest) + down_bias)
    return resid + gate_mlp * mlp_out

def reference(activations, condition, modulator, mod_bias, gain_attn, gain_mlp, query_key_value_matrix, output_matrix, up_matrix, up_offset_bias, down_matrix, down_bias, upstream, span_start, span_length, noise_level):
    parameters = (modulator.astype(jnp.float32), mod_bias, gain_attn, gain_mlp, query_key_value_matrix.astype(jnp.float32), output_matrix.astype(jnp.float32), up_matrix.astype(jnp.float32), up_offset_bias, down_matrix.astype(jnp.float32), down_bias)
    places = jnp.arange(L, dtype=jnp.int32)
    inside = (places[None, :] >= span_start[:, None]) & (places[None, :] < (span_start + span_length)[:, None])
    noise_sigma = noise_low + (noise_high - noise_low) * (noise_level.astype(jnp.float32) + 0.5) / LEVELS
    factor = 1.0 / (1.0 - jnp.exp(-noise_sigma))
    loss_weight = jnp.where(inside, factor[:, None], jnp.zeros_like(factor)[:, None])
    cotangent = loss_weight[:, :, None] * upstream.astype(jnp.float32)
    group_size = math.gcd(B, max(1, 4096 // L))
    group_count = B // group_size

    def step_group(totals, inputs_now):
        tokens, conds, cots = inputs_now
        outputs, pullback = jax.vjp(block_forward, parameters, tokens, conds)
        param_grads, token_grads, cond_grads = pullback(cots)
        totals = jax.tree.map(lambda first_one, second_one: first_one + second_one, totals, param_grads)
        return (totals, (outputs, token_grads, cond_grads))
    zero_grads = jax.tree.map(jnp.zeros_like, parameters)
    totals, (outputs, token_grads, cond_grads) = lax.scan(step_group, zero_grads, (activations.astype(jnp.float32).reshape(group_count, group_size, L, D), condition.reshape(group_count, group_size, COND), cotangent.reshape(group_count, group_size, L, D)))
    block_out = outputs.reshape(B, L, D).astype(jnp.bfloat16)
    entering_state_slope = token_grads.reshape(B, L, D)
    condition_grad = cond_grads.reshape(B, COND)
    return (block_out, entering_state_slope, condition_grad, totals[0], totals[1], totals[2], totals[3], totals[4], totals[5], totals[6], totals[7], totals[8], totals[9])
```

```python
import jax
import jax.numpy as jnp
from jax import lax
from jax.experimental import pallas as pl
from jax.experimental.pallas import tpu as pltpu
from jax.sharding import PartitionSpec as P

D = 768
HEAD = 64
L = 1024
LEVELS = 1024
Z = 4

noise_low = 0.1
noise_high = 3.0
epsilon = 1e-05
highest = lax.Precision.HIGHEST
f32 = jnp.float32
bf16 = jnp.bfloat16
PIECE = 96
MIB = 1 << 20


def send(values, target, dp_size):
    pairs = []
    for d in range(dp_size):
        for t in range(Z):
            to_d, to_t = target(d, t)
            pairs.append((d * Z + t, to_d * Z + to_t))
    return lax.ppermute(values, ("dp", "tensor"), pairs)


def to_core(d, t):
    return (d ^ 1, t)


def to_first(d, t):
    return (d ^ (4 if d & 1 else 2), t)


def to_second(d, t):
    return (d ^ (2 if d & 1 else 4), t)


def to_back(shift):
    return lambda d, t: (d, (t - shift) % Z)


def to_ahead(shift):
    return lambda d, t: (d, (t + shift) % Z)


def to_flip(bit):
    return lambda d, t: (d ^ bit, t)


def to_flip_z(bit):
    return lambda d, t: (d, t ^ bit)


def chip_a(d, t):
    return (2 * (d // 2) + t // 2, 2 * (d % 2) + t % 2)


def chip_b(d, t):
    return (2 * (d // 2) + t // 2, 2 * (d % 2) + 1 - t % 2)


def inverse(target, dp_size):
    table = {target(d, t): (d, t) for d in range(dp_size) for t in range(Z)}
    return lambda d, t: table[(d, t)]


def pick(values, index, axis=0):
    return lax.dynamic_index_in_dim(values, index, axis, keepdims=False)


def normalize(values):
    average = jnp.mean(values, axis=-1, keepdims=True)
    centred = values - average
    spread = jnp.mean(centred * centred, axis=-1, keepdims=True)
    rate = lax.rsqrt(spread + epsilon)
    return centred * rate, rate


def normalize_back(cot, unit, rate):
    return rate * (
        cot
        - jnp.mean(cot, axis=-1, keepdims=True)
        - unit * jnp.mean(cot * unit, axis=-1, keepdims=True)
    )


def rotary_tables(places):
    angular_rate = 10000.0 ** (-2.0 * jnp.arange(HEAD // 2, dtype=f32) / HEAD)
    angles = places[:, None] * angular_rate[None, :]
    cosine, sine = jnp.cos(angles), jnp.sin(angles)
    cosine = jnp.concatenate([cosine, cosine], axis=-1)
    sine = jnp.concatenate([-sine, sine], axis=-1)
    heads = D // HEAD
    return jnp.tile(cosine, (1, heads)), jnp.tile(sine, (1, heads))


def swap_halves(values):
    half = HEAD // 2
    lane = lax.broadcasted_iota(jnp.int32, values.shape, 1)
    return jnp.where(lane % HEAD < half, jnp.roll(values, -half, 1), jnp.roll(values, half, 1))


def rotate(values, cosine, sine):
    return values * cosine + swap_halves(values) * sine


def rotate_back(cot, cosine, sine):
    return cot * cosine + swap_halves(cot * sine)


def dot(a, b, contract):
    return lax.dot_general(a, b, (contract, ((), ())), preferred_element_type=f32)


NN = ((1,), (0,))
NT = ((1,), (1,))
TN = ((0,), (0,))
SCALE = HEAD ** (-0.5)
QUERY_CHUNK = 256


def attend_kernel(q_ref, k_ref, v_ref, o_ref, lse_ref):
    rows = q_ref.shape[0]
    k = k_ref[...]
    v = v_ref[...]
    for start in range(0, rows, QUERY_CHUNK):
        span = pl.ds(start, QUERY_CHUNK)
        q = q_ref[span, :]
        lane = lax.broadcasted_iota(jnp.int32, q.shape, 1)
        mixed = None
        for head in range(2):
            mine = (lane < HEAD) if head == 0 else (lane >= HEAD)
            scores = dot(jnp.where(mine, q, jnp.zeros_like(q)), k, NT) * SCALE
            top = jnp.max(scores, axis=1, keepdims=True)
            weights = jnp.exp(scores - top)
            total = jnp.sum(weights, axis=1, keepdims=True)
            out = dot((weights / total).astype(bf16), v, NN)
            mixed = out if head == 0 else jnp.where(mine, out, mixed)
            lse = jnp.broadcast_to(top + jnp.log(total), (QUERY_CHUNK, 128))
            lse_ref[0, pl.ds(head, 1), span] = lse.T[0:1]
        o_ref[span, :] = mixed.astype(bf16)


def attend_forward(q, k, v):
    rows, keys = q.shape[0], k.shape[0]
    pairs = D // (2 * HEAD)
    return pl.pallas_call(
        attend_kernel,
        grid=(pairs,),
        in_specs=[
            pl.BlockSpec((rows, 128), lambda i: (0, i)),
            pl.BlockSpec((keys, 128), lambda i: (0, i)),
            pl.BlockSpec((keys, 128), lambda i: (0, i)),
        ],
        out_specs=[
            pl.BlockSpec((rows, 128), lambda i: (0, i)),
            pl.BlockSpec((1, 8, rows), lambda i: (i, 0, 0)),
        ],
        out_shape=[
            jax.ShapeDtypeStruct((rows, D), bf16),
            jax.ShapeDtypeStruct((pairs, 8, rows), f32),
        ],
        compiler_params=pltpu.CompilerParams(vmem_limit_bytes=40 * MIB),
        cost_estimate=pl.CostEstimate(
            flops=4 * rows * keys * D, transcendentals=rows * keys * 12, bytes_accessed=6 * MIB
        ),
        name="attend_forward",
    )(q, k, v)


def attend_back_kernel(q_ref, k_ref, v_ref, c_ref, lse_ref, dq_ref, dk_ref, dv_ref):
    rows = q_ref.shape[0]
    k = k_ref[...]
    v = v_ref[...]
    key_lane = lax.broadcasted_iota(jnp.int32, k.shape, 1)
    for start in range(0, rows, QUERY_CHUNK):
        span = pl.ds(start, QUERY_CHUNK)
        q = q_ref[span, :]
        c = c_ref[span, :]
        lane = lax.broadcasted_iota(jnp.int32, q.shape, 1)
        dq = dk = dv = None
        for head in range(2):
            mine = (lane < HEAD) if head == 0 else (lane >= HEAD)
            key_mine = (key_lane < HEAD) if head == 0 else (key_lane >= HEAD)
            qh = jnp.where(mine, q, jnp.zeros_like(q))
            ch = jnp.where(mine, c, jnp.zeros_like(c))
            kh = jnp.where(key_mine, k, jnp.zeros_like(k))
            lse = lse_ref[0, pl.ds(head, 1), span]
            probs = jnp.exp(dot(k, qh, NT) * SCALE - lse)
            prob_cot = dot(v, ch, NT)
            inner = jnp.sum(probs * prob_cot, axis=0, keepdims=True)
            score_cot = (probs * (prob_cot - inner)).astype(bf16)
            dvh = dot(probs.astype(bf16), ch, NN)
            dkh = dot(score_cot, qh, NN)
            dqh = dot(score_cot, kh, TN)
            dq = dqh if head == 0 else dq + dqh
            dk = dkh if head == 0 else dk + dkh
            dv = dvh if head == 0 else dv + dvh
        dq_ref[span, :] = dq * SCALE
        if start == 0:
            dk_ref[...] = dk * SCALE
            dv_ref[...] = dv
        else:
            dk_ref[...] += dk * SCALE
            dv_ref[...] += dv


def attend_backward(q, k, v, cot, lse):
    rows, keys = q.shape[0], k.shape[0]
    pairs = D // (2 * HEAD)
    own = pl.BlockSpec((rows, 128), lambda i: (0, i))
    whole = pl.BlockSpec((keys, 128), lambda i: (0, i))
    return pl.pallas_call(
        attend_back_kernel,
        grid=(pairs,),
        in_specs=[own, whole, whole, own, pl.BlockSpec((1, 8, rows), lambda i: (i, 0, 0))],
        out_specs=[own, whole, whole],
        out_shape=[
            jax.ShapeDtypeStruct((rows, D), f32),
            jax.ShapeDtypeStruct((keys, D), f32),
            jax.ShapeDtypeStruct((keys, D), f32),
        ],
        compiler_params=pltpu.CompilerParams(vmem_limit_bytes=48 * MIB),
        cost_estimate=pl.CostEstimate(
            flops=10 * rows * keys * D, transcendentals=rows * keys * 12, bytes_accessed=16 * MIB
        ),
        name="attend_backward",
    )(q, k, v, cot, lse)


def gather_pieces(piece, dp_size):
    near = send(piece, to_second, dp_size)
    pair = jnp.stack([piece, near])
    far = send(pair, to_first, dp_size)
    four = jnp.concatenate([pair, far])
    other = send(four, to_core, dp_size)
    return [four, other]


def weight_group(own, base, positions, dp_size, by_kind):
    mine = lax.dynamic_slice_in_dim(own, base * PIECE, PIECE, 0)
    apart = jnp.stack([send(mine, to_back(r), dp_size) for r in range(1, Z)])
    four, other = gather_pieces(apart, dp_size)
    if by_kind:
        shape = (4, Z, 2, PIECE, D)
        out_spec = pl.BlockSpec(
            (1, Z, 1, PIECE, D), lambda i, place: (place[i] // 2, 0, place[i] % 2, 0, 0)
        )
    else:
        shape = (Z, 8, PIECE, D)
        out_spec = pl.BlockSpec((Z, 1, PIECE, D), lambda i, place: (0, place[i], 0, 0))

    def kernel(place_ref, own_ref, four_ref, other_ref, out_ref):
        i = pl.program_id(0)

        def put(r, block):
            if by_kind:
                out_ref[0, r, 0] = block
            else:
                out_ref[r, 0] = block

        put(0, own_ref[0])

        @pl.when(i < 4)
        def _():
            for r in range(1, Z):
                put(r, four_ref[0, r - 1])

        @pl.when(i >= 4)
        def _():
            for r in range(1, Z):
                put(r, other_ref[0, r - 1])

    part = (1, Z - 1, PIECE, D)
    return pl.pallas_call(
        kernel,
        grid_spec=pltpu.PrefetchScalarGridSpec(
            num_scalar_prefetch=1,
            grid=(8,),
            in_specs=[
                pl.BlockSpec((1, PIECE, D), lambda i, place: (place[i], 0, 0)),
                pl.BlockSpec(part, lambda i, place: (jnp.minimum(i, 3), 0, 0, 0)),
                pl.BlockSpec(part, lambda i, place: (jnp.maximum(i - 4, 0), 0, 0, 0)),
            ],
            out_specs=out_spec,
        ),
        out_shape=jax.ShapeDtypeStruct(shape, bf16),
        cost_estimate=pl.CostEstimate(flops=0, transcendentals=0, bytes_accessed=8 * MIB),
        name="place_weights",
    )(positions, own.reshape(8, PIECE, D), four, other)


def reduce_group(grad, core, first, second, dp_size):
    grad = grad.reshape(Z, 2, 2, 2, PIECE, D)
    got = send(pick(grad, 1 - core, 1).astype(bf16), to_core, dp_size)
    grad = pick(grad, core, 1) + got.astype(f32)
    got = send(pick(grad, 1 - first, 1).astype(bf16), to_first, dp_size)
    grad = pick(grad, first, 1) + got.astype(f32)
    got = send(pick(grad, 1 - second, 1).astype(bf16), to_second, dp_size)
    grad = pick(grad, second, 1) + got.astype(f32)
    total = grad[0]
    for r in range(1, Z):
        total = total + send(grad[r].astype(bf16), to_ahead(r), dp_size).astype(f32)
    bit = 8
    while bit < dp_size:
        total = total + send(total, to_flip(bit), dp_size)
        bit *= 2
    return total


def spread_group(total, positions, dp_size):
    four, other = gather_pieces(total, dp_size)

    def kernel(place_ref, four_ref, other_ref, out_ref):
        i = pl.program_id(0)

        @pl.when(i < 4)
        def _():
            out_ref[...] = four_ref[...]

        @pl.when(i >= 4)
        def _():
            out_ref[...] = other_ref[...]

    part = (1, PIECE, D)
    return pl.pallas_call(
        kernel,
        grid_spec=pltpu.PrefetchScalarGridSpec(
            num_scalar_prefetch=1,
            grid=(8,),
            in_specs=[
                pl.BlockSpec(part, lambda i, place: (jnp.minimum(i, 3), 0, 0)),
                pl.BlockSpec(part, lambda i, place: (jnp.maximum(i - 4, 0), 0, 0)),
            ],
            out_specs=pl.BlockSpec(part, lambda i, place: (place[i], 0, 0)),
        ),
        out_shape=jax.ShapeDtypeStruct((8, PIECE, D), f32),
        cost_estimate=pl.CostEstimate(flops=0, transcendentals=0, bytes_accessed=5 * MIB),
        name="place_gradient",
    )(positions, four, other).reshape(8 * PIECE, D)


def gelu_parts(values):
    rate = 0.7978845608
    square = values * values
    bent = jnp.tanh(rate * values * (1.0 + 0.044715 * square))
    half = 0.5 * (1.0 + bent)
    slope = half + 0.5 * values * (1.0 - bent * bent) * rate * (1.0 + 3 * 0.044715 * square)
    return values * half, slope


def shards(
    activations,
    condition,
    modulator,
    mod_bias,
    gain_attn,
    gain_mlp,
    query_key_value_matrix,
    output_matrix,
    up_matrix,
    up_offset_bias,
    down_matrix,
    down_bias,
    upstream,
    span_start,
    span_length,
    noise_level,
):
    dp_size = lax.axis_size("dp")
    d = lax.axis_index("dp")
    z = lax.axis_index("tensor")
    rows = activations.shape[1]
    core = d % 2
    x_bit, y_bit = (d // 2) % 2, (d // 4) % 2
    first = jnp.where(core == 0, x_bit, y_bit)
    second = jnp.where(core == 0, y_bit, x_bit)
    base = core * 4 + first * 2 + second
    across = (1 - core) * 4 + second * 2 + first
    positions = jnp.stack(
        [base, base ^ 1, base ^ 2, base ^ 3, across, across ^ 1, across ^ 2, across ^ 3]
    ).astype(jnp.int32)
    odd = z % 2

    def to_chip(values):
        return jnp.concatenate(
            [
                send(pick(values, odd), chip_a, dp_size),
                send(pick(values, 1 - odd), chip_b, dp_size),
            ]
        )

    def from_chip(values):
        block_a = send(values[:rows], inverse(chip_a, dp_size), dp_size)
        block_b = send(values[rows:], inverse(chip_b, dp_size), dp_size)
        return jnp.where(odd == 0, jnp.stack([block_a, block_b]), jnp.stack([block_b, block_a]))

    tokens = to_chip(activations).astype(f32)
    scalars = jnp.concatenate(
        [
            condition,
            span_start.astype(f32)[:, None],
            span_length.astype(f32)[:, None],
            noise_level.astype(f32)[:, None],
            jnp.zeros((2, 125), f32),
        ],
        axis=1,
    )
    scalars_other = send(scalars, to_core, dp_size)
    facts = jnp.where(core == z // 2, pick(scalars, odd), pick(scalars_other, odd))
    cond_row = facts[None, :128]
    start, length, level = facts[128], facts[129], facts[130]
    step = jnp.arange(rows, dtype=f32)
    places = jnp.concatenate(
        [
            (2 * core + odd).astype(f32) * rows + step,
            (2 * core + 1 - odd).astype(f32) * rows + step,
        ]
    )

    attn_block = jnp.concatenate(
        [jnp.transpose(query_key_value_matrix, (1, 2, 0)).reshape(-1, D), output_matrix]
    )
    attn_weights = weight_group(attn_block, base, positions, dp_size, True).reshape(4, D, D)
    up_weights = weight_group(up_matrix, base, positions, dp_size, False).reshape(Z, D, D)
    down_weights = weight_group(down_matrix, base, positions, dp_size, False).reshape(Z, D, D)
    up_row = up_offset_bias[None]
    up_bias = jnp.stack([up_row] + [send(up_row, to_back(r), dp_size) for r in range(1, Z)])
    upstream_rows = to_chip(upstream).astype(f32)

    modulator_wide = modulator.astype(f32)
    modulation = jnp.dot(cond_row, modulator_wide, precision=highest) + mod_bias
    shift_attn, scale_attn, gate_attn, shift_mlp, scale_mlp, gate_mlp = [
        modulation[:, D * i : D * (i + 1)] for i in range(6)
    ]
    gain_attn = gain_attn[None]
    gain_mlp = gain_mlp[None]

    unit_attn, rate_attn = normalize(tokens)
    first_in = (unit_attn * gain_attn * (1.0 + scale_attn) + shift_attn).astype(bf16)
    cosine, sine = rotary_tables(places)
    q = rotate(dot(first_in, attn_weights[0], NT), cosine, sine).astype(bf16)
    k = rotate(dot(first_in, attn_weights[1], NT), cosine, sine).astype(bf16)
    v = dot(first_in, attn_weights[2], NT).astype(bf16)
    kv = jnp.stack([k, v], axis=0)
    kv_other = send(kv, to_core, dp_size)
    k_all = jnp.concatenate([k, kv_other[0]])
    v_all = jnp.concatenate([v, kv_other[1]])
    mixed, lse = attend_forward(q, k_all, v_all)
    attn_out = dot(mixed, attn_weights[3], NN)
    resid = tokens + gate_attn * attn_out
    unit_mlp, rate_mlp = normalize(resid)
    second_in = (unit_mlp * gain_mlp * (1.0 + scale_mlp) + shift_mlp).astype(bf16)

    sigma = noise_low + (noise_high - noise_low) * (level + 0.5) / LEVELS
    factor = 1.0 / (1.0 - jnp.exp(-sigma))
    inside = (places >= start) & (places < start + length)
    loss_weight = jnp.where(inside, factor, 0.0)[:, None]
    out_cot = loss_weight * upstream_rows
    mlp_cot = (gate_mlp * out_cot).astype(bf16)
    downbias_part = jnp.sum(mlp_cot.astype(f32), axis=0, keepdims=True)

    mlp_out = down_bias[None]
    second_cot = 0.0
    up_grads, down_grads, upbias_parts = [], [], []
    for r in range(Z):
        up_pre = dot(second_in, up_weights[r], NN) + up_bias[r]
        hidden, slope = gelu_parts(up_pre)
        hidden = hidden.astype(bf16)
        mlp_out = mlp_out + dot(hidden, down_weights[r], NN)
        down_grads.append(dot(hidden, mlp_cot, TN))
        hidden_cot = dot(mlp_cot, down_weights[r], NT)
        up_cot = (hidden_cot * slope).astype(bf16)
        upbias_parts.append(jnp.sum(up_cot.astype(f32), axis=0, keepdims=True))
        up_grads.append(dot(second_in, up_cot, TN))
        second_cot = second_cot + dot(up_cot, up_weights[r], NT)
    block_out = from_chip((resid + gate_mlp * mlp_out).astype(bf16))
    gatemlp_grad = jnp.sum(mlp_out * out_cot, axis=0, keepdims=True)
    down_total = reduce_group(jnp.stack(down_grads), core, first, second, dp_size)
    up_total = reduce_group(jnp.stack(up_grads), core, first, second, dp_size)

    shiftmlp_grad = jnp.sum(second_cot, axis=0, keepdims=True)
    second_unit = jnp.sum(second_cot * unit_mlp, axis=0, keepdims=True)
    scalemlp_grad = second_unit * gain_mlp
    gainmlp_part = second_unit * (1.0 + scale_mlp)
    resid_cot = out_cot + normalize_back(
        second_cot * ((1.0 + scale_mlp) * gain_mlp), unit_mlp, rate_mlp
    )
    gateattn_grad = jnp.sum(attn_out * resid_cot, axis=0, keepdims=True)
    attn_cot = (gate_attn * resid_cot).astype(bf16)

    out_grad = dot(mixed, attn_cot, TN)
    mixed_cot = dot(attn_cot, attn_weights[3], NT).astype(bf16)
    dq, dk, dv = attend_backward(q, k_all, v_all, mixed_cot, lse)
    half_rows = 2 * rows
    dkv = jnp.stack([dk[half_rows:], dv[half_rows:]])
    dkv_other = send(dkv, to_core, dp_size)
    dk = dk[:half_rows] + dkv_other[0]
    dv = dv[:half_rows] + dkv_other[1]
    dq = rotate_back(dq, cosine, sine).astype(bf16)
    dk = rotate_back(dk, cosine, sine).astype(bf16)
    dv = dv.astype(bf16)
    blocks = [dot(one, first_in, TN).reshape(Z, -1, D) for one in (dq, dk, dv)]
    blocks.append(out_grad.reshape(Z, -1, D))
    attn_total = reduce_group(
        jnp.concatenate(blocks, axis=1), core, first, second, dp_size
    )
    first_cot = (
        dot(dq, attn_weights[0], NN) + dot(dk, attn_weights[1], NN) + dot(dv, attn_weights[2], NN)
    )
    shiftattn_grad = jnp.sum(first_cot, axis=0, keepdims=True)
    first_unit = jnp.sum(first_cot * unit_attn, axis=0, keepdims=True)
    scaleattn_grad = first_unit * gain_attn
    gainattn_part = first_unit * (1.0 + scale_attn)
    entering = resid_cot + normalize_back(
        first_cot * ((1.0 + scale_attn) * gain_attn), unit_attn, rate_attn
    )
    entering_state_slope = from_chip(entering)

    attn_grad = spread_group(attn_total, positions, dp_size)
    up_grad = spread_group(up_total, positions, dp_size)
    down_grad = spread_group(down_total, positions, dp_size)
    qkv_rows = attn_grad.shape[0] * 3 // 4
    qkv_grad = jnp.transpose(attn_grad[:qkv_rows].reshape(3, -1, D), (2, 0, 1))
    out_grad = attn_grad[qkv_rows:]

    vectors = jnp.concatenate(
        [
            shiftattn_grad,
            scaleattn_grad,
            gateattn_grad,
            shiftmlp_grad,
            scalemlp_grad,
            gatemlp_grad,
            gainattn_part,
            gainmlp_part,
            downbias_part,
            jnp.roll(jnp.concatenate(upbias_parts), z, axis=0),
        ]
    )
    vectors = vectors + send(vectors, to_core, dp_size)
    sums = vectors[6:]
    cond_pad = jnp.concatenate([cond_row, jnp.zeros((1, D - 128), f32)], axis=1)
    each = jnp.concatenate([vectors[:6], cond_pad])[None]
    bits = []
    bit = 2
    while bit < dp_size:
        bits.append((to_flip(bit), (d // bit) % 2))
        bit *= 2
    bits += [(to_flip_z(1), z % 2), (to_flip_z(2), z // 2)]
    for target, bit_here in bits:
        count = each.shape[0]
        load = jnp.concatenate([each.reshape(-1, D), sums])
        got = send(load, target, dp_size)
        sums = sums + got[count * 7 :]
        got_each = got[: count * 7].reshape(count, 7, D)
        each = jnp.where(
            bit_here == 0,
            jnp.concatenate([each, got_each]),
            jnp.concatenate([got_each, each]),
        )
    cots = each[:, :6].reshape(-1, 6 * D)
    conds = each[:, 6, :128]
    modulator_grad = lax.dot_general(
        conds, cots, (TN, ((), ())), precision=highest, preferred_element_type=f32
    )
    modbias_grad = jnp.sum(cots, axis=0)
    columns = cots.reshape(Z, dp_size // 2, 6 * D)
    mine = lax.dynamic_slice(columns, (2 * core, d // 2, 0), (2, 1, 6 * D)).reshape(2, 6 * D)
    condition_grad = lax.dot_general(
        mine, modulator_wide, (NT, ((), ())), precision=highest, preferred_element_type=f32
    )
    gainattn_grad, gainmlp_grad, downbias_grad = sums[0], sums[1], sums[2]
    upbias_grad = pick(sums[3:], z)
    return (
        block_out,
        entering_state_slope,
        condition_grad,
        modulator_grad,
        modbias_grad,
        gainattn_grad,
        gainmlp_grad,
        qkv_grad,
        out_grad,
        up_grad,
        upbias_grad,
        down_grad,
        downbias_grad,
    )


def solution(mesh):
    in_specs = (
        P("dp", "tensor", None),
        P("dp", None),
        P(),
        P(),
        P(),
        P(),
        P(None, None, "tensor"),
        P("tensor", None),
        P(None, "tensor"),
        P("tensor"),
        P("tensor", None),
        P(),
        P("dp", "tensor", None),
        P("dp"),
        P("dp"),
        P("dp"),
    )
    out_specs = (
        P("dp", "tensor", None),
        P("dp", "tensor", None),
        P("dp", None),
        P(),
        P(),
        P(),
        P(),
        P(None, None, "tensor"),
        P("tensor", None),
        P(None, "tensor"),
        P("tensor"),
        P("tensor", None),
        P(),
    )
    return jax.shard_map(shards, mesh=mesh, in_specs=in_specs, out_specs=out_specs, check_vma=False)
```

```python
import jax
import jax.numpy as jnp
import numpy as np
from jax import lax
from jax.experimental import pallas as pl
from jax.experimental.pallas import tpu as pltpu
from jax.sharding import PartitionSpec as P

D = 768
HALF = 384
HEAD = 64
HEADS = 12
L = 1024
LEVELS = 1024
Z = 4
KIND = 192
WIDE = 400

noise_low = 0.1
noise_high = 3.0
epsilon = 1e-05
highest = lax.Precision.HIGHEST
f32 = jnp.float32
bf16 = jnp.bfloat16
MIB = 1 << 20

NN = ((1,), (0,))
NT = ((1,), (1,))
TN = ((0,), (0,))
SCALE = HEAD ** (-0.5)
CROSS = (0, 2, 1, 3)


def dot(a, b, contract):
    return lax.dot_general(a, b, (contract, ((), ())), preferred_element_type=f32)


def struct(shape, dtype):
    return jax.ShapeDtypeStruct(shape, dtype)


def send(values, target, dp_size):
    pairs = []
    for d in range(dp_size):
        for t in range(Z):
            to_d, to_t = target(d, t)
            pairs.append((d * Z + t, to_d * Z + to_t))
    return lax.ppermute(values, ("dp", "tensor"), pairs)


def to_core(d, t):
    return (d ^ 1, t)


def to_first(d, t):
    return (d ^ (4 if d & 1 else 2), t)


def to_second(d, t):
    return (d ^ (2 if d & 1 else 4), t)


def to_back(shift):
    return lambda d, t: (d, (t - shift) % Z)


def to_ahead(shift):
    return lambda d, t: (d, (t + shift) % Z)


def to_flip(bit):
    return lambda d, t: (d ^ bit, t)


def to_flip_z(bit):
    return lambda d, t: (d, t ^ bit)


def chip_a(d, t):
    return (2 * (d // 2) + t // 2, 2 * (d % 2) + t % 2)


def chip_b(d, t):
    return (2 * (d // 2) + t // 2, 2 * (d % 2) + 1 - t % 2)


def inverse(target, dp_size):
    table = {target(d, t): (d, t) for d in range(dp_size) for t in range(Z)}
    return lambda d, t: table[(d, t)]


def pick(values, index, axis=0):
    return lax.dynamic_index_in_dim(values, index, axis, keepdims=False)


def meta_table(rows):
    table = np.zeros((8, Z, 32), np.int32)
    for d in range(8):
        core, x, y = d & 1, (d >> 1) & 1, (d >> 2) & 1
        kind = 2 * x + y
        second, first = (1, 2) if core == 0 else (2, 1)
        listed = [kind, kind ^ second, kind ^ first, kind ^ 3]
        for z in range(Z):
            table[d, z, 0] = core
            for e, k in enumerate(listed):
                table[d, z, 1 + k] = e
                table[d, z, 5 + k] = CROSS[e]
                table[d, z, 9 + e] = k
            for r in range(1, Z):
                table[d, z, 15 + r] = (z + r) % Z
            for e, k in enumerate(listed):
                chip = 4 * (k & 1) + 2 * (k >> 1)
                table[d, z, 20 + e] = chip + core
                table[d, z, 24 + e] = chip + 1 - core
            table[d, z, 13] = (2 * core + z % 2) * rows
            table[d, z, 14] = (2 * core + 1 - z % 2) * rows
    return jnp.asarray(table)


def mine_rest(meta):
    core = meta[0]
    return (
        pl.ds(pl.multiple_of(core * HALF, 128), HALF),
        pl.ds(pl.multiple_of((1 - core) * HALF, 128), HALF),
    )


def normalize(values):
    average = jnp.mean(values, axis=-1, keepdims=True)
    centred = values - average
    spread = jnp.mean(centred * centred, axis=-1, keepdims=True)
    rate = lax.rsqrt(spread + epsilon)
    return centred * rate, rate


def normalize_back(cot, unit, rate):
    return rate * (
        cot
        - jnp.mean(cot, axis=-1, keepdims=True)
        - unit * jnp.mean(cot * unit, axis=-1, keepdims=True)
    )


CHUNK = 64
(
    SHIFT_ATTN,
    SCALE_ATTN,
    GATE_ATTN,
    SHIFT_MLP,
    SCALE_MLP,
    GATE_MLP,
    GAIN_ATTN,
    GAIN_MLP,
    DOWN_BIAS,
    START,
    END,
    FACTOR,
) = range(12)


def row(ref, number):
    return ref[number : number + 1, :]


def loss_weight(meta, part, start, rows_ref):
    place = lax.broadcasted_iota(jnp.int32, (CHUNK, 1), 0) + (meta[13 + part] + start)
    place = place.astype(f32)
    inside = (place >= rows_ref[START : START + 1, 0:1]) & (place < rows_ref[END : END + 1, 0:1])
    return jnp.where(inside, rows_ref[FACTOR : FACTOR + 1, 0:1], 0.0)


def spec(shape, index=None):
    if index is None:
        index = lambda i, meta: (0,) * len(shape)
    return pl.BlockSpec(shape, index)


def call(kernel, meta, args, in_specs, out_shape, out_specs, grid, name, flops, moved, **more):
    scratch = more.pop("scratch", ())
    into = more.pop("into", ())
    after = list(into) + [one for one in more.pop("after", ()) if one is not None]
    count, extra = len(args), len(after)
    more = {1 + i: o for i, o in more.pop("alias", {}).items()}

    def body(meta_ref, *refs):
        kernel(meta_ref, *refs[:count], *refs[count + extra :])

    return pl.pallas_call(
        body,
        grid_spec=pltpu.PrefetchScalarGridSpec(
            num_scalar_prefetch=1,
            grid=(grid,),
            in_specs=list(in_specs) + [pl.BlockSpec(memory_space=pl.ANY)] * extra,
            out_specs=out_specs,
            scratch_shapes=list(scratch),
        ),
        out_shape=out_shape,
        compiler_params=pltpu.CompilerParams(vmem_limit_bytes=50 * MIB),
        cost_estimate=pl.CostEstimate(
            flops=int(flops), transcendentals=0, bytes_accessed=int(moved)
        ),
        name=name,
        input_output_aliases={1 + count + i: i for i in range(len(into))} | more,
    )(meta, *args, *after)


class Box:
    def __init__(self, array):
        self.a = array


class Flow:
    def __init__(self, dp_size):
        self.dp_size, self.open, self.token = dp_size, [], None

    def keep(self, array):
        box = Box(array)
        self.open.append(box)
        return box

    def tied(self, array):
        if self.token is None:
            return array
        return lax.optimization_barrier((array, self.token))[0]

    def send(self, array, target):
        return self.keep(send(self.tied(array), target, self.dp_size))

    def run(self, function, *args, **more):
        after = () if self.token is None else (self.token,)
        return [self.keep(one) for one in function(*args, after=after, **more)]

    def fence(self):
        arrays = lax.optimization_barrier(tuple(box.a for box in self.open))
        for box, array in zip(self.open, arrays):
            box.a = array
        self.token = min(arrays, key=lambda one: one.size)
        self.open = []


def prepare_kernel(meta, up_ref, down_ref, bias_ref, mine_ref, rest_ref, turned):
    mine, rest = mine_rest(meta)
    turned[...] = up_ref[...].astype(f32).T.astype(bf16)
    for e in range(4):
        kind = meta[9 + e]
        rows = pl.ds(pl.multiple_of(kind * KIND, KIND), KIND)
        for half, out, place in ((mine, mine_ref, e), (rest, rest_ref, CROSS[e])):
            out[place, 0:KIND] = turned[rows, half]
            out[place, KIND : 2 * KIND] = down_ref[rows, half]
            tail = bias_ref[kind]
            high = tail.astype(bf16)
            left = tail - high.astype(f32)
            middle = left.astype(bf16)
            low = (left - middle.astype(f32)).astype(bf16)
            number = lax.broadcasted_iota(jnp.int32, (16, HALF), 0)
            block = jnp.where(
                number == 0,
                high.astype(f32),
                jnp.where(
                    number == 1,
                    middle.astype(f32),
                    jnp.where(number == 2, low.astype(f32), 0.0),
                ),
            )
            out[place, 2 * KIND : WIDE] = block.astype(bf16)


def prepare(meta, up_matrix, down_matrix, up_bias, after=()):
    padded = jnp.pad(up_bias.reshape(4, 1, KIND), ((0, 0), (0, 0), (0, HALF - KIND)))
    out = (4, WIDE, HALF)
    return call(
        prepare_kernel,
        meta,
        (up_matrix, down_matrix, padded),
        [spec((D, D)), spec((D, D)), spec((4, 1, HALF))],
        [struct(out, bf16)] * 2,
        [spec(out)] * 2,
        1,
        "prepare_weights",
        0,
        5 * MIB,
        scratch=[pltpu.VMEM((D, D), bf16)],
        after=after,
    )


def enter_kernel(
    meta, xa, xb, rows_ref, cos_ref, sin_ref, own, four, other, first_ref, q_ref, kv_ref
):
    k = pl.program_id(0)
    mine, rest = mine_rest(meta)

    @pl.when(k == 0)
    def _():
        for part, ref in enumerate((xa, xb)):
            size = ref.shape[0]
            for start in range(0, size, CHUNK):
                some = pl.ds(start, CHUNK)
                x = jnp.concatenate([ref[some, mine], ref[some, rest]], axis=1).astype(f32)
                unit, _ = normalize(x)
                value = unit * row(rows_ref, GAIN_ATTN) * (1.0 + row(rows_ref, SCALE_ATTN))
                value = value + row(rows_ref, SHIFT_ATTN)
                value = value.astype(bf16)
                first_ref[pl.ds(part * size + start, CHUNK), :] = value

        kv_ref[2 * D :, :] = first_ref[:, HALF:].T

    first_m, first_o = first_ref[:, :HALF], first_ref[:, HALF:]
    near = dot(own[0, :, mine], first_m, NT) + dot(own[0, :, rest], first_o, NT)
    far = dot(four[0].reshape(3 * KIND, HALF), first_m, NT)
    far = far + dot(other[0].reshape(3 * KIND, HALF), first_o, NT)

    def head(h):
        return near[h * HEAD : (h + 1) * HEAD] if h < 3 else far[(h - 3) * HEAD : (h - 2) * HEAD]

    def put(write, turn):
        for h in range(HEADS):
            block = head(h)
            if turn:
                low, high = block[: HEAD // 2], block[HEAD // 2 :]
                cosine, sine = cos_ref[...], sin_ref[...]
                write(h * HEAD, (low * cosine - high * sine).astype(bf16))
                write(h * HEAD + HEAD // 2, (high * cosine + low * sine).astype(bf16))
            else:
                write(h * HEAD, block.astype(bf16))

    def write_q(start, block):
        q_ref[pl.ds(start, block.shape[0]), :] = block

    def write_k(start, block):
        kv_ref[pl.ds(start, block.shape[0]), :] = block

    def write_v(start, block):
        kv_ref[pl.ds(D + start, block.shape[0]), :] = block

    @pl.when(k == 0)
    def _():
        put(write_q, True)

    @pl.when(k == 1)
    def _():
        put(write_k, True)

    @pl.when(k == 2)
    def _():
        put(write_v, False)


def piece_specs(kind_of):
    return [
        spec((1, 3, KIND, HALF), lambda i, meta: (meta[1 + kind_of(i)], 0, 0, 0)),
        spec((1, 3, KIND, HALF), lambda i, meta: (meta[5 + kind_of(i)], 0, 0, 0)),
    ]


def enter(meta, xa, xb, rows, cosine, sine, own, four, other, after=()):
    tokens = 2 * xa.shape[0]
    return call(
        enter_kernel,
        meta,
        (xa, xb, rows, cosine, sine, own, four, other),
        [
            spec(xa.shape),
            spec(xb.shape),
            spec(rows.shape),
            spec(cosine.shape),
            spec(sine.shape),
            spec((1, KIND, D), lambda i, meta: (i, 0, 0)),
        ]
        + piece_specs(lambda i: i),
        [
            struct((tokens, D), bf16),
            struct((D, tokens), bf16),
            struct((2 * D + HALF, tokens), bf16),
        ],
        [
            spec((tokens, D)),
            spec((D, tokens)),
            spec((2 * D + HALF, tokens)),
        ],
        3,
        "norm_project",
        2 * 3 * tokens * D * D,
        8 * MIB,
        after=after,
    )


def attend_kernel(meta, q_ref, k_ref, v_ref, ko_ref, vo_ref, o_ref, lse_ref):
    tokens = q_ref.shape[1]
    width = min(256, tokens)
    for start in range(0, tokens, width):
        some = pl.ds(start, width)
        q = q_ref[:, some] * bf16(SCALE)
        near = dot(k_ref[...], q, TN)
        far = dot(ko_ref[...], q, TN)
        top = jnp.maximum(
            jnp.max(near, axis=0, keepdims=True), jnp.max(far, axis=0, keepdims=True)
        )
        near = jnp.exp(near - top)
        far = jnp.exp(far - top)
        total = jnp.sum(near, axis=0, keepdims=True) + jnp.sum(far, axis=0, keepdims=True)
        share = 1.0 / total
        mixed = dot(v_ref[...], (near * share).astype(bf16), NN)
        mixed = mixed + dot(vo_ref[...], (far * share).astype(bf16), NN)
        o_ref[:, some] = mixed.astype(bf16)
        lse_ref[0, :, some] = top + jnp.log(total)


def attend_forward(meta, base, count, q, kv, kv_other, after=()):
    tokens = q.shape[1]
    own = spec((HEAD, tokens), lambda i, meta: (base + i, 0))
    first = own
    second = spec((HEAD, tokens), lambda i, meta: (HEADS + base + i, 0))
    return call(
        attend_kernel,
        meta,
        (q, kv, kv, kv_other, kv_other),
        [own, first, second, first, second],
        [struct((count * HEAD, tokens), bf16), struct((count, 1, tokens), f32)],
        [
            spec((HEAD, tokens), lambda i, meta: (i, 0)),
            spec((1, 1, tokens), lambda i, meta: (i, 0, 0)),
        ],
        count,
        "attend_forward",
        16 * 2 * 2 * tokens * tokens * D * count // HEADS,
        5 * MIB * count // HEADS,
        after=after,
    )


def attend_back_kernel(
    meta,
    q_ref,
    k_ref,
    v_ref,
    ko_ref,
    vo_ref,
    c_ref,
    lse_ref,
    cos_ref,
    sin_ref,
    own_ref,
    give_ref,
):
    tokens = q_ref.shape[1]
    width = min(256, tokens)
    for start in range(0, tokens, width):
        some = pl.ds(start, width)
        q = q_ref[:, some] * bf16(SCALE)
        c = c_ref[:, some]
        lse = lse_ref[0, :, some]
        sides = ((k_ref[...], v_ref[...]), (ko_ref[...], vo_ref[...]))
        probs = [jnp.exp(dot(k, q, TN) - lse) for k, _ in sides]
        cots = [dot(v, c, TN) for _, v in sides]
        inner = jnp.sum(probs[0] * cots[0], axis=0, keepdims=True)
        inner = inner + jnp.sum(probs[1] * cots[1], axis=0, keepdims=True)
        dq = None
        for number, (k, _) in enumerate(sides):
            score_cot = (probs[number] * (cots[number] - inner)).astype(bf16)
            dk = dot(q, score_cot, NT)
            dv = dot(c, probs[number].astype(bf16), NT)
            if start == 0:
                own_ref[number, 0] = dk
                own_ref[number, 1] = dv
            else:
                own_ref[number, 0] += dk
                own_ref[number, 1] += dv
            part = dot(k, score_cot, NN)
            dq = part if dq is None else dq + part
        low, high = dq[: HEAD // 2] * SCALE, dq[HEAD // 2 :] * SCALE
        cosine, sine = cos_ref[:, some], sin_ref[:, some]
        give_ref[4, 0 : HEAD // 2, some] = (low * cosine + high * sine).astype(bf16)
        give_ref[4, HEAD // 2 : HEAD, some] = (high * cosine - low * sine).astype(bf16)
    for number in range(4):
        give_ref[number] = own_ref[number // 2, number % 2].astype(bf16)


def attend_backward(meta, base, count, q, kv, kv_other, cot, lse, cosine, sine, after=()):
    tokens = q.shape[1]
    own = spec((HEAD, tokens), lambda i, meta: (base + i, 0))
    first = own
    second = spec((HEAD, tokens), lambda i, meta: (HEADS + base + i, 0))
    part = (2, 2, HEAD, tokens)
    shape = (2, 2, count * HEAD, tokens)
    return call(
        attend_back_kernel,
        meta,
        (q, kv, kv, kv_other, kv_other, cot, lse, cosine, sine),
        [
            own,
            first,
            second,
            first,
            second,
            own,
            spec((1, 1, tokens), lambda i, meta: (i, 0, 0)),
            spec(cosine.shape),
            spec(sine.shape),
        ],
        [struct(shape, f32), struct((5, count * HEAD, tokens), bf16)],
        [
            spec(part, lambda i, meta: (0, 0, i, 0)),
            spec((5, HEAD, tokens), lambda i, meta: (0, i, 0)),
        ],
        count,
        "attend_backward",
        16 * 5 * 2 * tokens * tokens * D * count // HEADS,
        10 * MIB,
        after=after,
    )


def middle_kernel(
    meta,
    mixed_a,
    mixed_b,
    mixed_c,
    own,
    four,
    other,
    xa,
    xb,
    ua,
    ub,
    rows_ref,
    attn_ref,
    resid_ref,
    second_ref,
    cot_ref,
    give_ref,
    vec_ref,
):
    mine, rest = mine_rest(meta)
    near = mixed_a[:KIND, :]
    far = jnp.concatenate([mixed_a[KIND:, :], mixed_b[...], mixed_c[...]], axis=0)
    attn_ref[:, :HALF] = dot(near, own[:, mine], TN) + dot(
        far, four[0].reshape(3 * KIND, HALF), TN
    )
    attn_ref[:, HALF:] = dot(near, own[:, rest], TN) + dot(
        far, other[0].reshape(3 * KIND, HALF), TN
    )
    total = jnp.zeros((1, D), f32)
    for part, (x_ref, u_ref) in enumerate(((xa, ua), (xb, ub))):
        size = x_ref.shape[0]
        for start in range(0, size, CHUNK):
            some = pl.ds(start, CHUNK)
            here = pl.ds(part * size + start, CHUNK)
            x = jnp.concatenate([x_ref[some, mine], x_ref[some, rest]], axis=1).astype(f32)
            resid = x + row(rows_ref, GATE_ATTN) * attn_ref[here, :]
            resid_ref[here, :] = resid
            unit, _ = normalize(resid)
            value = unit * row(rows_ref, GAIN_MLP) * (1.0 + row(rows_ref, SCALE_MLP))
            second = (value + row(rows_ref, SHIFT_MLP)).astype(bf16)
            second_ref[here, :] = second
            give_ref[0, here, :] = second[:, HALF:]
            up = jnp.concatenate([u_ref[some, mine], u_ref[some, rest]], axis=1).astype(f32)
            cot = loss_weight(meta, part, start, rows_ref) * up
            cot = (row(rows_ref, GATE_MLP) * cot).astype(bf16)
            cot_ref[here, :] = cot
            give_ref[1, here, :] = cot[:, HALF:]
            total = total + jnp.sum(cot.astype(f32), axis=0, keepdims=True)
    vec_ref[...] = jnp.broadcast_to(total, (8, D))


def middle(meta, mixed, own, four, other, xa, xb, ua, ub, rows, after=()):
    tokens = mixed[0].shape[1]
    whole = (tokens, D)
    return call(
        middle_kernel,
        meta,
        (*mixed, own, four, other, xa, xb, ua, ub, rows),
        [spec(one.shape) for one in mixed]
        + [spec(own.shape)]
        + piece_specs(lambda i: 3)
        + [spec(xa.shape)] * 4
        + [spec(rows.shape)],
        [
            struct(whole, f32),
            struct(whole, f32),
            struct(whole, bf16),
            struct(whole, bf16),
            struct((2, tokens, HALF), bf16),
            struct((8, D), f32),
        ],
        [spec(whole)] * 4 + [spec((2, tokens, HALF)), spec((8, D))],
        1,
        "project_norm",
        2 * tokens * D * D,
        10 * MIB,
        after=after,
    )


def rows_of(refs, start):
    return jnp.concatenate([ref[0, 0, start : start + KIND] for ref in refs], axis=0)


def mlp_kernel(meta, second_ref, cot_ref, *refs):
    four, other = refs[:4], refs[4:8]
    out_in, back_in = refs[8:10] if len(refs) == 14 else (None, None)
    out_ref, back_ref, units_ref, pre = refs[-4:]
    tokens = second_ref.shape[0]
    up_m, up_o = rows_of(four, 0), rows_of(other, 0)
    down_m, down_o = rows_of(four, KIND), rows_of(other, KIND)
    pre[...] = dot(second_ref[:, :HALF], up_m, NT) + dot(second_ref[:, HALF:], up_o, NT)
    back = dot(cot_ref[:, :HALF], down_m, NT) + dot(cot_ref[:, HALF:], down_o, NT)
    rate = 0.7978845608
    tail = [
        jnp.sum(ref[0, 0, 2 * KIND : WIDE].astype(f32), axis=0, keepdims=True)[:, :KIND]
        for ref in four
    ]
    bias = jnp.concatenate(tail, axis=1)
    size = 32
    for start in range(0, tokens, size):
        some = slice(start, start + size)
        value = pre[some, :] + bias
        square = value * value
        bent = jnp.tanh(rate * value * (1.0 + 0.044715 * square))
        half = 0.5 * (1.0 + bent)
        units_ref[1, some, :] = (value * half).astype(bf16)
        slope = half + (0.5 * rate) * value * (1.0 - bent * bent) * (1.0 + 3 * 0.044715 * square)
        units_ref[0, some, :] = (back[some] * slope).astype(bf16)
    cots, units = units_ref[0], units_ref[1]
    for target, source, left, right_m, right_o in (
        (out_ref, out_in, units, down_m, down_o),
        (back_ref, back_in, cots, up_m, up_o),
    ):
        for some, right in ((slice(0, HALF), right_m), (slice(HALF, D), right_o)):
            part = dot(left, right, NN)
            target[:, some] = part if source is None else source[:, some] + part


def mlp_block(meta, second, cot, four, other, which, sums=(), after=()):
    tokens = second.shape[0]
    size = tokens // 2
    part = (1, 1, WIDE, HALF)
    parts = [spec(part, lambda i, meta, e=e: (e, which, 0, 0)) for e in range(4)]
    parts += [spec(part, lambda i, meta, e=e: (CROSS[e], which, 0, 0)) for e in range(4)]
    whole = spec((size, D), lambda i, meta: (i, 0))
    return call(
        mlp_kernel,
        meta,
        (second, cot, *[four] * 4, *[other] * 4, *sums),
        [whole, whole] + parts + [whole] * len(sums),
        [struct((tokens, D), f32), struct((tokens, D), f32), struct((2, tokens, D), bf16)],
        [whole, whole, spec((2, size, D), lambda i, meta: (0, i, 0))],
        2,
        "mlp_both_ways",
        8 * tokens * D * D,
        12 * MIB,
        scratch=[pltpu.VMEM((size, D), f32)],
        alias={10: 0, 11: 1} if sums else {},
        after=after,
    )


def mlp_grads_kernel(meta, *refs):
    count = (len(refs) - 4) // 3
    own, got = refs[:count], refs[count : 2 * count]
    second_ref, cot_ref, right_ref, keep_ref = refs[2 * count : 2 * count + 4]
    gives = refs[2 * count + 4 :]
    i = pl.program_id(0)

    def work(mine_ref, theirs_ref, give_ref):
        for number, right in ((0, second_ref), (1, cot_ref)):
            grad = dot(mine_ref[number], right[:, :HALF], TN)
            got = dot(theirs_ref[number], right_ref[number], TN)
            for e in range(4):
                block = grad[e * KIND : (e + 1) * KIND]
                block = block + got[CROSS[e] * KIND : (CROSS[e] + 1) * KIND]
                some = slice(number * KIND, (number + 1) * KIND)
                if e < 2:
                    keep_ref[e, 0, some] = block
                else:
                    give_ref[e - 2, some] = block.astype(bf16)
        total = jnp.sum(mine_ref[0].astype(f32), axis=0, keepdims=True)
        got = jnp.sum(theirs_ref[0].astype(f32), axis=0, keepdims=True)
        for e in range(4):
            line = total[:, e * KIND : (e + 1) * KIND]
            line = line + got[:, CROSS[e] * KIND : (CROSS[e] + 1) * KIND]
            line = jnp.broadcast_to(line, (16, KIND))
            line = jnp.concatenate([line, line], axis=1)
            if e < 2:
                keep_ref[e, 0, 2 * KIND : WIDE] = line
            else:
                give_ref[e - 2, 2 * KIND : WIDE] = line.astype(bf16)

    for number in range(count):

        @pl.when(i == number)
        def _(number=number):
            work(own[number], got[number], gives[number])


def mlp_grads(meta, own, got, second, cot, right, after=()):
    count = len(own)
    tokens = second.shape[0]
    part = (2, 1, WIDE, HALF)
    shape = (2, count, WIDE, HALF)
    block = spec(part, lambda i, meta: (0, i, 0, 0))
    return call(
        mlp_grads_kernel,
        meta,
        (*own, *got, second, cot, right),
        [spec(own[0].shape)] * (2 * count)
        + [spec((tokens, D)), spec((tokens, D)), spec(right.shape)],
        [struct(shape, f32)] + [struct((2, WIDE, HALF), bf16)] * count,
        [block] + [spec((2, WIDE, HALF))] * count,
        count,
        "mlp_grads",
        count * 4 * tokens * D * D,
        12 * MIB,
        after=after,
    )


def turn_kernel(
    meta,
    resid_ref,
    attn_ref,
    out_ref,
    back_ref,
    ua,
    ub,
    rows_ref,
    own,
    four,
    other,
    mixed_a,
    mixed_b,
    mixed_c,
    block_a,
    block_b,
    resid_cot_ref,
    mixed_cot_ref,
    keep_ref,
    give_ref,
    vec_ref,
    attn_cot_ref,
):
    mine, rest = mine_rest(meta)
    sums = [jnp.zeros((1, D), f32) for _ in range(4)]
    for part, (u_ref, block_ref) in enumerate(((ua, block_a), (ub, block_b))):
        size = u_ref.shape[0]
        for start in range(0, size, CHUNK):
            some = pl.ds(start, CHUNK)
            here = pl.ds(part * size + start, CHUNK)
            resid = resid_ref[here, :]
            mlp_out = out_ref[here, :] + row(rows_ref, DOWN_BIAS)
            result = (resid + row(rows_ref, GATE_MLP) * mlp_out).astype(bf16)
            block_ref[some, mine] = result[:, :HALF]
            block_ref[some, rest] = result[:, HALF:]
            up = jnp.concatenate([u_ref[some, mine], u_ref[some, rest]], axis=1).astype(f32)
            out_cot = loss_weight(meta, part, start, rows_ref) * up
            sums[3] = sums[3] + jnp.sum(mlp_out * out_cot, axis=0, keepdims=True)
            unit, rate = normalize(resid)
            cot = back_ref[here, :]
            sums[1] = sums[1] + jnp.sum(cot, axis=0, keepdims=True)
            sums[2] = sums[2] + jnp.sum(cot * unit, axis=0, keepdims=True)
            cot = cot * (1.0 + row(rows_ref, SCALE_MLP)) * row(rows_ref, GAIN_MLP)
            resid_cot = out_cot + normalize_back(cot, unit, rate)
            resid_cot_ref[here, :] = resid_cot
            sums[0] = sums[0] + jnp.sum(attn_ref[here, :] * resid_cot, axis=0, keepdims=True)
            attn_cot = (row(rows_ref, GATE_ATTN) * resid_cot).astype(bf16)
            attn_cot_ref[here, :] = attn_cot
    for i in range(4):
        vec_ref[i : i + 1, :] = sums[i]
    vec_ref[4:8, :] = jnp.zeros((4, D), f32)
    cot_m, cot_o = attn_cot_ref[:, :HALF], attn_cot_ref[:, HALF:]
    near = dot(own[:, mine], cot_m, NT) + dot(own[:, rest], cot_o, NT)
    mixed_cot_ref[:KIND, :] = near.astype(bf16)
    far = dot(four[0].reshape(3 * KIND, HALF), cot_m, NT)
    far = far + dot(other[0].reshape(3 * KIND, HALF), cot_o, NT)
    mixed_cot_ref[KIND:, :] = far.astype(bf16)
    mixed = jnp.concatenate([mixed_a[...], mixed_b[...], mixed_c[...]], axis=0)
    keep_ref[...] = dot(mixed, cot_m, NN).reshape(Z, KIND, HALF)
    give_ref[...] = dot(mixed, cot_o, NN).reshape(Z, KIND, HALF).astype(bf16)


def turn(meta, resid, attn, out, back, ua, ub, rows, own, four, other, mixed, after=()):
    tokens = resid.shape[0]
    whole = (tokens, D)
    return call(
        turn_kernel,
        meta,
        (resid, attn, out, back, ua, ub, rows, own, four, other, *mixed),
        [spec(whole)] * 4
        + [spec(ua.shape)] * 2
        + [spec(rows.shape), spec(own.shape)]
        + piece_specs(lambda i: 3)
        + [spec(one.shape) for one in mixed],
        [
            struct(ua.shape, bf16),
            struct(ub.shape, bf16),
            struct(whole, f32),
            struct((D, tokens), bf16),
            struct((Z, KIND, HALF), f32),
            struct((Z, KIND, HALF), bf16),
            struct((8, D), f32),
        ],
        [
            spec(ua.shape),
            spec(ub.shape),
            spec(whole),
            spec((D, tokens)),
            spec((Z, KIND, HALF)),
            spec((Z, KIND, HALF)),
            spec((8, D)),
        ],
        1,
        "norm_back",
        4 * tokens * D * D,
        12 * MIB,
        scratch=[pltpu.VMEM(whole, bf16)],
        after=after,
    )


def attn_grads_kernel(meta, *refs):
    parts = (len(refs) - 13) // 3
    own, give, got = [refs[parts * j : parts * (j + 1)] for j in range(3)]
    out_keep, out_got, first_ref, kv_got, cos_ref, sin_ref, cos_got, sin_got = refs[-13:-5]
    keep_ref, give_first, give_last, dkv_ref, left = refs[-5:]
    i = pl.program_id(0)
    e = lax.rem(i + 2, 4)
    kind = meta[9 + e]
    size_of = D // parts

    def write(grad):
        @pl.when(e < 2)
        def _():
            keep_ref[0] = grad

        @pl.when(e == 2)
        def _():
            give_first[...] = grad.astype(bf16)

        @pl.when(e == 3)
        def _():
            give_last[...] = grad.astype(bf16)

    def put(mine, theirs):
        grad = dot(mine, first_ref[:, :HALF], NN) + dot(theirs, kv_got[...], NT)
        write(grad.reshape(Z, KIND, HALF))

    @pl.when(kind == 3)
    def _():
        write(out_keep[...] + out_got[...].astype(f32))

    @pl.when(kind == 0)
    def _():
        put(
            jnp.concatenate([one[4] for one in give], axis=0),
            jnp.concatenate([one[4] for one in got], axis=0),
        )

    def together(number, side, low, size):
        group = low // size_of
        some = slice(low - group * size_of, low - group * size_of + size)
        theirs = got[group][2 * (1 - side) + number, some].astype(f32)
        return own[group][side, number, some] + theirs

    @pl.when(kind == 1)
    def _():
        for side, cosines, sines in ((0, cos_ref, sin_ref), (1, cos_got, sin_got)):
            cosine, sine = cosines[...], sines[...]
            for h in range(HEADS):
                start = h * HEAD
                low = together(0, side, start, HEAD // 2)
                high = together(0, side, start + HEAD // 2, HEAD // 2)
                left[side, start : start + HEAD // 2] = (low * cosine + high * sine).astype(bf16)
                left[side, start + HEAD // 2 : start + HEAD] = (
                    high * cosine - low * sine
                ).astype(bf16)
        dkv_ref[0] = left[0]
        put(left[0], left[1])

    @pl.when(kind == 2)
    def _():
        for side in range(2):
            for h in range(HEADS):
                start = h * HEAD
                left[side, start : start + HEAD] = together(1, side, start, HEAD).astype(bf16)
        dkv_ref[1] = left[0]
        put(left[0], left[1])


def attn_grads(meta, own, give, got, out_keep, out_got, first, kv_got, turns, turns_got, after=()):
    tokens = first.shape[0]
    full = (2, Z, KIND, HALF)
    args = (*own, *give, *got, out_keep, out_got, first, kv_got, *turns, *turns_got)
    specs = [spec(one.shape) for one in args]
    specs[3 * len(own) + 3] = spec((HALF, tokens), lambda i, meta: (2 * D // HALF, 0))
    shape = (1, Z, KIND, HALF)
    return call(
        attn_grads_kernel,
        meta,
        args,
        specs,
        [struct(full, f32)] + [struct(full[1:], bf16)] * 2 + [struct((2, D, tokens), bf16)],
        [
            spec(shape, lambda i, meta: (jnp.maximum(i - 2, 0), 0, 0, 0)),
            spec(full[1:]),
            spec(full[1:]),
            spec((2, D, tokens)),
        ],
        4,
        "attention_grads",
        3 * 2 * tokens * D * D,
        18 * MIB,
        scratch=[pltpu.VMEM((2, D, tokens), bf16)],
        after=after,
    )


def leave_kernel(
    meta,
    xa,
    xb,
    dq_ref,
    dq2_ref,
    dq3_ref,
    dkv_ref,
    resid_cot_ref,
    rows_ref,
    own,
    four0,
    four1,
    four2,
    other0,
    other1,
    other2,
    turn_ref,
    middle_ref,
    cond_ref,
    block_a,
    block_b,
    vec_ref,
    cot_ref,
):
    mine, rest = mine_rest(meta)
    near_q = dq_ref[0, :KIND, :]
    far_q = jnp.concatenate([dq_ref[0, KIND:, :], dq2_ref[0], dq3_ref[0]], axis=0)
    for half, cols, fars in (
        (slice(0, HALF), mine, (four0, four1, four2)),
        (slice(HALF, D), rest, (other0, other1, other2)),
    ):
        total = dot(near_q, own[0, :, cols], TN)
        total = total + dot(far_q, fars[0][0].reshape(3 * KIND, HALF), TN)
        for k in (1, 2):
            total = total + dot(dkv_ref[k - 1, :KIND, :], own[k, :, cols], TN)
            total = total + dot(dkv_ref[k - 1, KIND:, :], fars[k][0].reshape(3 * KIND, HALF), TN)
        cot_ref[:, half] = total
    sums = [jnp.zeros((1, D), f32) for _ in range(2)]
    for part, (x_ref, block_ref) in enumerate(((xa, block_a), (xb, block_b))):
        size = x_ref.shape[0]
        for start in range(0, size, CHUNK):
            some = pl.ds(start, CHUNK)
            here = pl.ds(part * size + start, CHUNK)
            x = jnp.concatenate([x_ref[some, mine], x_ref[some, rest]], axis=1).astype(f32)
            unit, rate = normalize(x)
            cot = cot_ref[here, :]
            sums[0] = sums[0] + jnp.sum(cot, axis=0, keepdims=True)
            sums[1] = sums[1] + jnp.sum(cot * unit, axis=0, keepdims=True)
            cot = cot * (1.0 + row(rows_ref, SCALE_ATTN)) * row(rows_ref, GAIN_ATTN)
            result = resid_cot_ref[here, :] + normalize_back(cot, unit, rate)
            result = result.astype(block_ref.dtype)
            block_ref[some, mine] = result[:, :HALF]
            block_ref[some, rest] = result[:, HALF:]
    nothing = jnp.zeros((1, D), f32)
    inner = row(turn_ref, 2)
    lines = [
        row(turn_ref, 0),
        row(turn_ref, 1),
        inner * row(rows_ref, GAIN_MLP),
        row(turn_ref, 3),
        jnp.where(meta[0] == 0, row(cond_ref, 0), nothing),
        sums[0],
        sums[1] * row(rows_ref, GAIN_ATTN),
        nothing,
        sums[1] * (1.0 + row(rows_ref, SCALE_ATTN)),
        inner * (1.0 + row(rows_ref, SCALE_MLP)),
        row(middle_ref, 0),
    ]
    for i in range(16):
        vec_ref[i : i + 1, :] = lines[i] if i < len(lines) else nothing


def leave(
    meta, xa, xb, dq, dkv, resid_cot, rows, own, four, other, turn_vec, middle_vec, cond, after=()
):
    tokens = 2 * xa.shape[0]
    return call(
        leave_kernel,
        meta,
        (
            xa,
            xb,
            *dq,
            dkv,
            resid_cot,
            rows,
            own,
            *[four] * 3,
            *[other] * 3,
            turn_vec,
            middle_vec,
            cond,
        ),
        [spec(xa.shape)] * 2
        + [spec((1, *dq[0].shape[1:]), lambda i, meta: (4, 0, 0))] * 3
        + [spec(dkv.shape), spec(resid_cot.shape), spec(rows.shape), spec(own.shape)]
        + [piece_specs(lambda i, k=k: k)[0] for k in range(3)]
        + [piece_specs(lambda i, k=k: k)[1] for k in range(3)]
        + [spec((8, D)), spec((8, D)), spec((1, D))],
        [struct(xa.shape, bf16)] * 2 + [struct((16, D), f32)],
        [spec(xa.shape)] * 2 + [spec((16, D))],
        1,
        "first_norm_back",
        6 * tokens * D * D,
        10 * MIB,
        scratch=[pltpu.VMEM((tokens, D), f32)],
        after=after,
    )


def place_attn_kernel(meta, four, other, qkv_ref, out_ref):
    mine, rest = mine_rest(meta)
    k = pl.program_id(0)

    @pl.when(k < 3)
    def _():
        qkv_ref[0, :, mine] = four[0].astype(f32)
        qkv_ref[0, :, rest] = other[0].astype(f32)

    @pl.when(k == 3)
    def _():
        out_ref[:, mine] = four[0].astype(f32)
        out_ref[:, rest] = other[0].astype(f32)


def place_attn(meta, four, other, after=()):
    return call(
        place_attn_kernel,
        meta,
        (four, other),
        [
            spec((1, KIND, HALF), lambda i, meta: (meta[1 + i], 0, 0)),
            spec((1, KIND, HALF), lambda i, meta: (meta[5 + i], 0, 0)),
        ],
        [struct((3, KIND, D), f32), struct((KIND, D), f32)],
        [
            spec((1, KIND, D), lambda i, meta: (jnp.minimum(i, 2), 0, 0)),
            spec((KIND, D)),
        ],
        4,
        "place_attention_grads",
        0,
        5 * MIB,
        after=after,
    )


def place_mlp_kernel(meta, four, other, up_ref, down_ref, bias_ref, turned):
    mine, rest = mine_rest(meta)
    k = pl.program_id(0)
    down_ref[:, mine] = four[0, KIND : 2 * KIND].astype(f32)
    down_ref[:, rest] = other[0, KIND : 2 * KIND].astype(f32)
    some = pl.ds(pl.multiple_of(k * KIND, KIND), KIND)
    turned[some, mine] = four[0, :KIND].astype(f32)
    turned[some, rest] = other[0, :KIND].astype(f32)
    bias_ref[0] = four[0, 2 * KIND : WIDE].astype(f32)

    @pl.when(k == 3)
    def _():
        up_ref[...] = turned[...].T


def place_mlp(meta, four, other, after=()):
    return call(
        place_mlp_kernel,
        meta,
        (four, other),
        [
            spec((1, WIDE, HALF), lambda i, meta: (meta[1 + i], 0, 0)),
            spec((1, WIDE, HALF), lambda i, meta: (meta[5 + i], 0, 0)),
        ],
        [struct((D, D), f32), struct((D, D), f32), struct((4, 16, HALF), f32)],
        [
            spec((D, D)),
            spec((KIND, D), lambda i, meta: (i, 0)),
            spec((1, 16, HALF), lambda i, meta: (i, 0, 0)),
        ],
        4,
        "place_mlp_grads",
        0,
        10 * MIB,
        after=after,
        scratch=[pltpu.VMEM((D, D), f32)],
    )


def merge_rows(table, got, here):
    each, got_each = table[:-8], got[:-8]
    return jnp.concatenate(
        [
            jnp.where(here == 0, each, got_each),
            jnp.where(here == 0, got_each, each),
            table[-8:] + got[-8:],
        ]
    )


def last_kernel(
    meta, mine_ref, rest_ref, modulator_ref, mod_ref, bias_ref, cond_ref, sum_ref, whole, cots
):
    mine, rest = mine_rest(meta)
    whole[:, mine] = mine_ref[...]
    whole[:, rest] = rest_ref[...]
    slots = cots.shape[1]
    sum_ref[...] = whole[8 * slots : 8 * slots + 8, :]
    for slot in range(slots):
        some = slice(slot, slot + 1)
        for j, line in enumerate((5, 6, 0, 1, 2, 3, 4)):
            cots[j, some, :] = whole[8 * slot + line : 8 * slot + line + 1, :]
    condition = cots[6, :, 0:128]
    total = jnp.zeros((2, 128), f32)
    for j in range(6):
        cot = cots[j]
        some = slice(j * D, (j + 1) * D)
        mod_ref[:, some] = lax.dot_general(
            condition, cot, (TN, ((), ())), precision=highest, preferred_element_type=f32
        )
        bias_ref[:, some] = jnp.sum(cot, axis=0, keepdims=True)
        pair = jnp.concatenate([cots[j, pl.ds(meta[32 + s], 1), :] for s in range(2)], axis=0)
        total = total + lax.dot_general(
            pair,
            modulator_ref[:, some].astype(f32),
            (NT, ((), ())),
            precision=highest,
            preferred_element_type=f32,
        )
    cond_ref[...] = total


def last(meta, mine, rest, modulator, slots, after=()):
    args = (mine, rest, modulator)
    return call(
        last_kernel,
        meta,
        args,
        [spec(one.shape) for one in args],
        [
            struct((128, 6 * D), f32),
            struct((1, 6 * D), f32),
            struct((2, 128), f32),
            struct((8, D), f32),
        ],
        [spec((128, 6 * D)), spec((1, 6 * D)), spec((2, 128)), spec((8, D))],
        1,
        "modulation_grads",
        0,
        5 * MIB,
        scratch=[pltpu.VMEM((8 * slots + 8, D), f32), pltpu.VMEM((7, slots, D), f32)],
        after=after,
    )


def shards(
    activations,
    condition,
    modulator,
    mod_bias,
    gain_attn,
    gain_mlp,
    query_key_value_matrix,
    output_matrix,
    up_matrix,
    up_offset_bias,
    down_matrix,
    down_bias,
    upstream,
    span_start,
    span_length,
    noise_level,
):
    dp_size = lax.axis_size("dp")
    d = lax.axis_index("dp")
    z = lax.axis_index("tensor")
    rows = activations.shape[1]
    tokens = 2 * rows
    meta = lax.dynamic_slice(meta_table(rows), (d % 8, z, 0), (1, 1, 32)).reshape(32)
    core = meta[0]
    odd = z % 2

    def swap(values):
        return jnp.where(core == 0, values, jnp.roll(values, HALF, axis=-1))

    flow = Flow(dp_size)

    qkv_block = jnp.transpose(query_key_value_matrix, (1, 2, 0))
    kind = meta[9]
    piece = jnp.where(
        kind < 3,
        lax.dynamic_slice(
            qkv_block, (jnp.minimum(kind, 2), 0, core * HALF), (1, KIND, HALF)
        ).reshape(KIND, HALF),
        lax.dynamic_slice(output_matrix, (0, core * HALF), (KIND, HALF)),
    )
    got = [flow.send(piece, to_back(r)) for r in range(1, Z)]
    xa = flow.send(pick(activations, odd), chip_a)
    xb = flow.send(pick(activations, 1 - odd), chip_b)
    flow.fence()

    apart = jnp.stack([one.a for one in got])
    near = flow.send(apart, to_second)
    facts = jnp.concatenate(
        [
            condition,
            span_start.astype(f32)[:, None],
            span_length.astype(f32)[:, None],
            noise_level.astype(f32)[:, None],
            jnp.zeros((2, 125), f32),
        ],
        axis=1,
    )
    facts_other = flow.send(facts, to_core)
    own_mine, own_rest = flow.run(prepare, meta, up_matrix, down_matrix, up_offset_bias)
    flow.fence()

    pair = jnp.stack([apart, near.a])
    far = flow.send(pair, to_first)
    facts = jnp.where(core == z // 2, pick(facts, odd), pick(facts_other.a, odd))
    cond_row = facts[None, :128]
    start, length, level = facts[128], facts[129], facts[130]
    sigma = noise_low + (noise_high - noise_low) * (level + 0.5) / LEVELS
    factor = 1.0 / (1.0 - jnp.exp(-sigma))
    modulation = jnp.dot(cond_row, modulator.astype(f32), precision=highest) + mod_bias
    modulation = modulation.reshape(6, D)
    table = jnp.concatenate(
        [
            modulation,
            gain_attn[None],
            gain_mlp[None],
            down_bias[None],
            jnp.broadcast_to(start, (1, D)),
            jnp.broadcast_to(start + length, (1, D)),
            jnp.broadcast_to(factor, (1, D)),
            jnp.zeros((4, D), f32),
        ]
    )
    table = flow.keep(swap(table))
    step = jnp.arange(rows, dtype=f32)
    angular_rate = 10000.0 ** (-2.0 * jnp.arange(HEAD // 2, dtype=f32) / HEAD)

    def turns_of(core_here):
        places = jnp.concatenate(
            [
                ((2 * core_here + odd) * rows).astype(f32) + step,
                ((2 * core_here + 1 - odd) * rows).astype(f32) + step,
            ]
        )
        angles = angular_rate[:, None] * places[None, :]
        return flow.keep(jnp.cos(angles)), flow.keep(jnp.sin(angles))

    (cosine, sine), (cosine_got, sine_got) = turns_of(core), turns_of(1 - core)
    flow.fence()

    attn_four = jnp.concatenate([pair, far.a])
    attn_other = flow.send(attn_four, to_core)
    flow.fence()
    attn_other, table = attn_other.a, table.a
    turns, turns_got = (cosine.a, sine.a), (cosine_got.a, sine_got.a)
    xa, xb = xa.a, xb.a

    mlp_piece = own_mine.a[0]
    got_1 = flow.send(mlp_piece, to_back(1))
    first, q, kv = flow.run(
        enter, meta, xa, xb, table, *turns, qkv_block, attn_four, attn_other
    )
    flow.fence()
    kv_got = flow.send(kv.a, to_core)
    near_1 = flow.send(got_1.a, to_second)
    flow.fence()
    third = HEADS // 3
    settings = (q.a, kv.a, kv_got.a)
    ua = flow.send(pick(upstream, odd), chip_a)
    pair_1 = jnp.stack([got_1.a, near_1.a])
    far_1 = flow.send(pair_1, to_first)
    mixed_a, lse_a = flow.run(attend_forward, meta, 0, third, *settings)
    flow.fence()
    ub = flow.send(pick(upstream, 1 - odd), chip_b)
    four_1 = jnp.concatenate([pair_1, far_1.a])[:, None]
    other_1 = flow.send(four_1, to_core)
    mixed_b, lse_b = flow.run(attend_forward, meta, third, third, *settings)
    flow.fence()
    got_2 = flow.send(mlp_piece, to_back(2))
    mixed_c, lse_c = flow.run(attend_forward, meta, 2 * third, third, *settings)
    flow.fence()
    mixed = (mixed_a.a, mixed_b.a, mixed_c.a)
    near_2 = flow.send(got_2.a, to_second)
    attn, resid, second, cot, right, middle_vec = flow.run(
        middle, meta, mixed, output_matrix, attn_four, attn_other, xa, xb, ua.a, ub.a, table
    )
    flow.fence()

    settings = (meta, second.a, cot.a)
    right_got = flow.send(right.a, to_core)
    got_3 = flow.send(mlp_piece, to_back(3))
    pair_2 = jnp.stack([got_2.a, near_2.a])
    far_2 = flow.send(pair_2, to_first)
    out, back, act_0 = flow.run(
        mlp_block, *settings, own_mine.a[:, None], own_rest.a[:, None], 0
    )
    flow.fence()
    act_0_got = flow.send(act_0.a, to_core)
    four_2 = jnp.concatenate([pair_2, far_2.a])[:, None]
    other_2 = flow.send(four_2, to_core)
    near_3 = flow.send(got_3.a, to_second)
    out, back, act_1 = flow.run(mlp_block, *settings, four_1, other_1.a, 0, (out.a, back.a))
    flow.fence()
    act_1_got = flow.send(act_1.a, to_core)
    pair_3 = jnp.stack([got_3.a, near_3.a])
    far_3 = flow.send(pair_3, to_first)
    out, back, act_2 = flow.run(mlp_block, *settings, four_2, other_2.a, 0, (out.a, back.a))
    flow.fence()
    act_2_got = flow.send(act_2.a, to_core)
    four_3 = jnp.concatenate([pair_3, far_3.a])[:, None]
    other_3 = flow.send(four_3, to_core)
    keep_1, give_0, give_1 = flow.run(
        mlp_grads,
        meta,
        (act_0.a, act_1.a),
        (act_0_got.a, act_1_got.a),
        second.a,
        cot.a,
        right_got.a,
    )
    flow.fence()
    first_0 = flow.send(give_0.a, to_first)
    out, back, act_3 = flow.run(mlp_block, *settings, four_3, other_3.a, 0, (out.a, back.a))
    flow.fence()
    act_3_got = flow.send(act_3.a, to_core)
    first_1 = flow.send(give_1.a, to_first)
    block_a, block_b, resid_cot, mixed_cot, out_keep, out_give, turn_vec = flow.run(
        turn,
        meta,
        resid.a,
        attn.a,
        out.a,
        back.a,
        ua.a,
        ub.a,
        table,
        output_matrix,
        attn_four,
        attn_other,
        mixed,
    )
    flow.fence()
    out_got = flow.send(out_give.a, to_core)
    firsts = jnp.stack([first_0.a, first_1.a], axis=1).astype(f32)
    second_1 = flow.send((keep_1.a[1] + firsts[1]).astype(bf16), to_second)
    blocks_1 = keep_1.a[0] + firsts[0]
    keep_2, give_2, give_3 = flow.run(
        mlp_grads,
        meta,
        (act_2.a, act_3.a),
        (act_2_got.a, act_3_got.a),
        second.a,
        cot.a,
        right_got.a,
    )
    flow.fence()

    settings = (q.a, kv.a, kv_got.a, mixed_cot.a)
    blocks_1 = blocks_1 + second_1.a.astype(f32)
    plane_1 = flow.send(blocks_1[1].astype(bf16), to_ahead(1))
    first_2 = flow.send(give_2.a, to_first)
    own_a, give_a = flow.run(attend_backward, meta, 0, third, *settings, lse_a.a, *turns)
    flow.fence()
    got_a = flow.send(give_a.a, to_core)
    first_3 = flow.send(give_3.a, to_first)
    back_a = flow.send(block_a.a, inverse(chip_a, dp_size))
    own_b, give_b = flow.run(attend_backward, meta, third, third, *settings, lse_b.a, *turns)
    flow.fence()
    got_b = flow.send(give_b.a, to_core)
    firsts = jnp.stack([first_2.a, first_3.a], axis=1).astype(f32)
    second_2 = flow.send((keep_2.a[1] + firsts[1]).astype(bf16), to_second)
    blocks_2 = keep_2.a[0] + firsts[0]
    back_b = flow.send(block_b.a, inverse(chip_b, dp_size))
    own_c, give_c = flow.run(attend_backward, meta, 2 * third, third, *settings, lse_c.a, *turns)
    flow.fence()
    got_c = flow.send(give_c.a, to_core)
    blocks_2 = blocks_2 + second_2.a.astype(f32)
    plane_3 = flow.send(blocks_2[1].astype(bf16), to_ahead(3))
    flow.fence()
    block_out = jnp.where(
        odd == 0, jnp.stack([back_a.a, back_b.a]), jnp.stack([back_b.a, back_a.a])
    )
    plane_2 = flow.send(blocks_2[0].astype(bf16), to_ahead(2))
    keep, give_e, give_f, dkv = flow.run(
        attn_grads,
        meta,
        (own_a.a, own_b.a, own_c.a),
        (give_a.a, give_b.a, give_c.a),
        (got_a.a, got_b.a, got_c.a),
        out_keep.a,
        out_got.a,
        first.a,
        kv_got.a,
        turns,
        turns_got,
    )
    flow.fence()

    def across(total):
        bit = 8
        while bit < dp_size:
            total = total + send(total, to_flip(bit), dp_size)
            bit *= 2
        return total.astype(bf16)

    first_e = flow.send(give_e.a, to_first)
    mlp_total = blocks_1[0] + plane_1.a.astype(f32) + plane_2.a.astype(f32)
    mlp_total = across(mlp_total + plane_3.a.astype(f32))
    slope_a, slope_b, late = flow.run(
        leave,
        meta,
        xa,
        xb,
        (give_a.a, give_b.a, give_c.a),
        dkv.a,
        resid_cot.a,
        table,
        qkv_block,
        attn_four,
        attn_other,
        turn_vec.a,
        middle_vec.a,
        jnp.concatenate([cond_row, jnp.zeros((1, D - 128), f32)], axis=1),
    )
    flow.fence()

    first_f = flow.send(give_f.a, to_first)
    slope_a = flow.send(slope_a.a, inverse(chip_a, dp_size))
    vectors = flow.send(late.a[:, HALF:], to_core)
    flow.fence()
    vectors = late.a[:, :HALF] + vectors.a
    bits = []
    bit = 2
    while bit < dp_size:
        bits.append((to_flip(bit), (d // bit) % 2))
        bit *= 2
    bits += [(to_flip_z(1), z % 2), (to_flip_z(2), z // 2)]

    def spread(vectors):
        target, here = bits.pop(0)
        return flow.send(vectors, target), here

    got, here = spread(vectors)
    got_second = flow.send((keep.a[1] + first_f.a.astype(f32)).astype(bf16), to_second)
    blocks = keep.a[0] + first_e.a.astype(f32)
    mlp_near = flow.send(mlp_total, to_second)
    slope_b = flow.send(slope_b.a, inverse(chip_b, dp_size))
    flow.fence()
    vectors = merge_rows(vectors, got.a, here)
    got, here = spread(vectors)
    blocks = blocks + got_second.a.astype(f32)
    planes = [flow.send(blocks[r].astype(bf16), to_ahead(r)) for r in range(1, Z)]
    mlp_pair = jnp.stack([mlp_total, mlp_near.a])
    mlp_far = flow.send(mlp_pair, to_first)
    flow.fence()
    vectors = merge_rows(vectors, got.a, here)
    got, here = spread(vectors)
    attn_total = blocks[0]
    for one in planes:
        attn_total = attn_total + one.a.astype(f32)
    attn_total = across(attn_total)
    attn_near = flow.send(attn_total, to_second)
    mlp_four = jnp.concatenate([mlp_pair, mlp_far.a])
    mlp_other = flow.send(mlp_four, to_core)
    slopes = (slope_a.a, slope_b.a)
    entering_state_slope = flow.keep(
        jnp.where(odd == 0, jnp.stack(slopes), jnp.stack(slopes[::-1])).astype(f32)
    )
    flow.fence()
    vectors = merge_rows(vectors, got.a, here)
    while len(bits) > 1:
        got, here = spread(vectors)
        flow.fence()
        vectors = merge_rows(vectors, got.a, here)
    got, here = spread(vectors)
    attn_pair = jnp.stack([attn_total, attn_near.a])
    attn_far = flow.send(attn_pair, to_first)
    up_grad, down_grad, units = flow.run(place_mlp, meta, mlp_four, mlp_other.a)
    flow.fence()
    vectors = merge_rows(vectors, got.a, here)
    vectors_other = flow.send(vectors, to_core)
    attn_four = jnp.concatenate([attn_pair, attn_far.a])
    attn_other = flow.send(attn_four, to_core)
    flow.fence()
    own_slots = jnp.stack([(2 * core + s) * (dp_size // 2) + d // 2 for s in range(2)])
    modulator_grad, modbias_grad, condition_grad, sums = last(
        jnp.concatenate([meta, own_slots.astype(jnp.int32)]),
        vectors,
        vectors_other.a,
        modulator,
        Z * (dp_size // 2),
    )
    qkv_grad, out_grad = place_attn(meta, attn_four, attn_other.a)
    qkv_grad = jnp.transpose(qkv_grad, (2, 0, 1))
    upbias_grad = units.a[:, 0, :KIND].reshape(-1)
    return (
        block_out,
        entering_state_slope.a,
        condition_grad,
        modulator_grad,
        modbias_grad.reshape(-1),
        sums[0],
        sums[1],
        qkv_grad,
        out_grad,
        up_grad.a,
        upbias_grad,
        down_grad.a,
        sums[2],
    )


def solution(mesh):
    in_specs = (
        P("dp", "tensor", None),
        P("dp", None),
        P(),
        P(),
        P(),
        P(),
        P(None, None, "tensor"),
        P("tensor", None),
        P(None, "tensor"),
        P("tensor"),
        P("tensor", None),
        P(),
        P("dp", "tensor", None),
        P("dp"),
        P("dp"),
        P("dp"),
    )
    out_specs = (
        P("dp", "tensor", None),
        P("dp", "tensor", None),
        P("dp", None),
        P(),
        P(),
        P(),
        P(),
        P(None, None, "tensor"),
        P("tensor", None),
        P(None, "tensor"),
        P("tensor"),
        P("tensor", None),
        P(),
    )
    return jax.shard_map(shards, mesh=mesh, in_specs=in_specs, out_specs=out_specs, check_vma=False)
```

```python
import functools

import jax
import jax.numpy as jnp
import numpy as np
from jax import lax
from jax.experimental import pallas as pl
from jax.experimental.pallas import tpu as pltpu
from jax.sharding import PartitionSpec as P

D = 768
HALF = 384
HEAD = 64
HEADS = 12
L = 1024
LEVELS = 1024
Z = 4
KIND = 192
WIDE = 400

noise_low = 0.1
noise_high = 3.0
epsilon = 1e-05
highest = lax.Precision.HIGHEST
f32 = jnp.float32
bf16 = jnp.bfloat16
MIB = 1 << 20

NN = ((1,), (0,))
NT = ((1,), (1,))
TN = ((0,), (0,))
SCALE = HEAD ** (-0.5)
CROSS = (0, 2, 1, 3)


def dot(a, b, contract):
    return lax.dot_general(a, b, (contract, ((), ())), preferred_element_type=f32)


def struct(shape, dtype):
    return jax.ShapeDtypeStruct(shape, dtype)


def send(values, target, dp_size):
    pairs = []
    for d in range(dp_size):
        for t in range(Z):
            to_d, to_t = target(d, t)
            pairs.append((d * Z + t, to_d * Z + to_t))
    return lax.ppermute(values, ("dp", "tensor"), pairs)


def to_core(d, t):
    return (d ^ 1, t)


def to_first(d, t):
    return (d ^ (4 if d & 1 else 2), t)


def to_second(d, t):
    return (d ^ (2 if d & 1 else 4), t)


def to_back(shift):
    return lambda d, t: (d, (t - shift) % Z)


def to_ahead(shift):
    return lambda d, t: (d, (t + shift) % Z)


def to_flip(bit):
    return lambda d, t: (d ^ bit, t)


def to_flip_z(bit):
    return lambda d, t: (d, t ^ bit)


def chip_a(d, t):
    return (2 * (d // 2) + t // 2, 2 * (d % 2) + t % 2)


def chip_b(d, t):
    return (2 * (d // 2) + t // 2, 2 * (d % 2) + 1 - t % 2)


def inverse(target, dp_size):
    table = {target(d, t): (d, t) for d in range(dp_size) for t in range(Z)}
    return lambda d, t: table[(d, t)]


def pick(values, index, axis=0):
    return lax.dynamic_index_in_dim(values, index, axis, keepdims=False)


def meta_table(rows):
    table = np.zeros((8, Z, 32), np.int32)
    for d in range(8):
        core, x, y = d & 1, (d >> 1) & 1, (d >> 2) & 1
        kind = 2 * x + y
        second, first = (1, 2) if core == 0 else (2, 1)
        listed = [kind, kind ^ second, kind ^ first, kind ^ 3]
        for z in range(Z):
            table[d, z, 0] = core
            for e, k in enumerate(listed):
                table[d, z, 1 + k] = e
                table[d, z, 5 + k] = CROSS[e]
                table[d, z, 9 + e] = k
            for r in range(1, Z):
                table[d, z, 15 + r] = (z + r) % Z
            for e, k in enumerate(listed):
                chip = 4 * (k & 1) + 2 * (k >> 1)
                table[d, z, 20 + e] = chip + core
                table[d, z, 24 + e] = chip + 1 - core
            table[d, z, 13] = (2 * core + z % 2) * rows
            table[d, z, 14] = (2 * core + 1 - z % 2) * rows
    return jnp.asarray(table)


def mine_rest(meta):
    core = meta[0]
    return (
        pl.ds(pl.multiple_of(core * HALF, 128), HALF),
        pl.ds(pl.multiple_of((1 - core) * HALF, 128), HALF),
    )


def normalize(values):
    average = jnp.mean(values, axis=-1, keepdims=True)
    centred = values - average
    spread = jnp.mean(centred * centred, axis=-1, keepdims=True)
    rate = lax.rsqrt(spread + epsilon)
    return centred * rate, rate


def normalize_back(cot, unit, rate):
    return rate * (
        cot
        - jnp.mean(cot, axis=-1, keepdims=True)
        - unit * jnp.mean(cot * unit, axis=-1, keepdims=True)
    )


CHUNK = 64


def chunks(count, size, work, totals=(), together=2):
    step = size * together

    def body(i, totals):
        for number in range(together):
            totals = work(pl.multiple_of(i * step, step) + number * size, totals)
        return totals

    if count == step:
        return body(0, totals)
    return lax.fori_loop(0, count // step, body, totals)


(
    SHIFT_ATTN,
    SCALE_ATTN,
    GATE_ATTN,
    SHIFT_MLP,
    SCALE_MLP,
    GATE_MLP,
    GAIN_ATTN,
    GAIN_MLP,
    DOWN_BIAS,
    START,
    END,
    FACTOR,
) = range(12)


def row(ref, number):
    return ref[number : number + 1, :]


def loss_weight(meta, part, start, rows_ref):
    place = lax.broadcasted_iota(jnp.int32, (CHUNK, 1), 0) + (meta[13 + part] + start)
    place = place.astype(f32)
    inside = (place >= rows_ref[START : START + 1, 0:1]) & (place < rows_ref[END : END + 1, 0:1])
    return jnp.where(inside, rows_ref[FACTOR : FACTOR + 1, 0:1], 0.0)


def spec(shape, index=None):
    if index is None:
        index = lambda i, meta: (0,) * len(shape)
    return pl.BlockSpec(shape, index)


VMEM = {"attention_grads": 44}


def call(kernel, meta, args, in_specs, out_shape, out_specs, grid, name, flops, moved, **more):
    scratch = more.pop("scratch", ())
    into = more.pop("into", ())
    after = list(into) + [one for one in more.pop("after", ()) if one is not None]
    count, extra = len(args), len(after)
    more = {1 + i: o for i, o in more.pop("alias", {}).items()}

    def body(meta_ref, *refs):
        kernel(meta_ref, *refs[:count], *refs[count + extra :])

    return pl.pallas_call(
        body,
        grid_spec=pltpu.PrefetchScalarGridSpec(
            num_scalar_prefetch=1,
            grid=(grid,),
            in_specs=list(in_specs) + [pl.BlockSpec(memory_space=pl.ANY)] * extra,
            out_specs=out_specs,
            scratch_shapes=list(scratch),
        ),
        out_shape=out_shape,
        compiler_params=pltpu.CompilerParams(vmem_limit_bytes=VMEM.get(name, 26) * MIB),
        cost_estimate=pl.CostEstimate(
            flops=int(flops), transcendentals=0, bytes_accessed=int(moved)
        ),
        name=name,
        input_output_aliases={1 + count + i: i for i in range(len(into))} | more,
    )(meta, *args, *after)


class Box:
    def __init__(self, array):
        self.a = array


class Flow:
    def __init__(self, dp_size):
        self.dp_size, self.open, self.token = dp_size, [], None

    def keep(self, array):
        box = Box(array)
        self.open.append(box)
        return box

    def tied(self, array):
        if self.token is None:
            return array
        return lax.optimization_barrier((array, self.token))[0]

    def send(self, array, target):
        return self.keep(send(self.tied(array), target, self.dp_size))

    def run(self, function, *args, **more):
        after = () if self.token is None else (self.token,)
        return [self.keep(one) for one in function(*args, after=after, **more)]

    def then(self, box):
        self.token = lax.optimization_barrier((self.token, box.a))[0]

    def fence(self):
        arrays = lax.optimization_barrier(tuple(box.a for box in self.open))
        for box, array in zip(self.open, arrays):
            box.a = array
        self.token = min(arrays, key=lambda one: one.size)
        self.open = []


def prepare_kernel(meta, up_ref, down_ref, bias_ref, mine_ref, rest_ref, turned):
    mine, rest = mine_rest(meta)
    turned[...] = up_ref[...].astype(f32).T.astype(bf16)
    for e in range(4):
        kind = meta[9 + e]
        rows = pl.ds(pl.multiple_of(kind * KIND, KIND), KIND)
        for half, out, place in ((mine, mine_ref, e), (rest, rest_ref, CROSS[e])):
            out[place, 0:KIND] = turned[rows, half]
            out[place, KIND : 2 * KIND] = down_ref[rows, half]
            tail = bias_ref[kind]
            high = tail.astype(bf16)
            left = tail - high.astype(f32)
            middle = left.astype(bf16)
            low = (left - middle.astype(f32)).astype(bf16)
            number = lax.broadcasted_iota(jnp.int32, (16, HALF), 0)
            block = jnp.where(
                number == 0,
                high.astype(f32),
                jnp.where(
                    number == 1,
                    middle.astype(f32),
                    jnp.where(number == 2, low.astype(f32), 0.0),
                ),
            )
            out[place, 2 * KIND : WIDE] = block.astype(bf16)


def prepare(meta, up_matrix, down_matrix, up_bias, after=()):
    padded = jnp.pad(up_bias.reshape(4, 1, KIND), ((0, 0), (0, 0), (0, HALF - KIND)))
    out = (4, WIDE, HALF)
    return call(
        prepare_kernel,
        meta,
        (up_matrix, down_matrix, padded),
        [spec((D, D)), spec((D, D)), spec((4, 1, HALF))],
        [struct(out, bf16)] * 2,
        [spec(out)] * 2,
        1,
        "prepare_weights",
        0,
        5 * MIB,
        scratch=[pltpu.VMEM((D, D), bf16)],
        after=after,
    )


def enter_kernel(
    meta,
    xa,
    xb,
    rows_ref,
    cos_ref,
    sin_ref,
    own,
    pair,
    far_pair,
    other_pair,
    other_far,
    first_ref,
    q_ref,
    kv_ref,
):
    k = pl.program_id(0)
    mine, rest = mine_rest(meta)

    @pl.when(k == 0)
    def _():
        for part, ref in enumerate((xa, xb)):
            size = ref.shape[0]

            def work(start, totals, part=part, ref=ref, size=size):
                some = pl.ds(start, CHUNK)
                x = jnp.concatenate([ref[some, mine], ref[some, rest]], axis=1).astype(f32)
                unit, _ = normalize(x)
                value = unit * row(rows_ref, GAIN_ATTN) * (1.0 + row(rows_ref, SCALE_ATTN))
                value = value + row(rows_ref, SHIFT_ATTN)
                first_ref[pl.ds(part * size + start, CHUNK), :] = value.astype(bf16)
                return totals

            chunks(size, CHUNK, work)

        kv_ref[2 * D :, :] = first_ref[:, HALF:].T

    first_m, first_o = first_ref[:, :HALF], first_ref[:, HALF:]
    near = dot(own[0, :, mine], first_m, NT) + dot(own[0, :, rest], first_o, NT)
    four = jnp.where(meta[1 + k] < 2, pair[0], far_pair[0])
    other = jnp.where(meta[5 + k] < 2, other_pair[0], other_far[0])
    far = dot(four.reshape(3 * KIND, HALF), first_m, NT)
    far = far + dot(other.reshape(3 * KIND, HALF), first_o, NT)

    def head(h):
        return near[h * HEAD : (h + 1) * HEAD] if h < 3 else far[(h - 3) * HEAD : (h - 2) * HEAD]

    def put(write, turn):
        for h in range(HEADS):
            block = head(h)
            if turn:
                low, high = block[: HEAD // 2], block[HEAD // 2 :]
                cosine, sine = cos_ref[...], sin_ref[...]
                write(h * HEAD, (low * cosine - high * sine).astype(bf16))
                write(h * HEAD + HEAD // 2, (high * cosine + low * sine).astype(bf16))
            else:
                write(h * HEAD, block.astype(bf16))

    def write_q(start, block):
        q_ref[pl.ds(start, block.shape[0]), :] = block

    def write_k(start, block):
        kv_ref[pl.ds(start, block.shape[0]), :] = block

    def write_v(start, block):
        kv_ref[pl.ds(D + start, block.shape[0]), :] = block

    @pl.when(k == 0)
    def _():
        put(write_q, True)

    @pl.when(k == 1)
    def _():
        put(write_k, True)

    @pl.when(k == 2)
    def _():
        put(write_v, False)


def piece_specs(kind_of):
    return [
        spec((1, 3, KIND, HALF), lambda i, meta: (meta[1 + kind_of(i)], 0, 0, 0)),
        spec((1, 3, KIND, HALF), lambda i, meta: (meta[5 + kind_of(i)], 0, 0, 0)),
    ]


def enter(meta, xa, xb, rows, cosine, sine, own, pair, far, other_pair, other_far, after=()):
    tokens = 2 * xa.shape[0]
    part = (1, 3, KIND, HALF)

    def near(first):
        return spec(part, lambda i, meta: (jnp.minimum(meta[first + i], 1), 0, 0, 0))

    def away(first):
        return spec(part, lambda i, meta: (jnp.maximum(meta[first + i] - 2, 0), 0, 0, 0))

    return call(
        enter_kernel,
        meta,
        (xa, xb, rows, cosine, sine, own, pair, far, other_pair, other_far),
        [
            spec(xa.shape),
            spec(xb.shape),
            spec(rows.shape),
            spec(cosine.shape),
            spec(sine.shape),
            spec((1, KIND, D), lambda i, meta: (i, 0, 0)),
            near(1),
            away(1),
            near(5),
            away(5),
        ],
        [
            struct((tokens, D), bf16),
            struct((D, tokens), bf16),
            struct((2 * D + HALF, tokens), bf16),
        ],
        [
            spec((tokens, D)),
            spec((D, tokens)),
            spec((2 * D + HALF, tokens)),
        ],
        3,
        "norm_project",
        2 * 3 * tokens * D * D,
        8 * MIB,
        after=after,
    )


def attend_kernel(meta, q_ref, k_ref, v_ref, ko_ref, vo_ref, o_ref, lse_ref):
    tokens = q_ref.shape[1]
    width = min(256, tokens)
    for start in range(0, tokens, width):
        some = pl.ds(start, width)
        q = q_ref[:, some] * bf16(SCALE)
        near = dot(k_ref[...], q, TN)
        far = dot(ko_ref[...], q, TN)
        top = jnp.maximum(
            jnp.max(near, axis=0, keepdims=True), jnp.max(far, axis=0, keepdims=True)
        )
        near = jnp.exp(near - top)
        far = jnp.exp(far - top)
        total = jnp.sum(near, axis=0, keepdims=True) + jnp.sum(far, axis=0, keepdims=True)
        share = 1.0 / total
        mixed = dot(v_ref[...], (near * share).astype(bf16), NN)
        mixed = mixed + dot(vo_ref[...], (far * share).astype(bf16), NN)
        o_ref[:, some] = mixed.astype(bf16)
        lse_ref[0, :, some] = top + jnp.log(total)


def attend_forward(meta, base, count, q, kv, kv_other, after=()):
    tokens = q.shape[1]
    own = spec((HEAD, tokens), lambda i, meta: (base + i, 0))
    first = own
    second = spec((HEAD, tokens), lambda i, meta: (HEADS + base + i, 0))
    return call(
        attend_kernel,
        meta,
        (q, kv, kv, kv_other, kv_other),
        [own, first, second, first, second],
        [struct((count * HEAD, tokens), bf16), struct((count, 1, tokens), f32)],
        [
            spec((HEAD, tokens), lambda i, meta: (i, 0)),
            spec((1, 1, tokens), lambda i, meta: (i, 0, 0)),
        ],
        count,
        "attend_forward",
        16 * 2 * 2 * tokens * tokens * D * count // HEADS,
        5 * MIB * count // HEADS,
        after=after,
    )


def attend_back_kernel(
    meta,
    q_ref,
    k_ref,
    v_ref,
    ko_ref,
    vo_ref,
    c_ref,
    lse_ref,
    cos_ref,
    sin_ref,
    give_ref,
    own_ref,
):
    tokens = q_ref.shape[1]
    width = min(256, tokens)
    for start in range(0, tokens, width):
        some = pl.ds(start, width)
        q = q_ref[:, some] * bf16(SCALE)
        c = c_ref[:, some]
        lse = lse_ref[0, :, some]
        sides = ((k_ref[...], v_ref[...]), (ko_ref[...], vo_ref[...]))
        probs = [jnp.exp(dot(k, q, TN) - lse) for k, _ in sides]
        cots = [dot(v, c, TN) for _, v in sides]
        inner = jnp.sum(probs[0] * cots[0], axis=0, keepdims=True)
        inner = inner + jnp.sum(probs[1] * cots[1], axis=0, keepdims=True)
        dq = None
        for number, (k, _) in enumerate(sides):
            score_cot = (probs[number] * (cots[number] - inner)).astype(bf16)
            dk = dot(q, score_cot, NT)
            dv = dot(c, probs[number].astype(bf16), NT)
            if start == 0:
                own_ref[number, 0] = dk
                own_ref[number, 1] = dv
            else:
                own_ref[number, 0] += dk
                own_ref[number, 1] += dv
            part = dot(k, score_cot, NN)
            dq = part if dq is None else dq + part
        low, high = dq[: HEAD // 2] * SCALE, dq[HEAD // 2 :] * SCALE
        cosine, sine = cos_ref[:, some], sin_ref[:, some]
        give_ref[4, 0 : HEAD // 2, some] = (low * cosine + high * sine).astype(bf16)
        give_ref[4, HEAD // 2 : HEAD, some] = (high * cosine - low * sine).astype(bf16)
    for number in range(4):
        give_ref[number] = own_ref[number // 2, number % 2].astype(bf16)


def attend_backward(meta, base, count, q, kv, kv_other, cot, lse, cosine, sine, after=()):
    tokens = q.shape[1]
    own = spec((HEAD, tokens), lambda i, meta: (base + i, 0))
    first = own
    second = spec((HEAD, tokens), lambda i, meta: (HEADS + base + i, 0))
    return call(
        attend_back_kernel,
        meta,
        (q, kv, kv, kv_other, kv_other, cot, lse, cosine, sine),
        [
            own,
            first,
            second,
            first,
            second,
            own,
            spec((1, 1, tokens), lambda i, meta: (i, 0, 0)),
            spec(cosine.shape),
            spec(sine.shape),
        ],
        [struct((5, count * HEAD, tokens), bf16)],
        [spec((5, HEAD, tokens), lambda i, meta: (0, i, 0))],
        count,
        "attend_backward",
        16 * 5 * 2 * tokens * tokens * D * count // HEADS,
        10 * MIB,
        scratch=[pltpu.VMEM((2, 2, HEAD, tokens), f32)],
        after=after,
    )


def middle_kernel(
    meta,
    mixed_a,
    mixed_b,
    mixed_c,
    own,
    four,
    other,
    xa,
    xb,
    ua,
    ub,
    rows_ref,
    attn_ref,
    resid_ref,
    second_ref,
    cot_ref,
    vec_ref,
):
    mine, rest = mine_rest(meta)
    near = mixed_a[:KIND, :]
    far = jnp.concatenate([mixed_a[KIND:, :], mixed_b[...], mixed_c[...]], axis=0)
    attn_ref[:, :HALF] = dot(near, own[:, mine], TN) + dot(
        far, four[0].reshape(3 * KIND, HALF), TN
    )
    attn_ref[:, HALF:] = dot(near, own[:, rest], TN) + dot(
        far, other[0].reshape(3 * KIND, HALF), TN
    )
    total = jnp.zeros((1, D), f32)
    for part, (x_ref, u_ref) in enumerate(((xa, ua), (xb, ub))):
        size = x_ref.shape[0]

        def work(start, total, part=part, x_ref=x_ref, u_ref=u_ref, size=size):
            some = pl.ds(start, CHUNK)
            here = pl.ds(part * size + start, CHUNK)
            x = jnp.concatenate([x_ref[some, mine], x_ref[some, rest]], axis=1).astype(f32)
            resid = x + row(rows_ref, GATE_ATTN) * attn_ref[here, :]
            resid_ref[here, :] = resid
            unit, _ = normalize(resid)
            value = unit * row(rows_ref, GAIN_MLP) * (1.0 + row(rows_ref, SCALE_MLP))
            second_ref[here, :] = (value + row(rows_ref, SHIFT_MLP)).astype(bf16)
            up = jnp.concatenate([u_ref[some, mine], u_ref[some, rest]], axis=1).astype(f32)
            cot = loss_weight(meta, part, start, rows_ref) * up
            cot = (row(rows_ref, GATE_MLP) * cot).astype(bf16)
            cot_ref[here, :] = cot
            return total + jnp.sum(cot.astype(f32), axis=0, keepdims=True)

        total = chunks(size, CHUNK, work, total)
    vec_ref[...] = jnp.broadcast_to(total, (8, D))


def middle(meta, mixed, own, four, other, xa, xb, ua, ub, rows, after=()):
    tokens = mixed[0].shape[1]
    whole = (tokens, D)
    return call(
        middle_kernel,
        meta,
        (*mixed, own, four, other, xa, xb, ua, ub, rows),
        [spec(one.shape) for one in mixed]
        + [spec(own.shape)]
        + piece_specs(lambda i: 3)
        + [spec(xa.shape)] * 4
        + [spec(rows.shape)],
        [
            struct(whole, f32),
            struct(whole, f32),
            struct(whole, bf16),
            struct(whole, bf16),
            struct((8, D), f32),
        ],
        [spec(whole)] * 4 + [spec((8, D))],
        1,
        "project_norm",
        2 * tokens * D * D,
        10 * MIB,
        after=after,
    )


def rows_of(refs, start):
    return jnp.concatenate([ref[0, 0, start : start + KIND] for ref in refs], axis=0)


def mlp_kernel(meta, second_ref, cot_ref, *refs):
    four, other = refs[:4], refs[4:8]
    out_in, back_in = refs[8:10] if len(refs) == 15 else (None, None)
    if out_in is None:
        units_ref = refs[-3]
        units_ref[2, :, :HALF] = second_ref[:, HALF:]
        units_ref[2, :, HALF:] = cot_ref[:, HALF:]
    out_ref, back_ref, units_ref, pre, back = refs[-5:]
    tokens = second_ref.shape[0]
    up_m, up_o = rows_of(four, 0), rows_of(other, 0)
    down_m, down_o = rows_of(four, KIND), rows_of(other, KIND)
    pre[...] = dot(second_ref[:, :HALF], up_m, NT) + dot(second_ref[:, HALF:], up_o, NT)
    back[...] = dot(cot_ref[:, :HALF], down_m, NT) + dot(cot_ref[:, HALF:], down_o, NT)
    rate = 0.7978845608
    tail = [
        jnp.sum(ref[0, 0, 2 * KIND : WIDE].astype(f32), axis=0, keepdims=True)[:, :KIND]
        for ref in four
    ]
    bias = jnp.concatenate(tail, axis=1)
    size = 32

    def work(start, totals):
        some = pl.ds(start, size)
        value = pre[some, :] + bias
        square = value * value
        bent = jnp.tanh(rate * value * (1.0 + 0.044715 * square))
        half = 0.5 * (1.0 + bent)
        units_ref[1, some, :] = (value * half).astype(bf16)
        slope = half + (0.5 * rate) * value * (1.0 - bent * bent) * (1.0 + 3 * 0.044715 * square)
        units_ref[0, some, :] = (back[some, :] * slope).astype(bf16)
        return totals

    chunks(tokens, size, work)
    cots, units = units_ref[0], units_ref[1]
    for target, source, left, right_m, right_o in (
        (out_ref, out_in, units, down_m, down_o),
        (back_ref, back_in, cots, up_m, up_o),
    ):
        for some, right in ((slice(0, HALF), right_m), (slice(HALF, D), right_o)):
            part = dot(left, right, NN)
            target[:, some] = part if source is None else source[:, some] + part


def mlp_block(meta, second, cot, four, other, which, sums=(), after=()):
    tokens = second.shape[0]
    size = tokens // 2
    slabs = 2 if sums else 3
    part = (1, 1, WIDE, HALF)
    parts = [spec(part, lambda i, meta, e=e: (e, which, 0, 0)) for e in range(4)]
    parts += [spec(part, lambda i, meta, e=e: (CROSS[e], which, 0, 0)) for e in range(4)]
    whole = spec((size, D), lambda i, meta: (i, 0))
    return call(
        mlp_kernel,
        meta,
        (second, cot, *[four] * 4, *[other] * 4, *sums),
        [whole, whole] + parts + [whole] * len(sums),
        [struct((tokens, D), f32), struct((tokens, D), f32), struct((slabs, tokens, D), bf16)],
        [whole, whole, spec((slabs, size, D), lambda i, meta: (0, i, 0))],
        2,
        "mlp_both_ways",
        8 * tokens * D * D,
        12 * MIB,
        scratch=[pltpu.VMEM((size, D), f32)] * 2,
        after=after,
    )


def mlp_grads_kernel(meta, mine_ref, theirs_ref, second_ref, cot_ref, right_ref, keep_ref, give_ref):
    for number, right in ((0, second_ref), (1, cot_ref)):
        grad = dot(mine_ref[number], right[:, :HALF], TN)
        got = dot(theirs_ref[number], right_ref[0, :, number * HALF : (number + 1) * HALF], TN)
        for e in range(4):
            block = grad[e * KIND : (e + 1) * KIND]
            block = block + got[CROSS[e] * KIND : (CROSS[e] + 1) * KIND]
            some = slice(number * KIND, (number + 1) * KIND)
            if e < 2:
                keep_ref[e, some] = block
            else:
                give_ref[e - 2, some] = block.astype(bf16)
    total = jnp.sum(mine_ref[0].astype(f32), axis=0, keepdims=True)
    got = jnp.sum(theirs_ref[0].astype(f32), axis=0, keepdims=True)
    for e in range(4):
        line = total[:, e * KIND : (e + 1) * KIND]
        line = line + got[:, CROSS[e] * KIND : (CROSS[e] + 1) * KIND]
        line = jnp.broadcast_to(line, (16, KIND))
        line = jnp.concatenate([line, line], axis=1)
        if e < 2:
            keep_ref[e, 2 * KIND : WIDE] = line
        else:
            give_ref[e - 2, 2 * KIND : WIDE] = line.astype(bf16)


def mlp_grads(meta, own, got, second, cot, right, after=()):
    tokens = second.shape[0]
    part = (2, WIDE, HALF)
    return call(
        mlp_grads_kernel,
        meta,
        (own, got, second, cot, right),
        [spec((2, tokens, D))] * 2
        + [spec((tokens, D))] * 2
        + [spec((1, tokens, D), lambda i, meta: (2, 0, 0))],
        [struct(part, f32), struct(part, bf16)],
        [spec(part), spec(part)],
        1,
        "mlp_grads",
        4 * tokens * D * D,
        6 * MIB,
        after=after,
    )


def turn_kernel(
    meta,
    resid_ref,
    attn_ref,
    out_ref,
    back_ref,
    ua,
    ub,
    rows_ref,
    own,
    four,
    other,
    mixed_a,
    mixed_b,
    mixed_c,
    block_a,
    block_b,
    resid_cot_ref,
    mixed_cot_ref,
    keep_ref,
    give_ref,
    vec_ref,
    attn_cot_ref,
):
    mine, rest = mine_rest(meta)
    sums = tuple(jnp.zeros((1, D), f32) for _ in range(4))
    for part, (u_ref, block_ref) in enumerate(((ua, block_a), (ub, block_b))):
        size = u_ref.shape[0]

        def work(start, sums, part=part, u_ref=u_ref, block_ref=block_ref, size=size):
            some = pl.ds(start, CHUNK)
            here = pl.ds(part * size + start, CHUNK)
            resid = resid_ref[here, :]
            mlp_out = out_ref[here, :] + row(rows_ref, DOWN_BIAS)
            result = (resid + row(rows_ref, GATE_MLP) * mlp_out).astype(bf16)
            block_ref[some, mine] = result[:, :HALF]
            block_ref[some, rest] = result[:, HALF:]
            up = jnp.concatenate([u_ref[some, mine], u_ref[some, rest]], axis=1).astype(f32)
            out_cot = loss_weight(meta, part, start, rows_ref) * up
            unit, rate = normalize(resid)
            cot = back_ref[here, :]
            total_1 = sums[1] + jnp.sum(cot, axis=0, keepdims=True)
            total_2 = sums[2] + jnp.sum(cot * unit, axis=0, keepdims=True)
            total_3 = sums[3] + jnp.sum(mlp_out * out_cot, axis=0, keepdims=True)
            cot = cot * (1.0 + row(rows_ref, SCALE_MLP)) * row(rows_ref, GAIN_MLP)
            resid_cot = out_cot + normalize_back(cot, unit, rate)
            resid_cot_ref[here, :] = resid_cot
            total_0 = sums[0] + jnp.sum(attn_ref[here, :] * resid_cot, axis=0, keepdims=True)
            attn_cot_ref[here, :] = (row(rows_ref, GATE_ATTN) * resid_cot).astype(bf16)
            return total_0, total_1, total_2, total_3

        sums = chunks(size, CHUNK, work, sums)
    for i in range(4):
        vec_ref[i : i + 1, :] = sums[i]
    vec_ref[4:8, :] = jnp.zeros((4, D), f32)
    cot_m, cot_o = attn_cot_ref[:, :HALF], attn_cot_ref[:, HALF:]
    near = dot(own[:, mine], cot_m, NT) + dot(own[:, rest], cot_o, NT)
    mixed_cot_ref[:KIND, :] = near.astype(bf16)
    far = dot(four[0].reshape(3 * KIND, HALF), cot_m, NT)
    far = far + dot(other[0].reshape(3 * KIND, HALF), cot_o, NT)
    mixed_cot_ref[KIND:, :] = far.astype(bf16)
    mixed = jnp.concatenate([mixed_a[...], mixed_b[...], mixed_c[...]], axis=0)
    keep_ref[...] = dot(mixed, cot_m, NN).reshape(Z, KIND, HALF)
    give_ref[...] = dot(mixed, cot_o, NN).reshape(Z, KIND, HALF).astype(bf16)


def turn(meta, resid, attn, out, back, ua, ub, rows, own, four, other, mixed, after=()):
    tokens = resid.shape[0]
    whole = (tokens, D)
    return call(
        turn_kernel,
        meta,
        (resid, attn, out, back, ua, ub, rows, own, four, other, *mixed),
        [spec(whole)] * 4
        + [spec(ua.shape)] * 2
        + [spec(rows.shape), spec(own.shape)]
        + piece_specs(lambda i: 3)
        + [spec(one.shape) for one in mixed],
        [
            struct(ua.shape, bf16),
            struct(ub.shape, bf16),
            struct(whole, f32),
            struct((D, tokens), bf16),
            struct((Z, KIND, HALF), f32),
            struct((Z, KIND, HALF), bf16),
            struct((8, D), f32),
        ],
        [
            spec(ua.shape),
            spec(ub.shape),
            spec(whole),
            spec((D, tokens)),
            spec((Z, KIND, HALF)),
            spec((Z, KIND, HALF)),
            spec((8, D)),
        ],
        1,
        "norm_back",
        4 * tokens * D * D,
        12 * MIB,
        scratch=[pltpu.VMEM(whole, bf16)],
        after=after,
    )


def attn_grads_kernel(keeps, meta, *refs):
    parts = (len(refs) - 12) // 2
    give, got = refs[:parts], refs[parts : 2 * parts]
    out_keep, out_got, first_ref, kv_got, cos_ref, sin_ref, cos_got, sin_got = refs[-12:-4]
    grad_first, grad_last, dkv_ref, left = refs[-4:]
    i = pl.program_id(0)
    kind = meta[(9 if keeps else 11) + i]
    size_of = D // parts

    def write(grad):
        grad = grad.astype(grad_first.dtype)

        @pl.when(i == 0)
        def _():
            grad_first[...] = grad

        @pl.when(i == 1)
        def _():
            grad_last[...] = grad

    def put(mine, theirs):
        grad = dot(mine, first_ref[:, :HALF], NN) + dot(theirs, kv_got[...], NT)
        write(grad.reshape(Z, KIND, HALF))

    @pl.when(kind == 3)
    def _():
        write(out_keep[...] + out_got[...].astype(f32))

    @pl.when(kind == 0)
    def _():
        put(
            jnp.concatenate([one[4] for one in give], axis=0),
            jnp.concatenate([one[4] for one in got], axis=0),
        )

    def together(number, side, low, size):
        group = low // size_of
        some = slice(low - group * size_of, low - group * size_of + size)
        theirs = got[group][2 * (1 - side) + number, some].astype(f32)
        return give[group][2 * side + number, some].astype(f32) + theirs

    @pl.when(kind == 1)
    def _():
        for side, cosines, sines in ((0, cos_ref, sin_ref), (1, cos_got, sin_got)):
            cosine, sine = cosines[...], sines[...]
            for h in range(HEADS):
                start = h * HEAD
                low = together(0, side, start, HEAD // 2)
                high = together(0, side, start + HEAD // 2, HEAD // 2)
                left[side, start : start + HEAD // 2] = (low * cosine + high * sine).astype(bf16)
                left[side, start + HEAD // 2 : start + HEAD] = (
                    high * cosine - low * sine
                ).astype(bf16)
        dkv_ref[0] = left[0]
        put(left[0], left[1])

    @pl.when(kind == 2)
    def _():
        for side in range(2):
            for h in range(HEADS):
                start = h * HEAD
                left[side, start : start + HEAD] = together(1, side, start, HEAD).astype(bf16)
        dkv_ref[1] = left[0]
        put(left[0], left[1])


def attn_grads(keeps, meta, give, got, out_keep, out_got, first, kv_got, turns, turns_got, after=()):
    tokens = first.shape[0]
    block = (Z, KIND, HALF)
    args = (*give, *got, out_keep, out_got, first, kv_got, *turns, *turns_got)
    specs = [spec(one.shape) for one in args]
    specs[2 * len(give) + 3] = spec((HALF, tokens), lambda i, meta: (2 * D // HALF, 0))
    dtype = f32 if keeps else bf16
    return call(
        functools.partial(attn_grads_kernel, keeps),
        meta,
        args,
        specs,
        [struct(block, dtype)] * 2 + [struct((2, D, tokens), bf16)],
        [spec(block), spec(block), spec((2, D, tokens))],
        2,
        "attention_grads",
        3 * tokens * D * D,
        14 * MIB,
        scratch=[pltpu.VMEM((2, D, tokens), bf16)],
        after=after,
    )


def leave_kernel(
    meta,
    xa,
    xb,
    dq_ref,
    dq2_ref,
    dq3_ref,
    dkv_sent,
    dkv_kept,
    resid_cot_ref,
    rows_ref,
    own,
    four0,
    four1,
    four2,
    other0,
    other1,
    other2,
    turn_ref,
    middle_ref,
    cond_ref,
    block_a,
    block_b,
    vec_ref,
    cot_ref,
):
    mine, rest = mine_rest(meta)
    dkv = [
        jnp.where(meta[1 + k] < 2, dkv_kept[k - 1], dkv_sent[k - 1]) for k in (1, 2)
    ]
    near_q = dq_ref[0, :KIND, :]
    far_q = jnp.concatenate([dq_ref[0, KIND:, :], dq2_ref[0], dq3_ref[0]], axis=0)
    for half, cols, fars in (
        (slice(0, HALF), mine, (four0, four1, four2)),
        (slice(HALF, D), rest, (other0, other1, other2)),
    ):
        total = dot(near_q, own[0, :, cols], TN)
        total = total + dot(far_q, fars[0][0].reshape(3 * KIND, HALF), TN)
        for k in (1, 2):
            total = total + dot(dkv[k - 1][:KIND, :], own[k, :, cols], TN)
            total = total + dot(dkv[k - 1][KIND:, :], fars[k][0].reshape(3 * KIND, HALF), TN)
        cot_ref[:, half] = total
    sums = tuple(jnp.zeros((1, D), f32) for _ in range(2))
    for part, (x_ref, block_ref) in enumerate(((xa, block_a), (xb, block_b))):
        size = x_ref.shape[0]

        def work(start, sums, part=part, x_ref=x_ref, block_ref=block_ref, size=size):
            some = pl.ds(start, CHUNK)
            here = pl.ds(part * size + start, CHUNK)
            x = jnp.concatenate([x_ref[some, mine], x_ref[some, rest]], axis=1).astype(f32)
            unit, rate = normalize(x)
            cot = cot_ref[here, :]
            total_0 = sums[0] + jnp.sum(cot, axis=0, keepdims=True)
            total_1 = sums[1] + jnp.sum(cot * unit, axis=0, keepdims=True)
            cot = cot * (1.0 + row(rows_ref, SCALE_ATTN)) * row(rows_ref, GAIN_ATTN)
            result = resid_cot_ref[here, :] + normalize_back(cot, unit, rate)
            result = result.astype(block_ref.dtype)
            block_ref[some, mine] = result[:, :HALF]
            block_ref[some, rest] = result[:, HALF:]
            return total_0, total_1

        sums = chunks(size, CHUNK, work, sums)
    nothing = jnp.zeros((1, D), f32)
    inner = row(turn_ref, 2)
    lines = [
        row(turn_ref, 0),
        row(turn_ref, 1),
        inner * row(rows_ref, GAIN_MLP),
        row(turn_ref, 3),
        jnp.where(meta[0] == 0, row(cond_ref, 0), nothing),
        sums[0],
        sums[1] * row(rows_ref, GAIN_ATTN),
        nothing,
        sums[1] * (1.0 + row(rows_ref, SCALE_ATTN)),
        inner * (1.0 + row(rows_ref, SCALE_MLP)),
        row(middle_ref, 0),
    ]
    for i in range(16):
        vec_ref[i : i + 1, :] = lines[i] if i < len(lines) else nothing


def leave(
    meta, xa, xb, dq, dkvs, resid_cot, rows, own, four, other, turn_vec, middle_vec, cond, after=()
):
    tokens = 2 * xa.shape[0]
    return call(
        leave_kernel,
        meta,
        (
            xa,
            xb,
            *dq,
            *dkvs,
            resid_cot,
            rows,
            own,
            *[four] * 3,
            *[other] * 3,
            turn_vec,
            middle_vec,
            cond,
        ),
        [spec(xa.shape)] * 2
        + [spec((1, *dq[0].shape[1:]), lambda i, meta: (4, 0, 0))] * 3
        + [spec(dkvs[0].shape)] * 2
        + [spec(resid_cot.shape), spec(rows.shape), spec(own.shape)]
        + [piece_specs(lambda i, k=k: k)[0] for k in range(3)]
        + [piece_specs(lambda i, k=k: k)[1] for k in range(3)]
        + [spec((8, D)), spec((8, D)), spec((1, D))],
        [struct(xa.shape, bf16)] * 2 + [struct((16, D), f32)],
        [spec(xa.shape)] * 2 + [spec((16, D))],
        1,
        "first_norm_back",
        6 * tokens * D * D,
        10 * MIB,
        scratch=[pltpu.VMEM((tokens, D), f32)],
        after=after,
    )


def place_attn_kernel(meta, four, other, qkv_ref, out_ref):
    mine, rest = mine_rest(meta)
    k = pl.program_id(0)

    @pl.when(k < 3)
    def _():
        qkv_ref[0, :, mine] = four[0].astype(f32)
        qkv_ref[0, :, rest] = other[0].astype(f32)

    @pl.when(k == 3)
    def _():
        out_ref[:, mine] = four[0].astype(f32)
        out_ref[:, rest] = other[0].astype(f32)


def place_attn(meta, four, other, after=()):
    return call(
        place_attn_kernel,
        meta,
        (four, other),
        [
            spec((1, KIND, HALF), lambda i, meta: (meta[1 + i], 0, 0)),
            spec((1, KIND, HALF), lambda i, meta: (meta[5 + i], 0, 0)),
        ],
        [struct((3, KIND, D), f32), struct((KIND, D), f32)],
        [
            spec((1, KIND, D), lambda i, meta: (jnp.minimum(i, 2), 0, 0)),
            spec((KIND, D)),
        ],
        4,
        "place_attention_grads",
        0,
        5 * MIB,
        after=after,
    )


def place_mlp_kernel(meta, four, other, up_ref, down_ref, bias_ref, turned):
    mine, rest = mine_rest(meta)
    k = pl.program_id(0)
    down_ref[:, mine] = four[0, KIND : 2 * KIND].astype(f32)
    down_ref[:, rest] = other[0, KIND : 2 * KIND].astype(f32)
    some = pl.ds(pl.multiple_of(k * KIND, KIND), KIND)
    turned[some, mine] = four[0, :KIND].astype(f32)
    turned[some, rest] = other[0, :KIND].astype(f32)
    bias_ref[0] = four[0, 2 * KIND : WIDE].astype(f32)

    @pl.when(k == 3)
    def _():
        up_ref[...] = turned[...].T


def place_mlp(meta, four, other, after=()):
    return call(
        place_mlp_kernel,
        meta,
        (four, other),
        [
            spec((1, WIDE, HALF), lambda i, meta: (meta[1 + i], 0, 0)),
            spec((1, WIDE, HALF), lambda i, meta: (meta[5 + i], 0, 0)),
        ],
        [struct((D, D), f32), struct((D, D), f32), struct((4, 16, HALF), f32)],
        [
            spec((D, D)),
            spec((KIND, D), lambda i, meta: (i, 0)),
            spec((1, 16, HALF), lambda i, meta: (i, 0, 0)),
        ],
        4,
        "place_mlp_grads",
        0,
        10 * MIB,
        after=after,
        scratch=[pltpu.VMEM((D, D), f32)],
    )


def in_order(arrays, me):
    found = []
    for number in range(len(arrays)):
        chosen = arrays[0]
        for i in range(1, len(arrays)):
            chosen = jnp.where((me ^ number) == i, arrays[i], chosen)
        found.append(chosen)
    return found


def merge_rows(tables):
    sums = tables[0][-8:]
    for one in tables[1:]:
        sums = sums + one[-8:]
    return jnp.concatenate([one[:-8] for one in tables] + [sums])


def last_kernel(
    meta, mine_ref, rest_ref, modulator_ref, mod_ref, bias_ref, cond_ref, sum_ref, whole, cots
):
    mine, rest = mine_rest(meta)
    j = pl.program_id(0)
    slots = cots.shape[1]

    @pl.when(j == 0)
    def _():
        whole[:, mine] = mine_ref[...]
        whole[:, rest] = rest_ref[...]
        sum_ref[...] = whole[8 * slots : 8 * slots + 8, :]
        for slot in range(slots):
            for number, line in enumerate((5, 6, 0, 1, 2, 3, 4)):
                cots[number, slot : slot + 1, :] = whole[8 * slot + line : 8 * slot + line + 1, :]
        cond_ref[...] = jnp.zeros_like(cond_ref)

    turned = cots[6, :, 0:128].T
    total = jnp.zeros((128, D), f32)
    for slot in range(slots):
        total = total + turned[:, slot : slot + 1] * cots[j, slot : slot + 1, :]
    mod_ref[...] = total
    bias_ref[...] = jnp.sum(cots[j], axis=0, keepdims=True)
    weight = modulator_ref[...].astype(f32)
    for s in range(2):
        product = weight * cots[j, pl.ds(meta[32 + s], 1), :]
        folded = product[:, :128]
        for k in range(1, D // 128):
            folded = folded + product[:, k * 128 : (k + 1) * 128]
        cond_ref[s : s + 1, :] += jnp.sum(folded.T, axis=0, keepdims=True)


def last(meta, mine, rest, modulator, slots, after=()):
    return call(
        last_kernel,
        meta,
        (mine, rest, modulator),
        [spec(mine.shape), spec(rest.shape), spec((128, D), lambda j, meta: (0, j))],
        [
            struct((128, 6 * D), f32),
            struct((1, 6 * D), f32),
            struct((2, 128), f32),
            struct((8, D), f32),
        ],
        [
            spec((128, D), lambda j, meta: (0, j)),
            spec((1, D), lambda j, meta: (0, j)),
            spec((2, 128)),
            spec((8, D)),
        ],
        6,
        "modulation_grads",
        0,
        5 * MIB,
        scratch=[pltpu.VMEM((8 * slots + 8, D), f32), pltpu.VMEM((7, slots, D), f32)],
        after=after,
    )


def shards(
    activations,
    condition,
    modulator,
    mod_bias,
    gain_attn,
    gain_mlp,
    query_key_value_matrix,
    output_matrix,
    up_matrix,
    up_offset_bias,
    down_matrix,
    down_bias,
    upstream,
    span_start,
    span_length,
    noise_level,
):
    dp_size = lax.axis_size("dp")
    d = lax.axis_index("dp")
    z = lax.axis_index("tensor")
    rows = activations.shape[1]
    tokens = 2 * rows
    meta = lax.dynamic_slice(meta_table(rows), (d % 8, z, 0), (1, 1, 32)).reshape(32)
    core = meta[0]
    odd = z % 2

    def swap(values):
        return jnp.where(core == 0, values, jnp.roll(values, HALF, axis=-1))

    flow = Flow(dp_size)

    qkv_block = jnp.transpose(query_key_value_matrix, (1, 2, 0))
    kind = meta[9]
    piece = jnp.where(
        kind < 3,
        lax.dynamic_slice(
            qkv_block, (jnp.minimum(kind, 2), 0, core * HALF), (1, KIND, HALF)
        ).reshape(KIND, HALF),
        lax.dynamic_slice(output_matrix, (0, core * HALF), (KIND, HALF)),
    )
    got = [flow.send(piece, to_back(r)) for r in range(1, Z)]
    facts = jnp.concatenate(
        [
            condition,
            span_start.astype(f32)[:, None],
            span_length.astype(f32)[:, None],
            noise_level.astype(f32)[:, None],
            jnp.zeros((2, 125), f32),
        ],
        axis=1,
    )
    facts_other = flow.send(facts, to_core)
    flow.fence()

    apart = jnp.stack([one.a for one in got])
    near = flow.send(apart, to_second)
    xa = flow.send(pick(activations, odd), chip_a)
    own_mine, own_rest = flow.run(prepare, meta, up_matrix, down_matrix, up_offset_bias)
    facts = jnp.where(core == z // 2, pick(facts, odd), pick(facts_other.a, odd))
    cond_row = facts[None, :128]
    start, length, level = facts[128], facts[129], facts[130]
    sigma = noise_low + (noise_high - noise_low) * (level + 0.5) / LEVELS
    factor = 1.0 / (1.0 - jnp.exp(-sigma))
    modulation = jnp.dot(cond_row, modulator.astype(f32), precision=highest) + mod_bias
    modulation = modulation.reshape(6, D)
    table = jnp.concatenate(
        [
            modulation,
            gain_attn[None],
            gain_mlp[None],
            down_bias[None],
            jnp.broadcast_to(start, (1, D)),
            jnp.broadcast_to(start + length, (1, D)),
            jnp.broadcast_to(factor, (1, D)),
            jnp.zeros((4, D), f32),
        ]
    )
    table = flow.keep(swap(table))
    step = jnp.arange(rows, dtype=f32)
    angular_rate = 10000.0 ** (-2.0 * jnp.arange(HEAD // 2, dtype=f32) / HEAD)

    def turns_of(core_here):
        places = jnp.concatenate(
            [
                ((2 * core_here + odd) * rows).astype(f32) + step,
                ((2 * core_here + 1 - odd) * rows).astype(f32) + step,
            ]
        )
        angles = angular_rate[:, None] * places[None, :]
        return flow.keep(jnp.cos(angles)), flow.keep(jnp.sin(angles))

    (cosine, sine), (cosine_got, sine_got) = turns_of(core), turns_of(1 - core)
    flow.fence()

    pair = jnp.stack([apart, near.a])
    far = flow.send(pair, to_first)
    other_pair = flow.send(pair, to_core)
    xb = flow.send(pick(activations, 1 - odd), chip_b)
    flow.fence()

    other_far = flow.send(far.a, to_core)
    flow.fence()
    table = table.a
    turns, turns_got = (cosine.a, sine.a), (cosine_got.a, sine_got.a)
    xa, xb = xa.a, xb.a

    mlp_piece = own_mine.a[0]
    ua = flow.send(pick(upstream, odd), chip_a)
    first, q, kv = flow.run(
        enter, meta, xa, xb, table, *turns, qkv_block, pair, far.a, other_pair.a, other_far.a
    )
    flow.fence()
    kv_got = flow.send(kv.a, to_core)
    attn_four = flow.keep(jnp.concatenate([pair, far.a]))
    attn_other = flow.keep(jnp.concatenate([other_pair.a, other_far.a]))
    flow.fence()
    attn_four, attn_other = attn_four.a, attn_other.a
    third = HEADS // 3
    settings = (q.a, kv.a, kv_got.a)
    ub = flow.send(pick(upstream, 1 - odd), chip_b)
    mixed_a, lse_a = flow.run(attend_forward, meta, 0, third, *settings)
    flow.fence()
    got_1 = flow.send(mlp_piece, to_back(1))
    mixed_b, lse_b = flow.run(attend_forward, meta, third, third, *settings)
    flow.fence()
    got_2 = flow.send(got_1.a, to_back(1))
    near_1 = flow.send(got_1.a, to_second)
    mixed_c, lse_c = flow.run(attend_forward, meta, 2 * third, third, *settings)
    flow.fence()
    mixed = (mixed_a.a, mixed_b.a, mixed_c.a)
    pair_1 = jnp.stack([got_1.a, near_1.a])
    far_1 = flow.send(pair_1, to_first)
    got_3 = flow.send(got_2.a, to_back(1))
    near_2 = flow.send(got_2.a, to_second)
    attn, resid, second, cot, middle_vec = flow.run(
        middle, meta, mixed, output_matrix, attn_four, attn_other, xa, xb, ua.a, ub.a, table
    )
    flow.fence()

    settings = (meta, second.a, cot.a)
    pair_2 = jnp.stack([got_2.a, near_2.a])
    far_2 = flow.send(pair_2, to_first)
    near_3 = flow.send(got_3.a, to_second)
    four_1 = jnp.concatenate([pair_1, far_1.a])[:, None]
    other_1 = flow.send(four_1, to_core)
    out, back, act_0 = flow.run(
        mlp_block, *settings, own_mine.a[:, None], own_rest.a[:, None], 0
    )
    flow.fence()
    pair_3 = jnp.stack([got_3.a, near_3.a])
    far_3 = flow.send(pair_3, to_first)
    act_0_got = flow.send(act_0.a, to_core)
    four_2 = jnp.concatenate([pair_2, far_2.a])[:, None]
    other_2 = flow.send(four_2, to_core)
    out, back, act_1 = flow.run(mlp_block, *settings, four_1, other_1.a, 0, (out.a, back.a))
    flow.fence()
    act_1_got = flow.send(act_1.a, to_core)
    four_3 = jnp.concatenate([pair_3, far_3.a])[:, None]
    other_3 = flow.send(four_3, to_core)
    sources = (second.a, cot.a, act_0_got.a)
    out, back, act_2 = flow.run(mlp_block, *settings, four_2, other_2.a, 0, (out.a, back.a))
    keep_0, give_0 = flow.run(mlp_grads, meta, act_0.a, act_0_got.a, *sources)
    flow.fence()
    act_2_got = flow.send(act_2.a, to_core)
    first_0 = flow.send(give_0.a, to_first)
    out, back, act_3 = flow.run(mlp_block, *settings, four_3, other_3.a, 0, (out.a, back.a))
    keep_1, give_1 = flow.run(mlp_grads, meta, act_1.a, act_1_got.a, *sources)
    flow.fence()

    def onward(keep, first):
        return (keep.a[1] + first.a[1].astype(f32)).astype(bf16)

    def total(keep, first, second):
        return keep.a[0] + first.a[0].astype(f32) + second.a.astype(f32)

    act_3_got = flow.send(act_3.a, to_core)
    first_1 = flow.send(give_1.a, to_first)
    second_0 = flow.send(onward(keep_0, first_0), to_second)
    block_a, block_b, resid_cot, mixed_cot, out_keep, out_give, turn_vec = flow.run(
        turn,
        meta,
        resid.a,
        attn.a,
        out.a,
        back.a,
        ua.a,
        ub.a,
        table,
        output_matrix,
        attn_four,
        attn_other,
        mixed,
    )
    keep_2, give_2 = flow.run(mlp_grads, meta, act_2.a, act_2_got.a, *sources)
    flow.fence()

    settings = (q.a, kv.a, kv_got.a, mixed_cot.a)
    first_2 = flow.send(give_2.a, to_first)
    second_1 = flow.send(onward(keep_1, first_1), to_second)
    back_a = flow.send(block_a.a, inverse(chip_a, dp_size))
    out_got = flow.send(out_give.a, to_core)
    block_0 = flow.keep(total(keep_0, first_0, second_0))
    keep_3, give_3 = flow.run(mlp_grads, meta, act_3.a, act_3_got.a, *sources)
    flow.then(give_3)
    (give_a,) = flow.run(attend_backward, meta, 0, third, *settings, lse_a.a, *turns)
    flow.fence()
    first_3 = flow.send(give_3.a, to_first)
    second_2 = flow.send(onward(keep_2, first_2), to_second)
    plane_1 = flow.send(total(keep_1, first_1, second_1).astype(bf16), to_ahead(1))
    got_a = flow.send(give_a.a, to_core)
    (give_b,) = flow.run(attend_backward, meta, third, third, *settings, lse_b.a, *turns)
    flow.fence()
    second_3 = flow.send(onward(keep_3, first_3), to_second)
    plane_2 = flow.send(total(keep_2, first_2, second_2).astype(bf16), to_ahead(2))
    got_b = flow.send(give_b.a, to_core)
    (give_c,) = flow.run(attend_backward, meta, 2 * third, third, *settings, lse_c.a, *turns)
    flow.fence()
    got_c = flow.send(give_c.a, to_core)
    block_3 = flow.keep(total(keep_3, first_3, second_3).astype(bf16))
    flow.fence()
    sources = (
        meta,
        (give_a.a, give_b.a, give_c.a),
        (got_a.a, got_b.a, got_c.a),
        out_keep.a,
        out_got.a,
        first.a,
        kv_got.a,
        turns,
        turns_got,
    )

    def across(total):
        bit = 8
        while bit < dp_size:
            total = total + send(total, to_flip(bit), dp_size)
            bit *= 2
        return total.astype(bf16)

    plane_3 = flow.send(block_3.a, to_ahead(3))
    give_e, give_f, dkv_sent = flow.run(attn_grads, False, *sources)
    flow.fence()
    first_e = flow.send(give_e.a, to_first)
    first_f = flow.send(give_f.a, to_first)
    mlp_total = block_0.a + plane_1.a.astype(f32) + plane_2.a.astype(f32)
    mlp_total = across(mlp_total + plane_3.a.astype(f32))
    mlp_near = flow.send(mlp_total, to_second)
    back_b = flow.send(block_b.a, inverse(chip_b, dp_size))
    keep_e, keep_f, dkv_kept = flow.run(attn_grads, True, *sources)
    flow.then(keep_e)
    slope_a, slope_b, late = flow.run(
        leave,
        meta,
        xa,
        xb,
        (give_a.a, give_b.a, give_c.a),
        (dkv_sent.a, dkv_kept.a),
        resid_cot.a,
        table,
        qkv_block,
        attn_four,
        attn_other,
        turn_vec.a,
        middle_vec.a,
        jnp.concatenate([cond_row, jnp.zeros((1, D - 128), f32)], axis=1),
    )
    flow.fence()

    got_second = flow.send((keep_f.a + first_f.a.astype(f32)).astype(bf16), to_second)
    slope_a = flow.send(slope_a.a, inverse(chip_a, dp_size))
    vectors = flow.send(late.a[:, HALF:], to_core)
    blocks = flow.keep(keep_e.a + first_e.a.astype(f32))
    mlp_pair = flow.keep(jnp.stack([mlp_total, mlp_near.a]))
    block_out = flow.keep(
        jnp.where(
            odd == 0, jnp.stack([back_a.a, back_b.a]), jnp.stack([back_b.a, back_a.a])
        )
    )
    flow.fence()
    vectors = late.a[:, :HALF] + vectors.a
    blocks = blocks.a + got_second.a.astype(f32)
    planes = [flow.send(blocks[r].astype(bf16), to_ahead(r)) for r in range(1, Z)]
    got = flow.send(vectors, to_flip(2))
    mlp_far = flow.send(mlp_pair.a, to_first)
    flow.fence()
    vectors = merge_rows(in_order([vectors, got.a], (d // 2) % 2))
    attn_total = blocks[0]
    for one in planes:
        attn_total = attn_total + one.a.astype(f32)
    attn_total = across(attn_total)
    attn_near = flow.send(attn_total, to_second)
    attn_far = flow.send(attn_total, to_first)
    attn_last = flow.send(attn_total, to_flip(6))
    got = flow.send(vectors, to_flip(4))
    mlp_four = jnp.concatenate([mlp_pair.a, mlp_far.a])
    mlp_other = flow.send(mlp_four, to_core)
    flow.fence()
    vectors = merge_rows(in_order([vectors, got.a], (d // 4) % 2))
    bit = 8
    while bit < dp_size:
        got = flow.send(vectors, to_flip(bit))
        flow.fence()
        vectors = merge_rows(in_order([vectors, got.a], (d // bit) % 2))
        bit *= 2
    got = [flow.send(vectors, to_flip_z(i)) for i in range(1, 4)]
    attn_four = jnp.stack([attn_total, attn_near.a, attn_far.a, attn_last.a])
    attn_other = flow.send(attn_four, to_core)
    slope_b = flow.send(slope_b.a, inverse(chip_b, dp_size))
    up_grad, down_grad, units = flow.run(place_mlp, meta, mlp_four, mlp_other.a)
    flow.fence()
    vectors = merge_rows(in_order([vectors] + [one.a for one in got], z))
    vectors_other = flow.send(vectors, to_core)
    slopes = (slope_a.a, slope_b.a)
    entering_state_slope = flow.keep(
        jnp.where(odd == 0, jnp.stack(slopes), jnp.stack(slopes[::-1])).astype(f32)
    )
    qkv_grad, out_grad = flow.run(place_attn, meta, attn_four, attn_other.a)
    flow.fence()
    own_slots = jnp.stack([(2 * core + s) * (dp_size // 2) + d // 2 for s in range(2)])
    modulator_grad, modbias_grad, condition_grad, sums = last(
        jnp.concatenate([meta, own_slots.astype(jnp.int32)]),
        vectors,
        vectors_other.a,
        modulator,
        Z * (dp_size // 2),
    )
    qkv_grad = jnp.transpose(qkv_grad.a, (2, 0, 1))
    upbias_grad = units.a[:, 0, :KIND].reshape(-1)
    return (
        block_out.a,
        entering_state_slope.a,
        condition_grad,
        modulator_grad,
        modbias_grad.reshape(-1),
        sums[0],
        sums[1],
        qkv_grad,
        out_grad.a,
        up_grad.a,
        upbias_grad,
        down_grad.a,
        sums[2],
    )


def solution(mesh):
    in_specs = (
        P("dp", "tensor", None),
        P("dp", None),
        P(),
        P(),
        P(),
        P(),
        P(None, None, "tensor"),
        P("tensor", None),
        P(None, "tensor"),
        P("tensor"),
        P("tensor", None),
        P(),
        P("dp", "tensor", None),
        P("dp"),
        P("dp"),
        P("dp"),
    )
    out_specs = (
        P("dp", "tensor", None),
        P("dp", "tensor", None),
        P("dp", None),
        P(),
        P(),
        P(),
        P(),
        P(None, None, "tensor"),
        P("tensor", None),
        P(None, "tensor"),
        P("tensor"),
        P("tensor", None),
        P(),
    )
    return jax.shard_map(shards, mesh=mesh, in_specs=in_specs, out_specs=out_specs, check_vma=False)
```

```python
import functools

import jax
import jax.numpy as jnp
import numpy as np
from jax import lax
from jax.experimental import pallas as pl
from jax.experimental.pallas import tpu as pltpu
from jax.sharding import PartitionSpec as P

D = 768
HALF = 384
HEAD = 64
HEADS = 12
L = 1024
LEVELS = 1024
Z = 4
KIND = 192
WIDE = 400

noise_low = 0.1
noise_high = 3.0
epsilon = 1e-05
highest = lax.Precision.HIGHEST
f32 = jnp.float32
bf16 = jnp.bfloat16
MIB = 1 << 20

NN = ((1,), (0,))
NT = ((1,), (1,))
TN = ((0,), (0,))
SCALE = HEAD ** (-0.5)
CROSS = (0, 2, 1, 3)


def dot(a, b, contract):
    return lax.dot_general(a, b, (contract, ((), ())), preferred_element_type=f32)


def struct(shape, dtype):
    return jax.ShapeDtypeStruct(shape, dtype)


def send(values, target, dp_size):
    pairs = []
    for d in range(dp_size):
        for t in range(Z):
            to_d, to_t = target(d, t)
            pairs.append((d * Z + t, to_d * Z + to_t))
    return lax.ppermute(values, ("dp", "tensor"), pairs)


def to_core(d, t):
    return (d ^ 1, t)


def to_first(d, t):
    return (d ^ (4 if d & 1 else 2), t)


def to_second(d, t):
    return (d ^ (2 if d & 1 else 4), t)


def to_back(shift):
    return lambda d, t: (d, (t - shift) % Z)


def to_ahead(shift):
    return lambda d, t: (d, (t + shift) % Z)


def to_flip(bit):
    return lambda d, t: (d ^ bit, t)


def to_flip_z(bit):
    return lambda d, t: (d, t ^ bit)


def chip_a(d, t):
    return (2 * (d // 2) + t // 2, 2 * (d % 2) + t % 2)


def chip_b(d, t):
    return (2 * (d // 2) + t // 2, 2 * (d % 2) + 1 - t % 2)


def inverse(target, dp_size):
    table = {target(d, t): (d, t) for d in range(dp_size) for t in range(Z)}
    return lambda d, t: table[(d, t)]


def pick(values, index, axis=0):
    return lax.dynamic_index_in_dim(values, index, axis, keepdims=False)


def meta_table(rows):
    table = np.zeros((8, Z, 32), np.int32)
    for d in range(8):
        core, x, y = d & 1, (d >> 1) & 1, (d >> 2) & 1
        kind = 2 * x + y
        second, first = (1, 2) if core == 0 else (2, 1)
        listed = [kind, kind ^ second, kind ^ first, kind ^ 3]
        for z in range(Z):
            table[d, z, 0] = core
            for e, k in enumerate(listed):
                table[d, z, 1 + k] = e
                table[d, z, 5 + k] = CROSS[e]
                table[d, z, 9 + e] = k
            for r in range(1, Z):
                table[d, z, 15 + r] = (z + r) % Z
            for e, k in enumerate(listed):
                chip = 4 * (k & 1) + 2 * (k >> 1)
                table[d, z, 20 + e] = chip + core
                table[d, z, 24 + e] = chip + 1 - core
            table[d, z, 13] = (2 * core + z % 2) * rows
            table[d, z, 14] = (2 * core + 1 - z % 2) * rows
    return jnp.asarray(table)


def mine_rest(meta):
    core = meta[0]
    return (
        pl.ds(pl.multiple_of(core * HALF, 128), HALF),
        pl.ds(pl.multiple_of((1 - core) * HALF, 128), HALF),
    )


def normalize(values):
    average = jnp.mean(values, axis=-1, keepdims=True)
    centred = values - average
    spread = jnp.mean(centred * centred, axis=-1, keepdims=True)
    rate = lax.rsqrt(spread + epsilon)
    return centred * rate, rate


def normalize_back(cot, unit, rate):
    return rate * (
        cot
        - jnp.mean(cot, axis=-1, keepdims=True)
        - unit * jnp.mean(cot * unit, axis=-1, keepdims=True)
    )


CHUNK = 64


def chunks(count, size, work, totals=(), together=2):
    step = size * together

    def body(i, totals):
        for number in range(together):
            totals = work(pl.multiple_of(i * step, step) + number * size, totals)
        return totals

    if count == step:
        return body(0, totals)
    return lax.fori_loop(0, count // step, body, totals)


(
    SHIFT_ATTN,
    SCALE_ATTN,
    GATE_ATTN,
    SHIFT_MLP,
    SCALE_MLP,
    GATE_MLP,
    GAIN_ATTN,
    GAIN_MLP,
    DOWN_BIAS,
    START,
    END,
    FACTOR,
) = range(12)


def row(ref, number):
    return ref[number : number + 1, :]


def loss_weight(meta, part, start, rows_ref):
    place = lax.broadcasted_iota(jnp.int32, (CHUNK, 1), 0) + (meta[13 + part] + start)
    place = place.astype(f32)
    inside = (place >= rows_ref[START : START + 1, 0:1]) & (place < rows_ref[END : END + 1, 0:1])
    return jnp.where(inside, rows_ref[FACTOR : FACTOR + 1, 0:1], 0.0)


def spec(shape, index=None):
    if index is None:
        index = lambda i, meta: (0,) * len(shape)
    return pl.BlockSpec(shape, index)


VMEM = {"attention_grads": 44}


def call(kernel, meta, args, in_specs, out_shape, out_specs, grid, name, flops, moved, **more):
    scratch = more.pop("scratch", ())
    into = more.pop("into", ())
    after = list(into) + [one for one in more.pop("after", ()) if one is not None]
    count, extra = len(args), len(after)
    more = {1 + i: o for i, o in more.pop("alias", {}).items()}

    def body(meta_ref, *refs):
        kernel(meta_ref, *refs[:count], *refs[count + extra :])

    return pl.pallas_call(
        body,
        grid_spec=pltpu.PrefetchScalarGridSpec(
            num_scalar_prefetch=1,
            grid=(grid,),
            in_specs=list(in_specs) + [pl.BlockSpec(memory_space=pl.ANY)] * extra,
            out_specs=out_specs,
            scratch_shapes=list(scratch),
        ),
        out_shape=out_shape,
        compiler_params=pltpu.CompilerParams(vmem_limit_bytes=VMEM.get(name, 26) * MIB),
        cost_estimate=pl.CostEstimate(
            flops=int(flops), transcendentals=0, bytes_accessed=int(moved)
        ),
        name=name,
        input_output_aliases={1 + count + i: i for i in range(len(into))} | more,
    )(meta, *args, *after)


class Box:
    def __init__(self, array):
        self.a = array


class Flow:
    def __init__(self, dp_size):
        self.dp_size, self.open, self.token = dp_size, [], None

    def keep(self, array):
        box = Box(array)
        self.open.append(box)
        return box

    def tied(self, array):
        if self.token is None:
            return array
        return lax.optimization_barrier((array, self.token))[0]

    def send(self, array, target):
        return self.keep(send(self.tied(array), target, self.dp_size))

    def run(self, function, *args, **more):
        after = () if self.token is None else (self.token,)
        return [self.keep(one) for one in function(*args, after=after, **more)]

    def then(self, box):
        self.token = lax.optimization_barrier((self.token, box.a))[0]

    def fence(self):
        arrays = lax.optimization_barrier(tuple(box.a for box in self.open))
        for box, array in zip(self.open, arrays):
            box.a = array
        self.token = min(arrays, key=lambda one: one.size)
        self.open = []


def prepare_kernel(meta, up_ref, down_ref, bias_ref, mine_ref, rest_ref, turned):
    mine, rest = mine_rest(meta)
    turned[...] = up_ref[...].astype(f32).T.astype(bf16)
    for e in range(4):
        kind = meta[9 + e]
        rows = pl.ds(pl.multiple_of(kind * KIND, KIND), KIND)
        for half, out, place in ((mine, mine_ref, e), (rest, rest_ref, CROSS[e])):
            out[place, 0:KIND] = turned[rows, half]
            out[place, KIND : 2 * KIND] = down_ref[rows, half]
            tail = bias_ref[kind]
            high = tail.astype(bf16)
            left = tail - high.astype(f32)
            middle = left.astype(bf16)
            low = (left - middle.astype(f32)).astype(bf16)
            number = lax.broadcasted_iota(jnp.int32, (16, HALF), 0)
            block = jnp.where(
                number == 0,
                high.astype(f32),
                jnp.where(
                    number == 1,
                    middle.astype(f32),
                    jnp.where(number == 2, low.astype(f32), 0.0),
                ),
            )
            out[place, 2 * KIND : WIDE] = block.astype(bf16)


def prepare(meta, up_matrix, down_matrix, up_bias, after=()):
    padded = jnp.pad(up_bias.reshape(4, 1, KIND), ((0, 0), (0, 0), (0, HALF - KIND)))
    out = (4, WIDE, HALF)
    return call(
        prepare_kernel,
        meta,
        (up_matrix, down_matrix, padded),
        [spec((D, D)), spec((D, D)), spec((4, 1, HALF))],
        [struct(out, bf16)] * 2,
        [spec(out)] * 2,
        1,
        "prepare_weights",
        0,
        5 * MIB,
        scratch=[pltpu.VMEM((D, D), bf16)],
        after=after,
    )


def enter_kernel(
    meta,
    xa,
    xb,
    rows_ref,
    cos_ref,
    sin_ref,
    own,
    pair,
    far_pair,
    other_pair,
    other_far,
    first_ref,
    q_ref,
    kv_ref,
):
    k = pl.program_id(0)
    mine, rest = mine_rest(meta)

    @pl.when(k == 0)
    def _():
        for part, ref in enumerate((xa, xb)):
            size = ref.shape[0]

            def work(start, totals, part=part, ref=ref, size=size):
                some = pl.ds(start, CHUNK)
                x = jnp.concatenate([ref[some, mine], ref[some, rest]], axis=1).astype(f32)
                unit, _ = normalize(x)
                value = unit * row(rows_ref, GAIN_ATTN) * (1.0 + row(rows_ref, SCALE_ATTN))
                value = value + row(rows_ref, SHIFT_ATTN)
                first_ref[pl.ds(part * size + start, CHUNK), :] = value.astype(bf16)
                return totals

            chunks(size, CHUNK, work)

        kv_ref[2 * D :, :] = first_ref[:, HALF:].T

    first_m, first_o = first_ref[:, :HALF], first_ref[:, HALF:]
    near = dot(own[0, :, mine], first_m, NT) + dot(own[0, :, rest], first_o, NT)
    four = jnp.where(meta[1 + k] < 2, pair[0], far_pair[0])
    other = jnp.where(meta[5 + k] < 2, other_pair[0], other_far[0])
    far = dot(four.reshape(3 * KIND, HALF), first_m, NT)
    far = far + dot(other.reshape(3 * KIND, HALF), first_o, NT)

    def head(h):
        return near[h * HEAD : (h + 1) * HEAD] if h < 3 else far[(h - 3) * HEAD : (h - 2) * HEAD]

    def put(write, turn):
        for h in range(HEADS):
            block = head(h)
            if turn:
                low, high = block[: HEAD // 2], block[HEAD // 2 :]
                cosine, sine = cos_ref[...], sin_ref[...]
                write(h * HEAD, (low * cosine - high * sine).astype(bf16))
                write(h * HEAD + HEAD // 2, (high * cosine + low * sine).astype(bf16))
            else:
                write(h * HEAD, block.astype(bf16))

    def write_q(start, block):
        q_ref[pl.ds(start, block.shape[0]), :] = block

    def write_k(start, block):
        kv_ref[pl.ds(start, block.shape[0]), :] = block

    def write_v(start, block):
        kv_ref[pl.ds(D + start, block.shape[0]), :] = block

    @pl.when(k == 0)
    def _():
        put(write_q, True)

    @pl.when(k == 1)
    def _():
        put(write_k, True)

    @pl.when(k == 2)
    def _():
        put(write_v, False)


def piece_specs(kind_of):
    return [
        spec((1, 3, KIND, HALF), lambda i, meta: (meta[1 + kind_of(i)], 0, 0, 0)),
        spec((1, 3, KIND, HALF), lambda i, meta: (meta[5 + kind_of(i)], 0, 0, 0)),
    ]


def enter(meta, xa, xb, rows, cosine, sine, own, pair, far, other_pair, other_far, after=()):
    tokens = 2 * xa.shape[0]
    part = (1, 3, KIND, HALF)

    def near(first):
        return spec(part, lambda i, meta: (jnp.minimum(meta[first + i], 1), 0, 0, 0))

    def away(first):
        return spec(part, lambda i, meta: (jnp.maximum(meta[first + i] - 2, 0), 0, 0, 0))

    return call(
        enter_kernel,
        meta,
        (xa, xb, rows, cosine, sine, own, pair, far, other_pair, other_far),
        [
            spec(xa.shape),
            spec(xb.shape),
            spec(rows.shape),
            spec(cosine.shape),
            spec(sine.shape),
            spec((1, KIND, D), lambda i, meta: (i, 0, 0)),
            near(1),
            away(1),
            near(5),
            away(5),
        ],
        [
            struct((tokens, D), bf16),
            struct((D, tokens), bf16),
            struct((2 * D + HALF, tokens), bf16),
        ],
        [
            spec((tokens, D)),
            spec((D, tokens)),
            spec((2 * D + HALF, tokens)),
        ],
        3,
        "norm_project",
        2 * 3 * tokens * D * D,
        8 * MIB,
        after=after,
    )


def attend_kernel(meta, q_ref, k_ref, v_ref, ko_ref, vo_ref, o_ref, lse_ref):
    tokens = q_ref.shape[1]
    width = min(512, tokens)
    for start in range(0, tokens, width):
        some = pl.ds(start, width)
        q = q_ref[:, some] * bf16(SCALE)
        near = dot(k_ref[...], q, TN)
        far = dot(ko_ref[...], q, TN)
        top = jnp.maximum(
            jnp.max(near, axis=0, keepdims=True), jnp.max(far, axis=0, keepdims=True)
        )
        near = jnp.exp(near - top)
        far = jnp.exp(far - top)
        total = jnp.sum(near, axis=0, keepdims=True) + jnp.sum(far, axis=0, keepdims=True)
        share = 1.0 / total
        mixed = dot(v_ref[...], (near * share).astype(bf16), NN)
        mixed = mixed + dot(vo_ref[...], (far * share).astype(bf16), NN)
        o_ref[:, some] = mixed.astype(bf16)
        lse_ref[0, :, some] = top + jnp.log(total)


def attend_forward(meta, base, count, q, kv, kv_other, after=()):
    tokens = q.shape[1]
    own = spec((HEAD, tokens), lambda i, meta: (base + i, 0))
    first = own
    second = spec((HEAD, tokens), lambda i, meta: (HEADS + base + i, 0))
    return call(
        attend_kernel,
        meta,
        (q, kv, kv, kv_other, kv_other),
        [own, first, second, first, second],
        [struct((count * HEAD, tokens), bf16), struct((count, 1, tokens), f32)],
        [
            spec((HEAD, tokens), lambda i, meta: (i, 0)),
            spec((1, 1, tokens), lambda i, meta: (i, 0, 0)),
        ],
        count,
        "attend_forward",
        16 * 2 * 2 * tokens * tokens * D * count // HEADS,
        5 * MIB * count // HEADS,
        after=after,
    )


def attend_back_kernel(
    meta,
    q_ref,
    k_ref,
    v_ref,
    ko_ref,
    vo_ref,
    c_ref,
    lse_ref,
    cos_ref,
    sin_ref,
    give_ref,
    own_ref,
):
    tokens = q_ref.shape[1]
    width = min(512, tokens)
    for start in range(0, tokens, width):
        some = pl.ds(start, width)
        q = q_ref[:, some] * bf16(SCALE)
        c = c_ref[:, some]
        lse = lse_ref[0, :, some]
        sides = ((k_ref[...], v_ref[...]), (ko_ref[...], vo_ref[...]))
        probs = [jnp.exp(dot(k, q, TN) - lse) for k, _ in sides]
        cots = [dot(v, c, TN) for _, v in sides]
        inner = jnp.sum(probs[0] * cots[0], axis=0, keepdims=True)
        inner = inner + jnp.sum(probs[1] * cots[1], axis=0, keepdims=True)
        dq = None
        for number, (k, _) in enumerate(sides):
            score_cot = (probs[number] * (cots[number] - inner)).astype(bf16)
            dk = dot(q, score_cot, NT)
            dv = dot(c, probs[number].astype(bf16), NT)
            if start == 0:
                own_ref[number, 0] = dk
                own_ref[number, 1] = dv
            else:
                own_ref[number, 0] += dk
                own_ref[number, 1] += dv
            part = dot(k, score_cot, NN)
            dq = part if dq is None else dq + part
        low, high = dq[: HEAD // 2] * SCALE, dq[HEAD // 2 :] * SCALE
        cosine, sine = cos_ref[:, some], sin_ref[:, some]
        give_ref[4, 0 : HEAD // 2, some] = (low * cosine + high * sine).astype(bf16)
        give_ref[4, HEAD // 2 : HEAD, some] = (high * cosine - low * sine).astype(bf16)
    for number in range(4):
        give_ref[number] = own_ref[number // 2, number % 2].astype(bf16)


def attend_backward(meta, base, count, q, kv, kv_other, cot, lse, cosine, sine, after=()):
    tokens = q.shape[1]
    own = spec((HEAD, tokens), lambda i, meta: (base + i, 0))
    first = own
    second = spec((HEAD, tokens), lambda i, meta: (HEADS + base + i, 0))
    return call(
        attend_back_kernel,
        meta,
        (q, kv, kv, kv_other, kv_other, cot, lse, cosine, sine),
        [
            own,
            first,
            second,
            first,
            second,
            own,
            spec((1, 1, tokens), lambda i, meta: (i, 0, 0)),
            spec(cosine.shape),
            spec(sine.shape),
        ],
        [struct((5, count * HEAD, tokens), bf16)],
        [spec((5, HEAD, tokens), lambda i, meta: (0, i, 0))],
        count,
        "attend_backward",
        16 * 5 * 2 * tokens * tokens * D * count // HEADS,
        10 * MIB,
        scratch=[pltpu.VMEM((2, 2, HEAD, tokens), f32)],
        after=after,
    )


def middle_kernel(
    meta,
    mixed_a,
    mixed_b,
    mixed_c,
    own,
    four,
    other,
    xa,
    xb,
    ua,
    ub,
    rows_ref,
    attn_ref,
    resid_ref,
    second_ref,
    cot_ref,
    vec_ref,
):
    mine, rest = mine_rest(meta)
    near = mixed_a[:KIND, :]
    far = jnp.concatenate([mixed_a[KIND:, :], mixed_b[...], mixed_c[...]], axis=0)
    attn_ref[:, :HALF] = dot(near, own[:, mine], TN) + dot(
        far, four[0].reshape(3 * KIND, HALF), TN
    )
    attn_ref[:, HALF:] = dot(near, own[:, rest], TN) + dot(
        far, other[0].reshape(3 * KIND, HALF), TN
    )
    total = jnp.zeros((1, D), f32)
    for part, (x_ref, u_ref) in enumerate(((xa, ua), (xb, ub))):
        size = x_ref.shape[0]

        def work(start, total, part=part, x_ref=x_ref, u_ref=u_ref, size=size):
            some = pl.ds(start, CHUNK)
            here = pl.ds(part * size + start, CHUNK)
            x = jnp.concatenate([x_ref[some, mine], x_ref[some, rest]], axis=1).astype(f32)
            resid = x + row(rows_ref, GATE_ATTN) * attn_ref[here, :]
            resid_ref[here, :] = resid
            unit, _ = normalize(resid)
            value = unit * row(rows_ref, GAIN_MLP) * (1.0 + row(rows_ref, SCALE_MLP))
            second_ref[here, :] = (value + row(rows_ref, SHIFT_MLP)).astype(bf16)
            up = jnp.concatenate([u_ref[some, mine], u_ref[some, rest]], axis=1).astype(f32)
            cot = loss_weight(meta, part, start, rows_ref) * up
            cot = (row(rows_ref, GATE_MLP) * cot).astype(bf16)
            cot_ref[here, :] = cot
            return total + jnp.sum(cot.astype(f32), axis=0, keepdims=True)

        total = chunks(size, CHUNK, work, total)
    vec_ref[...] = jnp.broadcast_to(total, (8, D))


def middle(meta, mixed, own, four, other, xa, xb, ua, ub, rows, after=()):
    tokens = mixed[0].shape[1]
    whole = (tokens, D)
    return call(
        middle_kernel,
        meta,
        (*mixed, own, four, other, xa, xb, ua, ub, rows),
        [spec(one.shape) for one in mixed]
        + [spec(own.shape)]
        + piece_specs(lambda i: 3)
        + [spec(xa.shape)] * 4
        + [spec(rows.shape)],
        [
            struct(whole, f32),
            struct(whole, f32),
            struct(whole, bf16),
            struct(whole, bf16),
            struct((8, D), f32),
        ],
        [spec(whole)] * 4 + [spec((8, D))],
        1,
        "project_norm",
        2 * tokens * D * D,
        10 * MIB,
        after=after,
    )


def rows_of(refs, start):
    return jnp.concatenate([ref[0, 0, start : start + KIND] for ref in refs], axis=0)


def mlp_kernel(meta, second_ref, cot_ref, *refs):
    four, other = refs[:4], refs[4:8]
    out_in, back_in = refs[8:10] if len(refs) == 15 else (None, None)
    if out_in is None:
        units_ref = refs[-3]
        units_ref[2, :, :HALF] = second_ref[:, HALF:]
        units_ref[2, :, HALF:] = cot_ref[:, HALF:]
    out_ref, back_ref, units_ref, pre, back = refs[-5:]
    tokens = second_ref.shape[0]
    up_m, up_o = rows_of(four, 0), rows_of(other, 0)
    down_m, down_o = rows_of(four, KIND), rows_of(other, KIND)
    pre[...] = dot(second_ref[:, :HALF], up_m, NT) + dot(second_ref[:, HALF:], up_o, NT)
    back[...] = dot(cot_ref[:, :HALF], down_m, NT) + dot(cot_ref[:, HALF:], down_o, NT)
    rate = 0.7978845608
    tail = [
        jnp.sum(ref[0, 0, 2 * KIND : WIDE].astype(f32), axis=0, keepdims=True)[:, :KIND]
        for ref in four
    ]
    bias = jnp.concatenate(tail, axis=1)
    size = 32

    def work(start, totals):
        some = pl.ds(start, size)
        value = pre[some, :] + bias
        square = value * value
        bent = jnp.tanh(rate * value * (1.0 + 0.044715 * square))
        half = 0.5 * (1.0 + bent)
        units_ref[1, some, :] = (value * half).astype(bf16)
        slope = half + (0.5 * rate) * value * (1.0 - bent * bent) * (1.0 + 3 * 0.044715 * square)
        units_ref[0, some, :] = (back[some, :] * slope).astype(bf16)
        return totals

    chunks(tokens, size, work, together=8)
    cots, units = units_ref[0], units_ref[1]
    for target, source, left, right_m, right_o in (
        (out_ref, out_in, units, down_m, down_o),
        (back_ref, back_in, cots, up_m, up_o),
    ):
        for some, right in ((slice(0, HALF), right_m), (slice(HALF, D), right_o)):
            part = dot(left, right, NN)
            target[:, some] = part if source is None else source[:, some] + part


def mlp_block(meta, second, cot, four, other, which, sums=(), after=()):
    tokens = second.shape[0]
    size = tokens // 2
    slabs = 2 if sums else 3
    part = (1, 1, WIDE, HALF)
    parts = [spec(part, lambda i, meta, e=e: (e, which, 0, 0)) for e in range(4)]
    parts += [spec(part, lambda i, meta, e=e: (CROSS[e], which, 0, 0)) for e in range(4)]
    whole = spec((size, D), lambda i, meta: (i, 0))
    return call(
        mlp_kernel,
        meta,
        (second, cot, *[four] * 4, *[other] * 4, *sums),
        [whole, whole] + parts + [whole] * len(sums),
        [struct((tokens, D), f32), struct((tokens, D), f32), struct((slabs, tokens, D), bf16)],
        [whole, whole, spec((slabs, size, D), lambda i, meta: (0, i, 0))],
        2,
        "mlp_both_ways",
        8 * tokens * D * D,
        12 * MIB,
        scratch=[pltpu.VMEM((size, D), f32)] * 2,
        after=after,
    )


def mlp_grads_kernel(meta, mine_ref, theirs_ref, second_ref, cot_ref, right_ref, keep_ref, give_ref):
    for number, right in ((0, second_ref), (1, cot_ref)):
        grad = dot(mine_ref[number], right[:, :HALF], TN)
        got = dot(theirs_ref[number], right_ref[0, :, number * HALF : (number + 1) * HALF], TN)
        for e in range(4):
            block = grad[e * KIND : (e + 1) * KIND]
            block = block + got[CROSS[e] * KIND : (CROSS[e] + 1) * KIND]
            some = slice(number * KIND, (number + 1) * KIND)
            if e < 2:
                keep_ref[e, some] = block
            else:
                give_ref[e - 2, some] = block.astype(bf16)
    total = jnp.sum(mine_ref[0].astype(f32), axis=0, keepdims=True)
    got = jnp.sum(theirs_ref[0].astype(f32), axis=0, keepdims=True)
    for e in range(4):
        line = total[:, e * KIND : (e + 1) * KIND]
        line = line + got[:, CROSS[e] * KIND : (CROSS[e] + 1) * KIND]
        line = jnp.broadcast_to(line, (16, KIND))
        line = jnp.concatenate([line, line], axis=1)
        if e < 2:
            keep_ref[e, 2 * KIND : WIDE] = line
        else:
            give_ref[e - 2, 2 * KIND : WIDE] = line.astype(bf16)


def mlp_grads(meta, own, got, second, cot, right, after=()):
    tokens = second.shape[0]
    part = (2, WIDE, HALF)
    return call(
        mlp_grads_kernel,
        meta,
        (own, got, second, cot, right),
        [spec((2, tokens, D))] * 2
        + [spec((tokens, D))] * 2
        + [spec((1, tokens, D), lambda i, meta: (2, 0, 0))],
        [struct(part, f32), struct(part, bf16)],
        [spec(part), spec(part)],
        1,
        "mlp_grads",
        4 * tokens * D * D,
        6 * MIB,
        after=after,
    )


def turn_kernel(
    meta,
    resid_ref,
    attn_ref,
    out_ref,
    back_ref,
    ua,
    ub,
    rows_ref,
    own,
    four,
    other,
    mixed_a,
    mixed_b,
    mixed_c,
    block_a,
    block_b,
    resid_cot_ref,
    mixed_cot_ref,
    keep_ref,
    give_ref,
    vec_ref,
    attn_cot_ref,
):
    mine, rest = mine_rest(meta)
    sums = tuple(jnp.zeros((1, D), f32) for _ in range(4))
    for part, (u_ref, block_ref) in enumerate(((ua, block_a), (ub, block_b))):
        size = u_ref.shape[0]

        def work(start, sums, part=part, u_ref=u_ref, block_ref=block_ref, size=size):
            some = pl.ds(start, CHUNK)
            here = pl.ds(part * size + start, CHUNK)
            resid = resid_ref[here, :]
            mlp_out = out_ref[here, :] + row(rows_ref, DOWN_BIAS)
            result = (resid + row(rows_ref, GATE_MLP) * mlp_out).astype(bf16)
            block_ref[some, mine] = result[:, :HALF]
            block_ref[some, rest] = result[:, HALF:]
            up = jnp.concatenate([u_ref[some, mine], u_ref[some, rest]], axis=1).astype(f32)
            out_cot = loss_weight(meta, part, start, rows_ref) * up
            unit, rate = normalize(resid)
            cot = back_ref[here, :]
            total_1 = sums[1] + jnp.sum(cot, axis=0, keepdims=True)
            total_2 = sums[2] + jnp.sum(cot * unit, axis=0, keepdims=True)
            total_3 = sums[3] + jnp.sum(mlp_out * out_cot, axis=0, keepdims=True)
            cot = cot * (1.0 + row(rows_ref, SCALE_MLP)) * row(rows_ref, GAIN_MLP)
            resid_cot = out_cot + normalize_back(cot, unit, rate)
            resid_cot_ref[here, :] = resid_cot
            total_0 = sums[0] + jnp.sum(attn_ref[here, :] * resid_cot, axis=0, keepdims=True)
            attn_cot_ref[here, :] = (row(rows_ref, GATE_ATTN) * resid_cot).astype(bf16)
            return total_0, total_1, total_2, total_3

        sums = chunks(size, CHUNK, work, sums)
    for i in range(4):
        vec_ref[i : i + 1, :] = sums[i]
    vec_ref[4:8, :] = jnp.zeros((4, D), f32)
    cot_m, cot_o = attn_cot_ref[:, :HALF], attn_cot_ref[:, HALF:]
    near = dot(own[:, mine], cot_m, NT) + dot(own[:, rest], cot_o, NT)
    mixed_cot_ref[:KIND, :] = near.astype(bf16)
    far = dot(four[0].reshape(3 * KIND, HALF), cot_m, NT)
    far = far + dot(other[0].reshape(3 * KIND, HALF), cot_o, NT)
    mixed_cot_ref[KIND:, :] = far.astype(bf16)
    mixed = jnp.concatenate([mixed_a[...], mixed_b[...], mixed_c[...]], axis=0)
    keep_ref[...] = dot(mixed, cot_m, NN).reshape(Z, KIND, HALF)
    give_ref[...] = dot(mixed, cot_o, NN).reshape(Z, KIND, HALF).astype(bf16)


def turn(meta, resid, attn, out, back, ua, ub, rows, own, four, other, mixed, after=()):
    tokens = resid.shape[0]
    whole = (tokens, D)
    return call(
        turn_kernel,
        meta,
        (resid, attn, out, back, ua, ub, rows, own, four, other, *mixed),
        [spec(whole)] * 4
        + [spec(ua.shape)] * 2
        + [spec(rows.shape), spec(own.shape)]
        + piece_specs(lambda i: 3)
        + [spec(one.shape) for one in mixed],
        [
            struct(ua.shape, bf16),
            struct(ub.shape, bf16),
            struct(whole, f32),
            struct((D, tokens), bf16),
            struct((Z, KIND, HALF), f32),
            struct((Z, KIND, HALF), bf16),
            struct((8, D), f32),
        ],
        [
            spec(ua.shape),
            spec(ub.shape),
            spec(whole),
            spec((D, tokens)),
            spec((Z, KIND, HALF)),
            spec((Z, KIND, HALF)),
            spec((8, D)),
        ],
        1,
        "norm_back",
        4 * tokens * D * D,
        12 * MIB,
        scratch=[pltpu.VMEM(whole, bf16)],
        after=after,
    )


def attn_grads_kernel(keeps, meta, *refs):
    parts = (len(refs) - 12) // 2
    give, got = refs[:parts], refs[parts : 2 * parts]
    out_keep, out_got, first_ref, kv_got, cos_ref, sin_ref, cos_got, sin_got = refs[-12:-4]
    grad_first, grad_last, dkv_ref, left = refs[-4:]
    i = pl.program_id(0)
    kind = meta[(9 if keeps else 11) + i]
    size_of = D // parts

    def write(grad):
        grad = grad.astype(grad_first.dtype)

        @pl.when(i == 0)
        def _():
            grad_first[...] = grad

        @pl.when(i == 1)
        def _():
            grad_last[...] = grad

    def put(mine, theirs):
        grad = dot(mine, first_ref[:, :HALF], NN) + dot(theirs, kv_got[...], NT)
        write(grad.reshape(Z, KIND, HALF))

    @pl.when(kind == 3)
    def _():
        write(out_keep[...] + out_got[...].astype(f32))

    @pl.when(kind == 0)
    def _():
        put(
            jnp.concatenate([one[4] for one in give], axis=0),
            jnp.concatenate([one[4] for one in got], axis=0),
        )

    def together(number, side, low, size):
        group = low // size_of
        some = slice(low - group * size_of, low - group * size_of + size)
        theirs = got[group][2 * (1 - side) + number, some].astype(f32)
        return give[group][2 * side + number, some].astype(f32) + theirs

    @pl.when(kind == 1)
    def _():
        for side, cosines, sines in ((0, cos_ref, sin_ref), (1, cos_got, sin_got)):
            cosine, sine = cosines[...], sines[...]
            for h in range(HEADS):
                start = h * HEAD
                low = together(0, side, start, HEAD // 2)
                high = together(0, side, start + HEAD // 2, HEAD // 2)
                left[side, start : start + HEAD // 2] = (low * cosine + high * sine).astype(bf16)
                left[side, start + HEAD // 2 : start + HEAD] = (
                    high * cosine - low * sine
                ).astype(bf16)
        dkv_ref[0] = left[0]
        put(left[0], left[1])

    @pl.when(kind == 2)
    def _():
        for side in range(2):
            for h in range(HEADS):
                start = h * HEAD
                left[side, start : start + HEAD] = together(1, side, start, HEAD).astype(bf16)
        dkv_ref[1] = left[0]
        put(left[0], left[1])


def attn_grads(keeps, meta, give, got, out_keep, out_got, first, kv_got, turns, turns_got, after=()):
    tokens = first.shape[0]
    block = (Z, KIND, HALF)
    args = (*give, *got, out_keep, out_got, first, kv_got, *turns, *turns_got)
    specs = [spec(one.shape) for one in args]
    specs[2 * len(give) + 3] = spec((HALF, tokens), lambda i, meta: (2 * D // HALF, 0))
    dtype = f32 if keeps else bf16
    return call(
        functools.partial(attn_grads_kernel, keeps),
        meta,
        args,
        specs,
        [struct(block, dtype)] * 2 + [struct((2, D, tokens), bf16)],
        [spec(block), spec(block), spec((2, D, tokens))],
        2,
        "attention_grads",
        3 * tokens * D * D,
        14 * MIB,
        scratch=[pltpu.VMEM((2, D, tokens), bf16)],
        after=after,
    )


def leave_kernel(
    meta,
    xa,
    xb,
    dq_ref,
    dq2_ref,
    dq3_ref,
    dkv_sent,
    dkv_kept,
    resid_cot_ref,
    rows_ref,
    own,
    four0,
    four1,
    four2,
    other0,
    other1,
    other2,
    turn_ref,
    middle_ref,
    cond_ref,
    block_a,
    block_b,
    vec_ref,
    cot_ref,
):
    mine, rest = mine_rest(meta)
    dkv = [
        jnp.where(meta[1 + k] < 2, dkv_kept[k - 1], dkv_sent[k - 1]) for k in (1, 2)
    ]
    near_q = dq_ref[0, :KIND, :]
    far_q = jnp.concatenate([dq_ref[0, KIND:, :], dq2_ref[0], dq3_ref[0]], axis=0)
    for half, cols, fars in (
        (slice(0, HALF), mine, (four0, four1, four2)),
        (slice(HALF, D), rest, (other0, other1, other2)),
    ):
        total = dot(near_q, own[0, :, cols], TN)
        total = total + dot(far_q, fars[0][0].reshape(3 * KIND, HALF), TN)
        for k in (1, 2):
            total = total + dot(dkv[k - 1][:KIND, :], own[k, :, cols], TN)
            total = total + dot(dkv[k - 1][KIND:, :], fars[k][0].reshape(3 * KIND, HALF), TN)
        cot_ref[:, half] = total
    sums = tuple(jnp.zeros((1, D), f32) for _ in range(2))
    for part, (x_ref, block_ref) in enumerate(((xa, block_a), (xb, block_b))):
        size = x_ref.shape[0]

        def work(start, sums, part=part, x_ref=x_ref, block_ref=block_ref, size=size):
            some = pl.ds(start, CHUNK)
            here = pl.ds(part * size + start, CHUNK)
            x = jnp.concatenate([x_ref[some, mine], x_ref[some, rest]], axis=1).astype(f32)
            unit, rate = normalize(x)
            cot = cot_ref[here, :]
            total_0 = sums[0] + jnp.sum(cot, axis=0, keepdims=True)
            total_1 = sums[1] + jnp.sum(cot * unit, axis=0, keepdims=True)
            cot = cot * (1.0 + row(rows_ref, SCALE_ATTN)) * row(rows_ref, GAIN_ATTN)
            result = resid_cot_ref[here, :] + normalize_back(cot, unit, rate)
            result = result.astype(block_ref.dtype)
            block_ref[some, mine] = result[:, :HALF]
            block_ref[some, rest] = result[:, HALF:]
            return total_0, total_1

        sums = chunks(size, CHUNK, work, sums)
    nothing = jnp.zeros((1, D), f32)
    inner = row(turn_ref, 2)
    lines = [
        row(turn_ref, 0),
        row(turn_ref, 1),
        inner * row(rows_ref, GAIN_MLP),
        row(turn_ref, 3),
        jnp.where(meta[0] == 0, row(cond_ref, 0), nothing),
        sums[0],
        sums[1] * row(rows_ref, GAIN_ATTN),
        nothing,
        sums[1] * (1.0 + row(rows_ref, SCALE_ATTN)),
        inner * (1.0 + row(rows_ref, SCALE_MLP)),
        row(middle_ref, 0),
    ]
    for i in range(16):
        vec_ref[i : i + 1, :] = lines[i] if i < len(lines) else nothing


def leave(
    meta, xa, xb, dq, dkvs, resid_cot, rows, own, four, other, turn_vec, middle_vec, cond, after=()
):
    tokens = 2 * xa.shape[0]
    return call(
        leave_kernel,
        meta,
        (
            xa,
            xb,
            *dq,
            *dkvs,
            resid_cot,
            rows,
            own,
            *[four] * 3,
            *[other] * 3,
            turn_vec,
            middle_vec,
            cond,
        ),
        [spec(xa.shape)] * 2
        + [spec((1, *dq[0].shape[1:]), lambda i, meta: (4, 0, 0))] * 3
        + [spec(dkvs[0].shape)] * 2
        + [spec(resid_cot.shape), spec(rows.shape), spec(own.shape)]
        + [piece_specs(lambda i, k=k: k)[0] for k in range(3)]
        + [piece_specs(lambda i, k=k: k)[1] for k in range(3)]
        + [spec((8, D)), spec((8, D)), spec((1, D))],
        [struct(xa.shape, bf16)] * 2 + [struct((16, D), f32)],
        [spec(xa.shape)] * 2 + [spec((16, D))],
        1,
        "first_norm_back",
        6 * tokens * D * D,
        10 * MIB,
        scratch=[pltpu.VMEM((tokens, D), f32)],
        after=after,
    )


def place_attn_kernel(meta, four, other, qkv_ref, out_ref):
    mine, rest = mine_rest(meta)
    k = pl.program_id(0)

    @pl.when(k < 3)
    def _():
        qkv_ref[0, :, mine] = four[0].astype(f32)
        qkv_ref[0, :, rest] = other[0].astype(f32)

    @pl.when(k == 3)
    def _():
        out_ref[:, mine] = four[0].astype(f32)
        out_ref[:, rest] = other[0].astype(f32)


def place_attn(meta, four, other, after=()):
    return call(
        place_attn_kernel,
        meta,
        (four, other),
        [
            spec((1, KIND, HALF), lambda i, meta: (meta[1 + i], 0, 0)),
            spec((1, KIND, HALF), lambda i, meta: (meta[5 + i], 0, 0)),
        ],
        [struct((3, KIND, D), f32), struct((KIND, D), f32)],
        [
            spec((1, KIND, D), lambda i, meta: (jnp.minimum(i, 2), 0, 0)),
            spec((KIND, D)),
        ],
        4,
        "place_attention_grads",
        0,
        5 * MIB,
        after=after,
    )


def place_mlp_kernel(meta, four, other, up_ref, down_ref, bias_ref, turned):
    mine, rest = mine_rest(meta)
    k = pl.program_id(0)
    down_ref[:, mine] = four[0, KIND : 2 * KIND].astype(f32)
    down_ref[:, rest] = other[0, KIND : 2 * KIND].astype(f32)
    some = pl.ds(pl.multiple_of(k * KIND, KIND), KIND)
    turned[some, mine] = four[0, :KIND].astype(f32)
    turned[some, rest] = other[0, :KIND].astype(f32)
    bias_ref[0] = four[0, 2 * KIND : WIDE].astype(f32)

    @pl.when(k == 3)
    def _():
        up_ref[...] = turned[...].T


def place_mlp(meta, four, other, after=()):
    return call(
        place_mlp_kernel,
        meta,
        (four, other),
        [
            spec((1, WIDE, HALF), lambda i, meta: (meta[1 + i], 0, 0)),
            spec((1, WIDE, HALF), lambda i, meta: (meta[5 + i], 0, 0)),
        ],
        [struct((D, D), f32), struct((D, D), f32), struct((4, 16, HALF), f32)],
        [
            spec((D, D)),
            spec((KIND, D), lambda i, meta: (i, 0)),
            spec((1, 16, HALF), lambda i, meta: (i, 0, 0)),
        ],
        4,
        "place_mlp_grads",
        0,
        10 * MIB,
        after=after,
        scratch=[pltpu.VMEM((D, D), f32)],
    )


def in_order(arrays, me):
    found = []
    for number in range(len(arrays)):
        chosen = arrays[0]
        for i in range(1, len(arrays)):
            chosen = jnp.where((me ^ number) == i, arrays[i], chosen)
        found.append(chosen)
    return found


def merge_rows(tables):
    sums = tables[0][-8:]
    for one in tables[1:]:
        sums = sums + one[-8:]
    return jnp.concatenate([one[:-8] for one in tables] + [sums])


def last_kernel(
    meta, mine_ref, rest_ref, modulator_ref, mod_ref, bias_ref, cond_ref, sum_ref, whole, cots
):
    mine, rest = mine_rest(meta)
    j = pl.program_id(0)
    slots = cots.shape[1]

    @pl.when(j == 0)
    def _():
        whole[:, mine] = mine_ref[...]
        whole[:, rest] = rest_ref[...]
        sum_ref[...] = whole[8 * slots : 8 * slots + 8, :]
        for slot in range(slots):
            for number, line in enumerate((5, 6, 0, 1, 2, 3, 4)):
                cots[number, slot : slot + 1, :] = whole[8 * slot + line : 8 * slot + line + 1, :]
        cond_ref[...] = jnp.zeros_like(cond_ref)

    turned = cots[6, :, 0:128].T
    total = jnp.zeros((128, D), f32)
    for slot in range(slots):
        total = total + turned[:, slot : slot + 1] * cots[j, slot : slot + 1, :]
    mod_ref[...] = total
    bias_ref[...] = jnp.sum(cots[j], axis=0, keepdims=True)
    weight = modulator_ref[...].astype(f32)
    for s in range(2):
        product = weight * cots[j, pl.ds(meta[32 + s], 1), :]
        folded = product[:, :128]
        for k in range(1, D // 128):
            folded = folded + product[:, k * 128 : (k + 1) * 128]
        cond_ref[s : s + 1, :] += jnp.sum(folded.T, axis=0, keepdims=True)


def last(meta, mine, rest, modulator, slots, after=()):
    return call(
        last_kernel,
        meta,
        (mine, rest, modulator),
        [spec(mine.shape), spec(rest.shape), spec((128, D), lambda j, meta: (0, j))],
        [
            struct((128, 6 * D), f32),
            struct((1, 6 * D), f32),
            struct((2, 128), f32),
            struct((8, D), f32),
        ],
        [
            spec((128, D), lambda j, meta: (0, j)),
            spec((1, D), lambda j, meta: (0, j)),
            spec((2, 128)),
            spec((8, D)),
        ],
        6,
        "modulation_grads",
        0,
        5 * MIB,
        scratch=[pltpu.VMEM((8 * slots + 8, D), f32), pltpu.VMEM((7, slots, D), f32)],
        after=after,
    )


def shards(
    activations,
    condition,
    modulator,
    mod_bias,
    gain_attn,
    gain_mlp,
    query_key_value_matrix,
    output_matrix,
    up_matrix,
    up_offset_bias,
    down_matrix,
    down_bias,
    upstream,
    span_start,
    span_length,
    noise_level,
):
    dp_size = lax.axis_size("dp")
    d = lax.axis_index("dp")
    z = lax.axis_index("tensor")
    rows = activations.shape[1]
    tokens = 2 * rows
    meta = lax.dynamic_slice(meta_table(rows), (d % 8, z, 0), (1, 1, 32)).reshape(32)
    core = meta[0]
    odd = z % 2

    def swap(values):
        return jnp.where(core == 0, values, jnp.roll(values, HALF, axis=-1))

    flow = Flow(dp_size)

    qkv_block = jnp.transpose(query_key_value_matrix, (1, 2, 0))
    kind = meta[9]
    piece = jnp.where(
        kind < 3,
        lax.dynamic_slice(
            qkv_block, (jnp.minimum(kind, 2), 0, core * HALF), (1, KIND, HALF)
        ).reshape(KIND, HALF),
        lax.dynamic_slice(output_matrix, (0, core * HALF), (KIND, HALF)),
    )
    got = [flow.send(piece, to_back(r)) for r in range(1, Z)]
    facts = jnp.concatenate(
        [
            condition,
            span_start.astype(f32)[:, None],
            span_length.astype(f32)[:, None],
            noise_level.astype(f32)[:, None],
            jnp.zeros((2, 125), f32),
        ],
        axis=1,
    )
    facts_other = flow.send(facts, to_core)
    flow.fence()

    apart = jnp.stack([one.a for one in got])
    near = flow.send(apart, to_second)
    xa = flow.send(pick(activations, odd), chip_a)
    own_mine, own_rest = flow.run(prepare, meta, up_matrix, down_matrix, up_offset_bias)
    facts = jnp.where(core == z // 2, pick(facts, odd), pick(facts_other.a, odd))
    cond_row = facts[None, :128]
    start, length, level = facts[128], facts[129], facts[130]
    sigma = noise_low + (noise_high - noise_low) * (level + 0.5) / LEVELS
    factor = 1.0 / (1.0 - jnp.exp(-sigma))
    modulation = jnp.dot(cond_row, modulator.astype(f32), precision=highest) + mod_bias
    modulation = modulation.reshape(6, D)
    table = jnp.concatenate(
        [
            modulation,
            gain_attn[None],
            gain_mlp[None],
            down_bias[None],
            jnp.broadcast_to(start, (1, D)),
            jnp.broadcast_to(start + length, (1, D)),
            jnp.broadcast_to(factor, (1, D)),
            jnp.zeros((4, D), f32),
        ]
    )
    table = flow.keep(swap(table))
    step = jnp.arange(rows, dtype=f32)
    angular_rate = 10000.0 ** (-2.0 * jnp.arange(HEAD // 2, dtype=f32) / HEAD)

    def turns_of(core_here):
        places = jnp.concatenate(
            [
                ((2 * core_here + odd) * rows).astype(f32) + step,
                ((2 * core_here + 1 - odd) * rows).astype(f32) + step,
            ]
        )
        angles = angular_rate[:, None] * places[None, :]
        return flow.keep(jnp.cos(angles)), flow.keep(jnp.sin(angles))

    (cosine, sine), (cosine_got, sine_got) = turns_of(core), turns_of(1 - core)
    flow.fence()

    pair = jnp.stack([apart, near.a])
    far = flow.send(pair, to_first)
    other_pair = flow.send(pair, to_core)
    xb = flow.send(pick(activations, 1 - odd), chip_b)
    flow.fence()

    other_far = flow.send(far.a, to_core)
    flow.fence()
    table = table.a
    turns, turns_got = (cosine.a, sine.a), (cosine_got.a, sine_got.a)
    xa, xb = xa.a, xb.a

    mlp_piece = own_mine.a[0]
    ua = flow.send(pick(upstream, odd), chip_a)
    first, q, kv = flow.run(
        enter, meta, xa, xb, table, *turns, qkv_block, pair, far.a, other_pair.a, other_far.a
    )
    flow.fence()
    kv_got = flow.send(kv.a, to_core)
    attn_four = flow.keep(jnp.concatenate([pair, far.a]))
    attn_other = flow.keep(jnp.concatenate([other_pair.a, other_far.a]))
    flow.fence()
    attn_four, attn_other = attn_four.a, attn_other.a
    third = HEADS // 3
    settings = (q.a, kv.a, kv_got.a)
    ub = flow.send(pick(upstream, 1 - odd), chip_b)
    mixed_a, lse_a = flow.run(attend_forward, meta, 0, third, *settings)
    flow.fence()
    got_1 = flow.send(mlp_piece, to_back(1))
    mixed_b, lse_b = flow.run(attend_forward, meta, third, third, *settings)
    flow.fence()
    got_2 = flow.send(got_1.a, to_back(1))
    near_1 = flow.send(got_1.a, to_second)
    mixed_c, lse_c = flow.run(attend_forward, meta, 2 * third, third, *settings)
    flow.fence()
    mixed = (mixed_a.a, mixed_b.a, mixed_c.a)
    pair_1 = jnp.stack([got_1.a, near_1.a])
    far_1 = flow.send(pair_1, to_first)
    got_3 = flow.send(got_2.a, to_back(1))
    near_2 = flow.send(got_2.a, to_second)
    attn, resid, second, cot, middle_vec = flow.run(
        middle, meta, mixed, output_matrix, attn_four, attn_other, xa, xb, ua.a, ub.a, table
    )
    flow.fence()

    settings = (meta, second.a, cot.a)
    pair_2 = jnp.stack([got_2.a, near_2.a])
    far_2 = flow.send(pair_2, to_first)
    near_3 = flow.send(got_3.a, to_second)
    four_1 = jnp.concatenate([pair_1, far_1.a])[:, None]
    other_1 = flow.send(four_1, to_core)
    out, back, act_0 = flow.run(
        mlp_block, *settings, own_mine.a[:, None], own_rest.a[:, None], 0
    )
    flow.fence()
    pair_3 = jnp.stack([got_3.a, near_3.a])
    far_3 = flow.send(pair_3, to_first)
    act_0_got = flow.send(act_0.a, to_core)
    four_2 = jnp.concatenate([pair_2, far_2.a])[:, None]
    other_2 = flow.send(four_2, to_core)
    out, back, act_1 = flow.run(mlp_block, *settings, four_1, other_1.a, 0, (out.a, back.a))
    flow.fence()
    act_1_got = flow.send(act_1.a, to_core)
    four_3 = jnp.concatenate([pair_3, far_3.a])[:, None]
    other_3 = flow.send(four_3, to_core)
    sources = (second.a, cot.a, act_0_got.a)
    out, back, act_2 = flow.run(mlp_block, *settings, four_2, other_2.a, 0, (out.a, back.a))
    keep_0, give_0 = flow.run(mlp_grads, meta, act_0.a, act_0_got.a, *sources)
    flow.fence()
    act_2_got = flow.send(act_2.a, to_core)
    first_0 = flow.send(give_0.a, to_first)
    out, back, act_3 = flow.run(mlp_block, *settings, four_3, other_3.a, 0, (out.a, back.a))
    keep_1, give_1 = flow.run(mlp_grads, meta, act_1.a, act_1_got.a, *sources)
    flow.fence()

    def onward(keep, first):
        return (keep.a[1] + first.a[1].astype(f32)).astype(bf16)

    def total(keep, first, second):
        return keep.a[0] + first.a[0].astype(f32) + second.a.astype(f32)

    act_3_got = flow.send(act_3.a, to_core)
    first_1 = flow.send(give_1.a, to_first)
    second_0 = flow.send(onward(keep_0, first_0), to_second)
    block_a, block_b, resid_cot, mixed_cot, out_keep, out_give, turn_vec = flow.run(
        turn,
        meta,
        resid.a,
        attn.a,
        out.a,
        back.a,
        ua.a,
        ub.a,
        table,
        output_matrix,
        attn_four,
        attn_other,
        mixed,
    )
    keep_2, give_2 = flow.run(mlp_grads, meta, act_2.a, act_2_got.a, *sources)
    flow.fence()

    settings = (q.a, kv.a, kv_got.a, mixed_cot.a)
    first_2 = flow.send(give_2.a, to_first)
    second_1 = flow.send(onward(keep_1, first_1), to_second)
    back_a = flow.send(block_a.a, inverse(chip_a, dp_size))
    out_got = flow.send(out_give.a, to_core)
    block_0 = flow.keep(total(keep_0, first_0, second_0))
    keep_3, give_3 = flow.run(mlp_grads, meta, act_3.a, act_3_got.a, *sources)
    flow.then(give_3)
    (give_a,) = flow.run(attend_backward, meta, 0, third, *settings, lse_a.a, *turns)
    flow.fence()
    first_3 = flow.send(give_3.a, to_first)
    second_2 = flow.send(onward(keep_2, first_2), to_second)
    plane_1 = flow.send(total(keep_1, first_1, second_1).astype(bf16), to_ahead(1))
    got_a = flow.send(give_a.a, to_core)
    (give_b,) = flow.run(attend_backward, meta, third, third, *settings, lse_b.a, *turns)
    flow.fence()
    second_3 = flow.send(onward(keep_3, first_3), to_second)
    plane_2 = flow.send(total(keep_2, first_2, second_2).astype(bf16), to_ahead(2))
    got_b = flow.send(give_b.a, to_core)
    (give_c,) = flow.run(attend_backward, meta, 2 * third, third, *settings, lse_c.a, *turns)
    flow.fence()
    got_c = flow.send(give_c.a, to_core)
    block_3 = flow.keep(total(keep_3, first_3, second_3).astype(bf16))
    flow.fence()
    sources = (
        meta,
        (give_a.a, give_b.a, give_c.a),
        (got_a.a, got_b.a, got_c.a),
        out_keep.a,
        out_got.a,
        first.a,
        kv_got.a,
        turns,
        turns_got,
    )

    def across(total):
        bit = 8
        while bit < dp_size:
            total = total + send(total, to_flip(bit), dp_size)
            bit *= 2
        return total.astype(bf16)

    plane_3 = flow.send(block_3.a, to_ahead(3))
    give_e, give_f, dkv_sent = flow.run(attn_grads, False, *sources)
    flow.fence()
    first_e = flow.send(give_e.a, to_first)
    first_f = flow.send(give_f.a, to_first)
    mlp_total = block_0.a + plane_1.a.astype(f32) + plane_2.a.astype(f32)
    mlp_total = across(mlp_total + plane_3.a.astype(f32))
    mlp_near = flow.send(mlp_total, to_second)
    back_b = flow.send(block_b.a, inverse(chip_b, dp_size))
    keep_e, keep_f, dkv_kept = flow.run(attn_grads, True, *sources)
    flow.then(keep_e)
    slope_a, slope_b, late = flow.run(
        leave,
        meta,
        xa,
        xb,
        (give_a.a, give_b.a, give_c.a),
        (dkv_sent.a, dkv_kept.a),
        resid_cot.a,
        table,
        qkv_block,
        attn_four,
        attn_other,
        turn_vec.a,
        middle_vec.a,
        jnp.concatenate([cond_row, jnp.zeros((1, D - 128), f32)], axis=1),
    )
    flow.fence()

    got_second = flow.send((keep_f.a + first_f.a.astype(f32)).astype(bf16), to_second)
    slope_a = flow.send(slope_a.a, inverse(chip_a, dp_size))
    vectors = flow.send(late.a[:, HALF:], to_core)
    blocks = flow.keep(keep_e.a + first_e.a.astype(f32))
    mlp_pair = flow.keep(jnp.stack([mlp_total, mlp_near.a]))
    block_out = flow.keep(
        jnp.where(
            odd == 0, jnp.stack([back_a.a, back_b.a]), jnp.stack([back_b.a, back_a.a])
        )
    )
    flow.fence()
    vectors = late.a[:, :HALF] + vectors.a
    blocks = blocks.a + got_second.a.astype(f32)
    planes = [flow.send(blocks[r].astype(bf16), to_ahead(r)) for r in range(1, Z)]
    got = flow.send(vectors, to_flip(2))
    mlp_far = flow.send(mlp_pair.a, to_first)
    flow.fence()
    vectors = merge_rows(in_order([vectors, got.a], (d // 2) % 2))
    attn_total = blocks[0]
    for one in planes:
        attn_total = attn_total + one.a.astype(f32)
    attn_total = across(attn_total)
    attn_near = flow.send(attn_total, to_second)
    attn_far = flow.send(attn_total, to_first)
    attn_last = flow.send(attn_total, to_flip(6))
    got = flow.send(vectors, to_flip(4))
    mlp_four = jnp.concatenate([mlp_pair.a, mlp_far.a])
    mlp_other = flow.send(mlp_four, to_core)
    flow.fence()
    vectors = merge_rows(in_order([vectors, got.a], (d // 4) % 2))
    bit = 8
    while bit < dp_size:
        got = flow.send(vectors, to_flip(bit))
        flow.fence()
        vectors = merge_rows(in_order([vectors, got.a], (d // bit) % 2))
        bit *= 2
    got = [flow.send(vectors, to_flip_z(i)) for i in range(1, 4)]
    attn_four = jnp.stack([attn_total, attn_near.a, attn_far.a, attn_last.a])
    attn_other = flow.send(attn_four, to_core)
    slope_b = flow.send(slope_b.a, inverse(chip_b, dp_size))
    up_grad, down_grad, units = flow.run(place_mlp, meta, mlp_four, mlp_other.a)
    flow.fence()
    vectors = merge_rows(in_order([vectors] + [one.a for one in got], z))
    vectors_other = flow.send(vectors, to_core)
    slopes = (slope_a.a, slope_b.a)
    entering_state_slope = flow.keep(
        jnp.where(odd == 0, jnp.stack(slopes), jnp.stack(slopes[::-1])).astype(f32)
    )
    qkv_grad, out_grad = flow.run(place_attn, meta, attn_four, attn_other.a)
    flow.fence()
    own_slots = jnp.stack([(2 * core + s) * (dp_size // 2) + d // 2 for s in range(2)])
    modulator_grad, modbias_grad, condition_grad, sums = last(
        jnp.concatenate([meta, own_slots.astype(jnp.int32)]),
        vectors,
        vectors_other.a,
        modulator,
        Z * (dp_size // 2),
    )
    qkv_grad = jnp.transpose(qkv_grad.a, (2, 0, 1))
    upbias_grad = units.a[:, 0, :KIND].reshape(-1)
    return (
        block_out.a,
        entering_state_slope.a,
        condition_grad,
        modulator_grad,
        modbias_grad.reshape(-1),
        sums[0],
        sums[1],
        qkv_grad,
        out_grad.a,
        up_grad.a,
        upbias_grad,
        down_grad.a,
        sums[2],
    )


def solution(mesh):
    in_specs = (
        P("dp", "tensor", None),
        P("dp", None),
        P(),
        P(),
        P(),
        P(),
        P(None, None, "tensor"),
        P("tensor", None),
        P(None, "tensor"),
        P("tensor"),
        P("tensor", None),
        P(),
        P("dp", "tensor", None),
        P("dp"),
        P("dp"),
        P("dp"),
    )
    out_specs = (
        P("dp", "tensor", None),
        P("dp", "tensor", None),
        P("dp", None),
        P(),
        P(),
        P(),
        P(),
        P(None, None, "tensor"),
        P("tensor", None),
        P(None, "tensor"),
        P("tensor"),
        P("tensor", None),
        P(),
    )
    return jax.shard_map(shards, mesh=mesh, in_specs=in_specs, out_specs=out_specs, check_vma=False)
```
